32 devices in a mesh: pot: 8 (over y, x, core), grid: 4 (over z).
Axes of the slice: x: 2, y: 2, z: 4, core: 2. Of those that a mesh axis runs over, the one named last changes fastest.
Arguments:
- potentials: float32 [8, 32, 4096], P('pot', 'grid'), may hold values from -6 to 6
- orbitals: bfloat16 [32, 32, 4096], P(None, 'grid', 'pot'), may hold values from -0.5 to 2
- energies: float32 [32], replicated, may hold values from -2 to -0.2
- local_potential: float32 [32, 4096], replicated, may hold values from 0 to 3
- inverse_factor: bfloat16 [8, 8], replicated, may hold values from -8 to 8, as said below
Outputs:
- updated: float32 [8, 32, 4096], P('pot', 'grid')
- margins: float32 [8, 8], P('pot')
The draws below stay inside these ranges and needn't reach their ends.
Inputs may be any that keep to these rules, and one draw needn't show every extreme that they name: `inverse_factor`: lower triangular with a positive diagonal.
All inputs are finite; a program needn't handle non-finite values.
Results may differ from the reference program's by a relative error of at most 0.0029.
Values may be sent and summed in bfloat16 or wider, within the bound.
No kernel may reach another device: no remote copies, remote signals or barrier semaphores. Data moves between devices by JAX's collectives and lax.ppermute only.
A program may use at most 64 MiB of HBM per device.

```python
import jax
import jax.numpy as jnp
from jax import lax

NX = 64
NY = 64
NZ = 32
ORBITALS = 32
SWEEPS = 4
POTENTIALS = 8


def draw_inverse_factor(key, part):
    key_lower, key_diagonal = jax.random.split(jax.random.fold_in(key, 11), 2)
    count_all = POTENTIALS
    strict_lower = jnp.tril(jax.random.normal(key_lower, (count_all, count_all), jnp.float32) * 0.5 / jnp.sqrt(1.0 * count_all), -1)
    diagonal = jnp.exp(jax.random.uniform(key_diagonal, (count_all,), jnp.float32, jnp.log(0.5), jnp.log(2.0)))
    matrix = strict_lower + jnp.diag(diagonal)
    return matrix.astype(jnp.bfloat16)


def raised(array, key, source, target, shards_of, factor):
    def block_of(dim):
        return (jnp.arange(array.shape[dim]) // (array.shape[dim] // shards_of)).reshape((-1,) + (1,) * (array.ndim - 1 - dim))

    near = jax.random.permutation(key, shards_of)[block_of(target)]
    far = (block_of(target) + shards_of // 2) % shards_of
    return jnp.where((block_of(source) == near) | (block_of(source) == far), factor * array, array)


def steps_of(rng, extent, cuts, least, largest):
    gain = 1.0
    for position, shards_of in cuts:
        draws = jax.random.uniform(jax.random.fold_in(jax.random.fold_in(rng, 6), position), (shards_of,), jnp.float32, least / len(cuts), largest / len(cuts))
        gain = gain * jnp.repeat(jnp.exp(draws), extent[position] // shards_of).reshape((-1,) + (1,) * (len(extent) - 1 - position))
    return gain


def noise_with(stream_key, shape, spread, most, pieces, heavy, kind=jnp.bfloat16):
    array = spread * jax.random.normal(stream_key, shape, jnp.float32)
    if pieces:
        array = array * steps_of(stream_key, shape, pieces, -0.22, 0.18)
    return jnp.clip(raised(array, jax.random.fold_in(stream_key, 3), *heavy), -most, most).astype(kind)


def setup_inputs(seed: int = 0) -> dict:
    streams_of = jax.random.split(jax.random.key(seed), 6)
    return {
        "potentials": noise_with(streams_of[0], (POTENTIALS, NZ, NX * NY), 1.0, 6.0, ((0, 8), (1, 4)), (2, 0, 8, 2.0), jnp.float32),
        "orbitals": jnp.clip(-0.5 + 2.5 * jax.random.uniform(streams_of[1], (ORBITALS, NZ, NX * NY), jnp.float32) ** steps_of(streams_of[1], (ORBITALS, NZ, NX * NY), ((1, 4), (2, 8)), -0.2, 0.2), -0.5, 2.0).astype(jnp.bfloat16),
        "energies": jnp.clip(jax.random.uniform(streams_of[2], (ORBITALS,), jnp.float32, -2.0, -0.2), -2.0, -0.2),
        "local_potential": jnp.clip(jax.random.uniform(streams_of[3], (NZ, NX * NY), jnp.float32, 0.0, 3.0), 0.0, 3.0),
        "inverse_factor": draw_inverse_factor(jax.random.fold_in(streams_of[5], 71), 0),
    }


DAMPING = 0.8


def plane_neighbours(field, row_width):
    plane_size = field.shape[-1]
    widths = [(0, 0)] * (field.ndim - 1)
    padded = jnp.pad(field, widths + [(row_width, row_width)])
    along_y = padded[..., 2 * row_width:] + padded[..., :plane_size]
    column = jnp.arange(plane_size, dtype=jnp.int32) % row_width
    padded = jnp.pad(field, widths + [(1, 1)])
    right_side = jnp.where(column == row_width - 1, 0.0, padded[..., 2:])
    left_side = jnp.where(column == 0, 0.0, padded[..., :plane_size])
    return along_y + right_side + left_side


def plane_pairs(field):
    padded = jnp.pad(field, [(0, 0)] * (field.ndim - 2) + [(1, 1), (0, 0)])
    return padded[..., 2:, :] + padded[..., :-2, :]


def reference(potentials, orbitals, energies, local_potential, inverse_factor):
    def per_orbital(summed, member):
        orbital, energy = member
        orbital = orbital.astype(jnp.float32)
        diagonal = 3.0 + local_potential - energy
        source = -orbital * potentials
        answer = DAMPING * source / diagonal
        for sweep_index in range(SWEEPS - 1):
            nearby = plane_pairs(answer) + plane_neighbours(answer, NX)
            answer = answer + DAMPING * (source - diagonal * answer + 0.5 * nearby) / diagonal
        return summed + orbital * answer, None

    summed, _ = lax.scan(per_orbital, jnp.zeros_like(potentials), (orbitals, energies))
    trial_block = (potentials + (4.0 / ORBITALS) * summed).astype(jnp.bfloat16)
    flattened = trial_block.reshape(trial_block.shape[0], -1)
    margins = lax.dot_general(flattened, flattened, (((1,), (1,)), ((), ())), preferred_element_type=jnp.float32)
    margins = margins / (NX * NY * NZ)
    updated = jnp.dot(inverse_factor, flattened, preferred_element_type=jnp.float32).reshape(trial_block.shape)
    return updated, margins
```

```python
import math

import jax
import jax.numpy as jnp
from jax import lax
from jax.experimental import pallas as pl
from jax.experimental.pallas import tpu as pltpu
from jax.sharding import PartitionSpec as P

NX = 64
SWEEPS = 4
DAMPING = 0.8
COEFFS = tuple(
    sum(math.comb(n, m) * (1.0 - DAMPING) ** (n - m) for n in range(m, SWEEPS))
    for m in range(SWEEPS)
)
HALO = SWEEPS - 1
LEAD = HALO + HALO % 2
LANES = 128


def padded_2(block, sides, width):
    for axis, dim in sides:
        count = lax.axis_size(axis)
        forward = [(i, i + 1) for i in range(count - 1)]
        backward = [(target, source) for source, target in forward]
        low = lax.ppermute(
            lax.slice_in_dim(block, block.shape[dim] - width, None, axis=dim), axis, forward
        )
        high = lax.ppermute(lax.slice_in_dim(block, 0, width, axis=dim), axis, backward)
        block = jnp.concatenate([low, block, high], axis=dim)
    return block


def plane_neighbours(field, row_width):
    plane_size = field.shape[-1]
    widths = [(0, 0)] * (field.ndim - 1)
    padded = jnp.pad(field, widths + [(row_width, row_width)])
    along_y = padded[..., 2 * row_width :] + padded[..., :plane_size]
    column = jnp.arange(plane_size, dtype=jnp.int32) % row_width
    padded = jnp.pad(field, widths + [(1, 1)])
    right_side = jnp.where(column == row_width - 1, 0.0, padded[..., 2:])
    left_side = jnp.where(column == 0, 0.0, padded[..., :plane_size])
    return along_y + right_side + left_side


def across_slabs(answer):
    padded = padded_2(answer, (("grid", 2),), 1)
    return padded[:, :, 2:] + padded[:, :, :-2]


def absorb(orbital_block, energy_block, fields, local_here, along_planes):
    orbital = orbital_block.astype(jnp.float32)[:, None]
    diagonal = (3.0 + local_here[None] - energy_block[:, None, None])[:, None]
    source = -orbital * fields[None]
    answer = DAMPING * source / diagonal
    for sweep_index in range(SWEEPS - 1):
        nearby = along_planes(answer) + plane_neighbours(answer, NX)
        answer = answer + DAMPING * (source - diagonal * answer + 0.5 * nearby) / diagonal
    return jnp.sum(orbital * answer, axis=0)


def gathered_plan(potentials, orbitals, energies, local_potential, inverse_factor):
    slab_depth = potentials.shape[1]
    count = orbitals.shape[0]
    cells = local_potential.size
    grid_index = lax.axis_index("grid")
    local_here = lax.dynamic_slice_in_dim(local_potential, grid_index * slab_depth, slab_depth, 0)
    blocks = 4 if count % 4 == 0 else 1
    block_size = count // blocks
    response = jnp.zeros(potentials.shape, jnp.float32)
    for number in range(blocks):
        orbital_block = orbitals[number * block_size : (number + 1) * block_size]
        gathered = lax.all_gather(orbital_block, "pot", axis=2, tiled=True)
        energy_block = energies[number * block_size : (number + 1) * block_size]
        response = response + absorb(gathered, energy_block, potentials, local_here, across_slabs)
    trial_block = (potentials + 4.0 / count * response).astype(jnp.bfloat16)
    by_cells = lax.all_to_all(trial_block, "pot", split_axis=2, concat_axis=0, tiled=True)
    row_count = by_cells.shape[0]
    flattened = by_cells.reshape(row_count, -1)
    partial_margins = lax.dot_general(
        flattened, flattened, (((1,), (1,)), ((), ())), preferred_element_type=jnp.float32
    )
    combined = jnp.dot(inverse_factor, flattened, preferred_element_type=jnp.float32).reshape(
        by_cells.shape
    )
    updated = lax.all_to_all(combined, "pot", split_axis=0, concat_axis=2, tiled=True)
    scattered = lax.psum_scatter(partial_margins, "pot", scatter_dimension=0, tiled=True)
    own_rows = lax.psum(scattered, "grid")
    margins = own_rows / cells
    return (updated, margins)


def halo_rows(depth):
    return [(d, d - HALO, depth + 2 * (HALO - d)) for d in range(1, HALO + 1)]


def lane_halves(shape):
    return lax.broadcasted_iota(jnp.int32, shape, len(shape) - 1) < NX


def pack_kernel(v_ref, orb_ref, own_ref, low_ref, high_ref):
    fields, depth, width = v_ref.shape
    half = orb_ref.shape[0] // 2
    orb = jnp.transpose(orb_ref[...].astype(jnp.float32), (1, 0, 2))
    pot = jnp.transpose(v_ref[...], (1, 0, 2))
    left_o = lane_halves((half, LANES))
    left_v = lane_halves((fields, LANES))
    for z in range(depth):
        for m in range(width // LANES):
            lanes = slice(m * LANES, (m + 1) * LANES)
            first = orb[z, :half, lanes]
            second = orb[z, half:, lanes]
            value = pot[z, :, lanes]
            upper = value.astype(jnp.bfloat16).astype(jnp.float32)
            lower = value - upper
            pairs = (
                (
                    jnp.where(left_o, first, pltpu.roll(second, NX, 1)),
                    jnp.where(left_v, upper, pltpu.roll(lower, NX, 1)),
                ),
                (
                    jnp.where(left_o, pltpu.roll(first, NX, 1), second),
                    jnp.where(left_v, pltpu.roll(upper, NX, 1), lower),
                ),
            )
            for odd, (o, v) in enumerate(pairs):
                y = 2 * m + odd
                tile = jnp.concatenate([o, v], axis=0).astype(jnp.bfloat16)
                own_ref[z, y] = tile
                if z < HALO:
                    low_ref[z, y] = tile
                if z >= depth - HALO:
                    high_ref[z - (depth - HALO), y] = tile


def rows_kernel(own_ref, below_ref, above_ref, a_ref, b_ref):
    depth, rows = own_ref.shape[:2]
    even = lax.rem(lax.axis_index("pot"), 2) == 0

    def fill(out_ref, top):
        at = 0
        for d, start, planes in halo_rows(depth):
            y = jnp.where(top, rows - d, d - 1)
            for z in range(start, start + planes):
                if z < 0:
                    out_ref[at] = below_ref[z + HALO, y]
                elif z < depth:
                    out_ref[at] = own_ref[z, y]
                else:
                    out_ref[at] = above_ref[z - depth, y]
                at += 1

    fill(a_ref, even)
    fill(b_ref, jnp.logical_not(even))


def sweep_kernel(
    energy_ref, own_ref, below_ref, above_ref, a_ref, b_ref, lp_ref, inverse_ref,
    out_ref, r_ref, o_ref, v_ref, x_ref, y_ref, acc_ref, m_ref, lp_rows_ref,
):
    depth, rows = own_ref.shape[:2]
    planes_all, plane_cells = lp_ref.shape
    rows_all = plane_cells // NX
    fields = v_ref.shape[2]
    half = o_ref.shape[2]
    count = 2 * half
    row_index = lax.axis_index("pot")
    even = lax.rem(row_index, 2) == 0
    z_base = lax.axis_index("grid") * depth
    y_base = row_index * rows

    left = lane_halves((half, LANES))
    row_of = lax.broadcasted_iota(jnp.int32, (half, LANES), 0)
    shift = jnp.zeros((half, LANES), jnp.float32)
    for q in range(half):
        pair = jnp.where(left, 3.0 - energy_ref[q], 3.0 - energy_ref[q + half])
        shift = jnp.where(row_of == q, pair, shift)
    for m in range(lp_rows_ref.shape[0]):
        at = jnp.clip((y_base - LEAD) // 2 + m, 0, rows_all // 2 - 1) * LANES
        lp_rows_ref[m] = lp_ref[:, pl.ds(pl.multiple_of(at, LANES), LANES)]
    right_half = lax.broadcasted_iota(jnp.int32, (1, LANES), 1) >= NX

    def place(tile, z, y):
        zg = z_base + z
        yg = y_base + y
        inside = (zg >= 0) & (zg < planes_all) & (yg >= 0) & (yg < rows_all)
        zc = jnp.clip(zg, 0, planes_all - 1)
        pair = lp_rows_ref[lax.div(y + LEAD, 2), pl.ds(zc, 1), :]
        own_half = right_half == (lax.rem(y + LEAD, 2) == 1)
        lp = jnp.where(own_half, pair, pltpu.roll(pair, NX, 1))
        zi, yi = z + HALO, y + HALO
        scale = jnp.where(inside, 0.5 * DAMPING, 0.0)
        r_ref[zi, yi] = scale / (shift + lp)
        wide = tile.astype(jnp.float32)
        o_ref[zi, yi] = -2.0 * wide[:half]
        packed = wide[half:]
        v_ref[zi, yi] = packed + pltpu.roll(packed, NX, 1)

    def plane(z, carry):
        for y in range(rows):
            place(own_ref[z, y], z, y)
        return carry

    lax.fori_loop(0, depth, plane, 0)

    def side(k, carry):
        for y in range(rows):
            place(below_ref[k, y], k - HALO, y)
            place(above_ref[k, y], k + depth, y)
        return carry

    lax.fori_loop(0, HALO, side, 0)
    at = 0
    for d, start, planes in halo_rows(depth):
        y_a = jnp.where(even, rows - 1 + d, -d)
        y_b = jnp.where(even, -d, rows - 1 + d)

        def edge(k, carry, at=at, start=start, y_a=y_a, y_b=y_b):
            place(a_ref[at + k], start + k, y_a)
            place(b_ref[at + k], start + k, y_b)
            return carry

        lax.fori_loop(0, planes, edge, 0)
        at += planes

    lane = lax.broadcasted_iota(jnp.int32, (fields, LANES), 1) % NX
    first_x = lane == 0
    last_x = lane == NX - 1
    buffers = (x_ref, y_ref)
    acc_ref[...] = jnp.zeros_like(acc_ref)

    def orbital_pair(q, carry):
        def stage(number, z, reach):
            source = buffers[(number + 1) % 2]
            target = buffers[number % 2]
            coeff = COEFFS[SWEEPS - 1 - number]
            here = None
            for y in range(HALO - reach, HALO + rows + reach):
                r = r_ref[z, y, pl.ds(q, 1), :]
                o = o_ref[z, y, pl.ds(q, 1), :]
                s = (coeff * o) * v_ref[z, y]
                if number == 0:
                    target[z, y] = r * s
                    continue
                if here is None:
                    before, here = source[z, y - 1], source[z, y]
                after = source[z, y + 1]
                near = (before + after) + (source[z - 1, y] + source[z + 1, y])
                near = near + jnp.where(first_x, 0.0, pltpu.roll(here, 1, 1))
                near = near + jnp.where(last_x, 0.0, pltpu.roll(here, LANES - 1, 1))
                new = r * (near + s)
                before, here = here, after
                if number == SWEEPS - 1:
                    acc_ref[z - HALO, y - HALO] += o * new
                else:
                    target[z, y] = new

        for number in range(SWEEPS):
            reach = HALO - number

            def inner(z, c, number=number, reach=reach):
                stage(number, z + HALO, reach)
                return c

            for d in range(1, reach + 1):
                stage(number, HALO - d, reach - d)
                stage(number, HALO + depth - 1 + d, reach - d)
            lax.fori_loop(0, depth, inner, 0)
        return carry

    lax.fori_loop(0, half, orbital_pair, 0)

    left = lane_halves((fields, LANES))
    factor = 4.0 / count * -0.5
    planes = []
    for z in range(depth):
        tiles = []
        for y in range(rows):
            acc = acc_ref[z, y]
            total = acc + pltpu.roll(acc, NX, 1)
            tiles.append(v_ref[z + HALO, y + HALO] + factor * total)
        pieces = [jnp.where(left, tiles[y], tiles[y + 1]) for y in range(0, rows, 2)]
        planes.append(jnp.concatenate(pieces, axis=1))
    stacked = jnp.concatenate(planes, axis=0).astype(jnp.bfloat16)
    size = depth * fields

    def iota(shape, dim):
        return lax.broadcasted_iota(jnp.int32, shape, dim)

    pick = (iota((size, fields), 0) // depth == iota((size, fields), 1)).astype(jnp.bfloat16)
    tile = (iota((fields, size), 1) % fields == iota((fields, size), 0)).astype(jnp.bfloat16)
    spread = jnp.dot(pick, inverse_ref[...], preferred_element_type=jnp.float32)
    spread = jnp.dot(spread.astype(jnp.bfloat16), tile, preferred_element_type=jnp.float32)
    same = iota((size, size), 0) % depth == iota((size, size), 1) // fields
    spread = jnp.where(same, spread, 0.0).astype(jnp.bfloat16)
    updated = jnp.dot(spread, stacked, preferred_element_type=jnp.float32)

    m_ref[...] = jnp.zeros_like(m_ref)
    gram = jnp.zeros((fields, fields), jnp.float32)
    for z in range(depth):
        one = planes[z].astype(jnp.bfloat16)
        gram = gram + lax.dot_general(
            one, one, (((1,), (1,)), ((), ())), preferred_element_type=jnp.float32
        )
    m_ref[:, :fields] = gram
    pieces = rows * NX // LANES
    for p in range(fields):
        for t in range(pieces):
            out_ref[p, t] = updated[p * depth : (p + 1) * depth, t * LANES : (t + 1) * LANES]
        out_ref[p, pieces] = jnp.broadcast_to(m_ref[p : p + 1, :], (depth, LANES))


VMEM = pl.BlockSpec(memory_space=pltpu.VMEM)
SMEM = pl.BlockSpec(memory_space=pltpu.SMEM)


def rows_plan(potentials, orbitals, energies, local_potential, inverse_factor):
    pots = lax.axis_size("pot")
    grids = lax.axis_size("grid")
    depth = potentials.shape[1]
    count, _, width = orbitals.shape
    rows = width // NX
    fields = pots
    half = count // 2
    f32, bf16 = jnp.float32, jnp.bfloat16
    shape = jax.ShapeDtypeStruct
    tile = (half + fields, LANES)

    blocks = potentials.reshape(depth, pots, width).transpose(1, 0, 2)
    by_rows = lax.all_to_all(blocks, "pot", 0, 0, tiled=True)

    own, low, high = pl.pallas_call(
        pack_kernel,
        out_shape=[
            shape((depth, rows) + tile, bf16),
            shape((HALO, rows) + tile, bf16),
            shape((HALO, rows) + tile, bf16),
        ],
        in_specs=[VMEM] * 2,
        out_specs=[VMEM] * 3,
        name="pack",
    )(by_rows, orbitals)

    forward = [(i, i + 1) for i in range(grids - 1)]
    below = lax.ppermute(high, "grid", forward)
    above = lax.ppermute(low, "grid", [(t, s) for s, t in forward])

    edge = sum(planes for _, _, planes in halo_rows(depth))
    to_a, to_b = pl.pallas_call(
        rows_kernel,
        out_shape=[shape((edge,) + tile, bf16)] * 2,
        in_specs=[VMEM] * 3,
        out_specs=[VMEM] * 2,
        name="rows",
    )(own, below, above)
    pairs_a = [(i, i ^ 1) for i in range(pots)]
    pairs_b = [(i, i + 1 if i % 2 else i - 1) for i in range(1, pots - 1)]
    got_a = lax.ppermute(to_a, "pot", pairs_a)
    got_b = lax.ppermute(to_b, "pot", pairs_b)

    region = (depth + 2 * HALO, rows + 2 * HALO)
    pieces = width // LANES
    sent = pl.pallas_call(
        sweep_kernel,
        out_shape=shape((fields, pieces + 1, depth, LANES), f32),
        in_specs=[SMEM] + [VMEM] * 7,
        out_specs=VMEM,
        scratch_shapes=[
            pltpu.VMEM(region + (half, LANES), f32),
            pltpu.VMEM(region + (half, LANES), f32),
            pltpu.VMEM(region + (fields, LANES), f32),
            pltpu.VMEM(region + (fields, LANES), f32),
            pltpu.VMEM(region + (fields, LANES), f32),
            pltpu.VMEM((depth, rows, fields, LANES), f32),
            pltpu.VMEM((fields, LANES), f32),
            pltpu.VMEM((rows // 2 + LEAD, local_potential.shape[0], LANES), f32),
        ],
        name="sweeps",
    )(energies, own, below, above, got_a, got_b, local_potential, inverse_factor)

    back = lax.all_to_all(sent, "pot", 0, 0, tiled=True)
    updated = back[:, :pieces].reshape(pots * pieces, depth, LANES).transpose(1, 0, 2)
    updated = updated.reshape(1, depth, pots * width)
    margins = jnp.sum(back[:, pieces], axis=0)
    step = 1
    while step < grids:
        margins = margins + lax.ppermute(margins, "grid", [(i, i ^ step) for i in range(grids)])
        step *= 2
    margins = margins[:1, :fields] / local_potential.size
    return updated, margins


def local(potentials, orbitals, energies, local_potential, inverse_factor):
    pots = lax.axis_size("pot")
    grids = lax.axis_size("grid")
    depth = potentials.shape[1]
    count, _, width = orbitals.shape
    fits = (
        potentials.shape[0] == 1
        and pots == 8
        and width % LANES == 0
        and LANES == 2 * NX
        and width // NX >= HALO
        and depth == 8
        and count % 32 == 0
        and grids & (grids - 1) == 0
    )
    plan = rows_plan if fits else gathered_plan
    return plan(potentials, orbitals, energies, local_potential, inverse_factor)


def solution(mesh):
    in_specs = (P("pot", "grid", None), P(None, "grid", "pot"), P(), P(), P())
    out_specs = (P("pot", "grid", None), P("pot", None))
    return jax.shard_map(local, mesh=mesh, in_specs=in_specs, out_specs=out_specs, check_vma=False)
```

```python
import math

import jax
import jax.numpy as jnp
from jax import lax
from jax.experimental import pallas as pl
from jax.experimental.pallas import tpu as pltpu
from jax.sharding import PartitionSpec as P

NX = 64
SWEEPS = 4
DAMPING = 0.8
COEFFS = tuple(
    sum(math.comb(n, m) * (1.0 - DAMPING) ** (n - m) for n in range(m, SWEEPS))
    for m in range(SWEEPS)
)
HALO = SWEEPS - 1
LEAD = HALO + HALO % 2
LANES = 128


def padded_2(block, sides, width):
    for axis, dim in sides:
        count = lax.axis_size(axis)
        forward = [(i, i + 1) for i in range(count - 1)]
        backward = [(target, source) for source, target in forward]
        low = lax.ppermute(
            lax.slice_in_dim(block, block.shape[dim] - width, None, axis=dim), axis, forward
        )
        high = lax.ppermute(lax.slice_in_dim(block, 0, width, axis=dim), axis, backward)
        block = jnp.concatenate([low, block, high], axis=dim)
    return block


def plane_neighbours(field, row_width):
    plane_size = field.shape[-1]
    widths = [(0, 0)] * (field.ndim - 1)
    padded = jnp.pad(field, widths + [(row_width, row_width)])
    along_y = padded[..., 2 * row_width :] + padded[..., :plane_size]
    column = jnp.arange(plane_size, dtype=jnp.int32) % row_width
    padded = jnp.pad(field, widths + [(1, 1)])
    right_side = jnp.where(column == row_width - 1, 0.0, padded[..., 2:])
    left_side = jnp.where(column == 0, 0.0, padded[..., :plane_size])
    return along_y + right_side + left_side


def across_slabs(answer):
    padded = padded_2(answer, (("grid", 2),), 1)
    return padded[:, :, 2:] + padded[:, :, :-2]


def absorb(orbital_block, energy_block, fields, local_here, along_planes):
    orbital = orbital_block.astype(jnp.float32)[:, None]
    diagonal = (3.0 + local_here[None] - energy_block[:, None, None])[:, None]
    source = -orbital * fields[None]
    answer = DAMPING * source / diagonal
    for sweep_index in range(SWEEPS - 1):
        nearby = along_planes(answer) + plane_neighbours(answer, NX)
        answer = answer + DAMPING * (source - diagonal * answer + 0.5 * nearby) / diagonal
    return jnp.sum(orbital * answer, axis=0)


def gathered_plan(potentials, orbitals, energies, local_potential, inverse_factor):
    slab_depth = potentials.shape[1]
    count = orbitals.shape[0]
    cells = local_potential.size
    grid_index = lax.axis_index("grid")
    local_here = lax.dynamic_slice_in_dim(local_potential, grid_index * slab_depth, slab_depth, 0)
    blocks = 4 if count % 4 == 0 else 1
    block_size = count // blocks
    response = jnp.zeros(potentials.shape, jnp.float32)
    for number in range(blocks):
        orbital_block = orbitals[number * block_size : (number + 1) * block_size]
        gathered = lax.all_gather(orbital_block, "pot", axis=2, tiled=True)
        energy_block = energies[number * block_size : (number + 1) * block_size]
        response = response + absorb(gathered, energy_block, potentials, local_here, across_slabs)
    trial_block = (potentials + 4.0 / count * response).astype(jnp.bfloat16)
    by_cells = lax.all_to_all(trial_block, "pot", split_axis=2, concat_axis=0, tiled=True)
    row_count = by_cells.shape[0]
    flattened = by_cells.reshape(row_count, -1)
    partial_margins = lax.dot_general(
        flattened, flattened, (((1,), (1,)), ((), ())), preferred_element_type=jnp.float32
    )
    combined = jnp.dot(inverse_factor, flattened, preferred_element_type=jnp.float32).reshape(
        by_cells.shape
    )
    updated = lax.all_to_all(combined, "pot", split_axis=0, concat_axis=2, tiled=True)
    scattered = lax.psum_scatter(partial_margins, "pot", scatter_dimension=0, tiled=True)
    own_rows = lax.psum(scattered, "grid")
    margins = own_rows / cells
    return (updated, margins)


def halo_rows(depth):
    return [(d, d - HALO, depth + 2 * (HALO - d)) for d in range(1, HALO + 1)]


def iota(shape, dim):
    return lax.broadcasted_iota(jnp.int32, shape, dim)


def bf16_dot(a, b):
    return jnp.dot(a, b, preferred_element_type=jnp.float32)


def one_hot(mask):
    return mask.astype(jnp.float32).astype(jnp.bfloat16)


def lane_halves(shape):
    return iota(shape, len(shape) - 1) < NX


SPLIT = 4
STEPS = NX // SPLIT
BATCH = LANES // STEPS


def pack_kernel(v_ref, orb_ref, own_ref, low_ref, high_ref, s_ref):
    fields, depth, width = v_ref.shape
    count = orb_ref.shape[0]
    groups = count // BATCH
    rows = width // NX
    lane_in, lane_out = iota((LANES, LANES), 0), iota((LANES, LANES), 1)
    wanted = (lane_out // NX) * NX + SPLIT * (lane_out % STEPS) + lane_out // STEPS % SPLIT
    permute = one_hot(lane_in == wanted)
    lane = iota((depth, LANES), 1) // STEPS
    for t in range(width // LANES):
        lanes = slice(t * LANES, (t + 1) * LANES)
        tile = orb_ref[:, :, lanes].astype(jnp.float32).reshape(count * depth, LANES)
        tile = bf16_dot(tile.astype(jnp.bfloat16), permute)
        for g in range(groups):
            first = g * BATCH * depth
            regs = [tile[first + b * depth : first + (b + 1) * depth] for b in range(BATCH)]
            step = BATCH // 2
            while step:
                stays = lane // step % 2 == 0
                for b in range(BATCH):
                    if b & step == 0:
                        lo, hi = regs[b], regs[b + step]
                        regs[b] = jnp.where(stays, lo, pltpu.roll(hi, step * STEPS, 1))
                        regs[b + step] = jnp.where(
                            stays, pltpu.roll(lo, LANES - step * STEPS, 1), hi
                        )
                step //= 2
            for c in range(BATCH):
                y, m = 2 * t + c // SPLIT, c % SPLIT
                at = ((m * groups + g) * rows + y) * depth
                s_ref[at : at + depth] = regs[c]
    pot = jnp.transpose(v_ref[...], (1, 0, 2))
    left = lane_halves((fields, LANES))
    for z in range(depth):
        for y in range(rows):
            o = s_ref[pl.ds(y * depth + z, SPLIT * groups, stride=rows * depth), :]
            value = pot[z, :, y // 2 * LANES : (y // 2 + 1) * LANES]
            upper = value.astype(jnp.bfloat16).astype(jnp.float32)
            lower = value - upper
            if y % 2:
                v = jnp.where(left, pltpu.roll(upper, NX, 1), lower)
            else:
                v = jnp.where(left, upper, pltpu.roll(lower, NX, 1))
            tile = jnp.concatenate([o, v], axis=0).astype(jnp.bfloat16)
            own_ref[z, y] = tile
            if z < HALO:
                low_ref[z, y] = tile
            if z >= depth - HALO:
                high_ref[z - (depth - HALO), y] = tile


def split_kernel(energy_ref, lp_ref, r_ref, *part_refs):
    planes_all, plane_cells = lp_ref.shape
    rows_all = plane_cells // NX
    region_z, region_y, size, _ = r_ref.shape
    depth, rows = region_z - 2 * HALO, region_y - 2 * HALO
    groups = size // SPLIT
    z_base = lax.axis_index("grid") * depth
    y_base = lax.axis_index("pot") * rows

    shift = jnp.zeros((size, LANES), jnp.float32)
    group_of = iota((size, LANES), 0) % groups
    member = iota((size, LANES), 1) // STEPS
    for g in range(groups):
        for b in range(BATCH):
            here = (group_of == g) & (member == b)
            shift = jnp.where(here, 3.0 - energy_ref[g * BATCH + b], shift)

    pairs = part_refs[0].shape[0]
    for p in range(pairs):
        at = jnp.clip((y_base - LEAD) // 2 + p, 0, rows_all // 2 - 1) * LANES
        rest = lp_ref[:, pl.ds(pl.multiple_of(at, LANES), LANES)]
        for part_ref in part_refs:
            part = rest.astype(jnp.bfloat16).astype(jnp.float32)
            part_ref[p] = part
            rest = rest - part
    from_lane, to_lane = iota((LANES, 2 * LANES), 0), iota((LANES, 2 * LANES), 1)
    pick = one_hot(
        (from_lane // NX == to_lane // LANES) & (from_lane % NX // SPLIT == to_lane % STEPS)
    )
    keep = iota((size, LANES), 1) % SPLIT == iota((size, LANES), 0) // groups

    def plane(zi, carry):
        zg = z_base + zi - HALO
        z_inside = (zg >= 0) & (zg < planes_all)
        zc = jnp.clip(zg, 0, planes_all - 1)
        for p in range(pairs):
            spread = [
                jnp.where(keep, jnp.broadcast_to(ref[p, pl.ds(zc, 1), :], keep.shape), 0.0)
                for ref in part_refs
            ]
            stacked = jnp.concatenate(spread, axis=0).astype(jnp.bfloat16)
            parts = bf16_dot(stacked, pick)
            lp = (parts[:size] + parts[size : 2 * size]) + parts[2 * size :]
            for odd in range(2):
                y = 2 * p + odd - LEAD
                if -HALO <= y < rows + HALO:
                    yg = y_base + y
                    inside = z_inside & (yg >= 0) & (yg < rows_all)
                    scale = jnp.where(inside, 0.5 * DAMPING, 0.0)
                    value = shift + lp[:, odd * LANES : (odd + 1) * LANES]
                    r_ref[zi, y + HALO] = scale / value
        return carry

    lax.fori_loop(0, region_z, plane, 0)


def rows_kernel(own_ref, below_ref, above_ref, a_ref, b_ref):
    depth, rows = own_ref.shape[:2]
    even = lax.rem(lax.axis_index("pot"), 2) == 0

    def fill(out_ref, top):
        at = 0
        for d, start, planes in halo_rows(depth):
            y = jnp.where(top, rows - d, d - 1)
            for z in range(start, start + planes):
                if z < 0:
                    out_ref[at] = below_ref[z + HALO, y]
                elif z < depth:
                    out_ref[at] = own_ref[z, y]
                else:
                    out_ref[at] = above_ref[z - depth, y]
                at += 1

    fill(a_ref, even)
    fill(b_ref, jnp.logical_not(even))


def sweep_kernel(
    own_ref, below_ref, above_ref, a_ref, b_ref, r_ref, inverse_ref,
    out_ref, o_ref, ro_ref, v_ref, first_ref, x_ref, y_ref, acc_ref, m_ref,
):
    depth, rows = own_ref.shape[:2]
    fields = v_ref.shape[3]
    size = o_ref.shape[2]
    groups = size // SPLIT
    count = groups * BATCH
    even = lax.rem(lax.axis_index("pot"), 2) == 0

    from_lane = iota((LANES, SPLIT * LANES), 0)
    to_lane = iota((LANES, SPLIT * LANES), 1)
    spread = one_hot(from_lane % NX == SPLIT * (to_lane % STEPS) + to_lane // LANES)

    def place(tiles):
        wide = [tile.astype(jnp.float32) for tile, _, _ in tiles]
        packed = jnp.concatenate([w[size:] for w in wide], axis=0).astype(jnp.bfloat16)
        values = bf16_dot(packed, spread)
        for number, (_, z, y) in enumerate(tiles):
            zi, yi = z + HALO, y + HALO
            o = -2.0 * wide[number][:size]
            o_ref[zi, yi] = o
            ro_ref[zi, yi] = r_ref[zi, yi] * o
            for m in range(SPLIT):
                v_ref[zi, yi, m] = values[
                    number * fields : (number + 1) * fields, m * LANES : (m + 1) * LANES
                ]

    def plane(z, carry):
        place([(own_ref[z, y], z, y) for y in range(rows)])
        return carry

    lax.fori_loop(0, depth, plane, 0)

    def side(k, carry):
        place([(below_ref[k, y], k - HALO, y) for y in range(rows)])
        place([(above_ref[k, y], k + depth, y) for y in range(rows)])
        return carry

    lax.fori_loop(0, HALO, side, 0)
    at = 0
    for d, start, planes in halo_rows(depth):
        y_a = jnp.where(even, rows - 1 + d, -d)
        y_b = jnp.where(even, -d, rows - 1 + d)

        def edge(k, carry, at=at, start=start, y_a=y_a, y_b=y_b):
            place(
                [(a_ref[at + 2 * k + i], start + 2 * k + i, y_a) for i in range(2)]
                + [(b_ref[at + 2 * k + i], start + 2 * k + i, y_b) for i in range(2)]
            )
            return carry

        lax.fori_loop(0, planes // 2, edge, 0)
        at += planes

    step = iota((fields, LANES), 1) % STEPS
    first_k = step == 0
    last_k = step == STEPS - 1
    buffers = (first_ref, x_ref, y_ref)
    acc_ref[...] = jnp.zeros_like(acc_ref)

    def group(g, carry):
        def stage(number, z, reach, deep):
            coeff = COEFFS[SWEEPS - 1 - number]
            target = buffers[min(number, SWEEPS - 2)]
            source = buffers[number - 1]

            def of_group(ref, i, y, m):
                return jnp.broadcast_to(ref[z + i, y, pl.ds(m * groups + g, 1), :], (fields, LANES))

            def row(i, y):
                return [source[z + i, y, m] for m in range(SPLIT)]

            ys = range(HALO - reach, HALO + rows + reach)
            if number == 0:
                for i in range(deep):
                    for y in ys:
                        for m in range(SPLIT):
                            target[z + i, y, m] = of_group(ro_ref, i, y, m) * v_ref[z + i, y, m]
                return
            before = [row(i, ys[0] - 1) for i in range(deep)]
            here = [row(i, ys[0]) for i in range(deep)]
            for y in ys:
                after = [row(i, y + 1) for i in range(deep)]
                under, over = row(-1, y), row(deep, y)
                for i in range(deep):
                    lower = here[i - 1] if i else under
                    upper = here[i + 1] if i + 1 < deep else over
                    mid = here[i]
                    for m in range(SPLIT):
                        if m:
                            left = mid[m - 1]
                        else:
                            left = jnp.where(first_k, 0.0, pltpu.roll(mid[SPLIT - 1], 1, 1))
                        if m + 1 < SPLIT:
                            right = mid[m + 1]
                        else:
                            right = jnp.where(last_k, 0.0, pltpu.roll(mid[0], LANES - 1, 1))
                        near = (before[i][m] + after[i][m]) + (lower[m] + upper[m])
                        near = near + (left + right)
                        base = mid[m] if number == 1 else first_ref[z + i, y, m]
                        new = of_group(r_ref, i, y, m) * near + coeff * base
                        if number == SWEEPS - 1:
                            acc_ref[z + i - HALO, y - HALO, m] += of_group(o_ref, i, y, m) * new
                        else:
                            target[z + i, y, m] = new
                before, here = here, after

        for number in range(SWEEPS):
            reach = HALO - number

            def inner(pair, c, number=number, reach=reach):
                stage(number, HALO + 2 * pair, reach, 2)
                return c

            for d in range(1, reach + 1):
                stage(number, HALO - d, reach - d, 1)
                stage(number, HALO + depth - 1 + d, reach - d, 1)
            lax.fori_loop(0, depth // 2, inner, 0)
        return carry

    lax.fori_loop(0, groups, group, 0)

    lane_in, x_out = iota((SPLIT * LANES, LANES), 0), iota((SPLIT * LANES, LANES), 1) % NX
    gather = one_hot(x_out == SPLIT * (lane_in % STEPS) + lane_in // LANES)
    left = lane_halves((fields, LANES))
    factor = 4.0 / count * -0.5
    planes = []
    for z in range(depth):
        parts = [
            jnp.concatenate([acc_ref[z, y, m] for y in range(rows)], axis=0) for m in range(SPLIT)
        ]
        acc = jnp.concatenate(parts, axis=1)
        upper = acc.astype(jnp.bfloat16)
        lower = (acc - upper.astype(jnp.float32)).astype(jnp.bfloat16)
        total = bf16_dot(upper, gather) + bf16_dot(lower, gather)
        tiles = []
        for y in range(rows):
            packed = own_ref[z, y].astype(jnp.float32)[size:]
            value = packed + pltpu.roll(packed, NX, 1)
            tiles.append(value + factor * total[y * fields : (y + 1) * fields])
        pieces = [jnp.where(left, tiles[y], tiles[y + 1]) for y in range(0, rows, 2)]
        planes.append(jnp.concatenate(pieces, axis=1))
    stacked = jnp.concatenate(planes, axis=0).astype(jnp.bfloat16)
    all_rows = depth * fields

    pick = one_hot(iota((all_rows, fields), 0) // depth == iota((all_rows, fields), 1))
    tile = one_hot(iota((fields, all_rows), 1) % fields == iota((fields, all_rows), 0))
    wide = bf16_dot(bf16_dot(pick, inverse_ref[...]).astype(jnp.bfloat16), tile)
    square = (all_rows, all_rows)
    same = iota(square, 0) % depth == iota(square, 1) // fields
    wide = jnp.where(same, wide, 0.0).astype(jnp.bfloat16)
    updated = bf16_dot(wide, stacked)

    m_ref[...] = jnp.zeros_like(m_ref)
    gram = jnp.zeros((fields, fields), jnp.float32)
    for z in range(depth):
        one = planes[z].astype(jnp.bfloat16)
        gram = gram + lax.dot_general(
            one, one, (((1,), (1,)), ((), ())), preferred_element_type=jnp.float32
        )
    m_ref[:, :fields] = gram
    pieces = rows * NX // LANES
    for p in range(fields):
        for t in range(pieces):
            out_ref[p, t] = updated[p * depth : (p + 1) * depth, t * LANES : (t + 1) * LANES]
        out_ref[p, pieces] = jnp.broadcast_to(m_ref[p : p + 1, :], (depth, LANES))


VMEM = pl.BlockSpec(memory_space=pltpu.VMEM)
SMEM = pl.BlockSpec(memory_space=pltpu.SMEM)


def rows_plan(potentials, orbitals, energies, local_potential, inverse_factor):
    pots = lax.axis_size("pot")
    grids = lax.axis_size("grid")
    depth = potentials.shape[1]
    count, _, width = orbitals.shape
    rows = width // NX
    fields = pots
    half = count // 2
    f32, bf16 = jnp.float32, jnp.bfloat16
    shape = jax.ShapeDtypeStruct
    tile = (half + fields, LANES)

    blocks = potentials.reshape(depth, pots, width).transpose(1, 0, 2)
    by_rows = lax.all_to_all(blocks, "pot", 0, 0, tiled=True)

    own, low, high = pl.pallas_call(
        pack_kernel,
        out_shape=[
            shape((depth, rows) + tile, bf16),
            shape((HALO, rows) + tile, bf16),
            shape((HALO, rows) + tile, bf16),
        ],
        in_specs=[VMEM] * 2,
        out_specs=[VMEM] * 3,
        scratch_shapes=[pltpu.VMEM((half * depth * rows, LANES), f32)],
        name="pack",
    )(by_rows, orbitals)

    forward = [(i, i + 1) for i in range(grids - 1)]
    below = lax.ppermute(high, "grid", forward)
    above = lax.ppermute(low, "grid", [(t, s) for s, t in forward])

    edge = sum(planes for _, _, planes in halo_rows(depth))
    to_a, to_b = pl.pallas_call(
        rows_kernel,
        out_shape=[shape((edge,) + tile, bf16)] * 2,
        in_specs=[VMEM] * 3,
        out_specs=[VMEM] * 2,
        name="rows",
    )(own, below, above)
    pairs_a = [(i, i ^ 1) for i in range(pots)]
    pairs_b = [(i, i + 1 if i % 2 else i - 1) for i in range(1, pots - 1)]
    got_a = lax.ppermute(to_a, "pot", pairs_a)
    got_b = lax.ppermute(to_b, "pot", pairs_b)

    region = (depth + 2 * HALO, rows + 2 * HALO)
    inverse_diagonal = pl.pallas_call(
        split_kernel,
        out_shape=shape(region + (half, LANES), f32),
        in_specs=[SMEM, VMEM],
        out_specs=VMEM,
        scratch_shapes=[pltpu.VMEM((rows // 2 + LEAD, local_potential.shape[0], LANES), f32)] * 3,
        name="diagonal",
    )(energies, local_potential)
    pieces = width // LANES
    sent = pl.pallas_call(
        sweep_kernel,
        out_shape=shape((fields, pieces + 1, depth, LANES), f32),
        in_specs=[VMEM] * 7,
        out_specs=VMEM,
        scratch_shapes=[
            pltpu.VMEM(region + (half, LANES), f32),
            pltpu.VMEM(region + (half, LANES), f32),
            pltpu.VMEM(region + (SPLIT, fields, LANES), f32),
            pltpu.VMEM(region + (SPLIT, fields, LANES), f32),
            pltpu.VMEM(region + (SPLIT, fields, LANES), f32),
            pltpu.VMEM(region + (SPLIT, fields, LANES), f32),
            pltpu.VMEM((depth, rows, SPLIT, fields, LANES), f32),
            pltpu.VMEM((fields, LANES), f32),
        ],
        name="sweeps",
    )(own, below, above, got_a, got_b, inverse_diagonal, inverse_factor)

    back = lax.all_to_all(sent, "pot", 0, 0, tiled=True)
    updated = back[:, :pieces].reshape(pots * pieces, depth, LANES).transpose(1, 0, 2)
    updated = updated.reshape(1, depth, pots * width)
    margins = jnp.sum(back[:, pieces], axis=0)
    step = 1
    while step < grids:
        margins = margins + lax.ppermute(margins, "grid", [(i, i ^ step) for i in range(grids)])
        step *= 2
    margins = margins[:1, :fields] / local_potential.size
    return updated, margins


def local(potentials, orbitals, energies, local_potential, inverse_factor):
    pots = lax.axis_size("pot")
    grids = lax.axis_size("grid")
    depth = potentials.shape[1]
    count, _, width = orbitals.shape
    fits = (
        potentials.shape[0] == 1
        and pots == 8
        and width % LANES == 0
        and LANES == 2 * NX
        and width // NX >= HALO
        and depth == 8
        and count % 32 == 0
        and grids & (grids - 1) == 0
    )
    plan = rows_plan if fits else gathered_plan
    return plan(potentials, orbitals, energies, local_potential, inverse_factor)


def solution(mesh):
    in_specs = (P("pot", "grid", None), P(None, "grid", "pot"), P(), P(), P())
    out_specs = (P("pot", "grid", None), P("pot", None))
    return jax.shard_map(local, mesh=mesh, in_specs=in_specs, out_specs=out_specs, check_vma=False)
```

```python
import math

import jax
import jax.numpy as jnp
from jax import lax
from jax.experimental import pallas as pl
from jax.experimental.pallas import tpu as pltpu
from jax.sharding import PartitionSpec as P

NX = 64
SWEEPS = 4
DAMPING = 0.8
COEFFS = tuple(
    sum(math.comb(n, m) * (1.0 - DAMPING) ** (n - m) for n in range(m, SWEEPS))
    for m in range(SWEEPS)
)
HALO = SWEEPS - 1
LEAD = HALO + HALO % 2
LANES = 128
SUBLANES = 8


def padded_2(block, sides, width):
    for axis, dim in sides:
        count = lax.axis_size(axis)
        forward = [(i, i + 1) for i in range(count - 1)]
        backward = [(target, source) for source, target in forward]
        low = lax.ppermute(
            lax.slice_in_dim(block, block.shape[dim] - width, None, axis=dim), axis, forward
        )
        high = lax.ppermute(lax.slice_in_dim(block, 0, width, axis=dim), axis, backward)
        block = jnp.concatenate([low, block, high], axis=dim)
    return block


def plane_neighbours(field, row_width):
    plane_size = field.shape[-1]
    widths = [(0, 0)] * (field.ndim - 1)
    padded = jnp.pad(field, widths + [(row_width, row_width)])
    along_y = padded[..., 2 * row_width :] + padded[..., :plane_size]
    column = jnp.arange(plane_size, dtype=jnp.int32) % row_width
    padded = jnp.pad(field, widths + [(1, 1)])
    right_side = jnp.where(column == row_width - 1, 0.0, padded[..., 2:])
    left_side = jnp.where(column == 0, 0.0, padded[..., :plane_size])
    return along_y + right_side + left_side


def across_slabs(answer):
    padded = padded_2(answer, (("grid", 2),), 1)
    return padded[:, :, 2:] + padded[:, :, :-2]


def absorb(orbital_block, energy_block, fields, local_here, along_planes):
    orbital = orbital_block.astype(jnp.float32)[:, None]
    diagonal = (3.0 + local_here[None] - energy_block[:, None, None])[:, None]
    source = -orbital * fields[None]
    answer = DAMPING * source / diagonal
    for sweep_index in range(SWEEPS - 1):
        nearby = along_planes(answer) + plane_neighbours(answer, NX)
        answer = answer + DAMPING * (source - diagonal * answer + 0.5 * nearby) / diagonal
    return jnp.sum(orbital * answer, axis=0)


def gathered_plan(potentials, orbitals, energies, local_potential, inverse_factor):
    slab_depth = potentials.shape[1]
    count = orbitals.shape[0]
    cells = local_potential.size
    grid_index = lax.axis_index("grid")
    local_here = lax.dynamic_slice_in_dim(local_potential, grid_index * slab_depth, slab_depth, 0)
    blocks = 4 if count % 4 == 0 else 1
    block_size = count // blocks
    response = jnp.zeros(potentials.shape, jnp.float32)
    for number in range(blocks):
        orbital_block = orbitals[number * block_size : (number + 1) * block_size]
        gathered = lax.all_gather(orbital_block, "pot", axis=2, tiled=True)
        energy_block = energies[number * block_size : (number + 1) * block_size]
        response = response + absorb(gathered, energy_block, potentials, local_here, across_slabs)
    trial_block = (potentials + 4.0 / count * response).astype(jnp.bfloat16)
    by_cells = lax.all_to_all(trial_block, "pot", split_axis=2, concat_axis=0, tiled=True)
    row_count = by_cells.shape[0]
    flattened = by_cells.reshape(row_count, -1)
    partial_margins = lax.dot_general(
        flattened, flattened, (((1,), (1,)), ((), ())), preferred_element_type=jnp.float32
    )
    combined = jnp.dot(inverse_factor, flattened, preferred_element_type=jnp.float32).reshape(
        by_cells.shape
    )
    updated = lax.all_to_all(combined, "pot", split_axis=0, concat_axis=2, tiled=True)
    scattered = lax.psum_scatter(partial_margins, "pot", scatter_dimension=0, tiled=True)
    own_rows = lax.psum(scattered, "grid")
    margins = own_rows / cells
    return (updated, margins)


def halo_cells(depth):
    reach = [(d, z) for d in range(1, HALO + 1) for z in range(d - HALO, depth + HALO - d)]
    inner = [(d, z) for d, z in reach if 0 <= z < depth]
    return inner, [(d, z) for d, z in reach if not 0 <= z < depth]


def iota(shape, dim):
    return lax.broadcasted_iota(jnp.int32, shape, dim)


def bf16_dot(a, b):
    return jnp.dot(a, b, preferred_element_type=jnp.float32)


def one_hot(mask):
    return mask.astype(jnp.float32).astype(jnp.bfloat16)


def lane_halves(shape):
    return iota(shape, len(shape) - 1) < NX


SPLIT = 4
STEPS = NX // SPLIT
BATCH = LANES // STEPS


def orbital_kernel(orb_ref, s_ref):
    count, depth, width = orb_ref.shape
    groups = count // BATCH
    rows = width // NX
    lane_in, lane_out = iota((LANES, LANES), 0), iota((LANES, LANES), 1)
    wanted = (lane_out // NX) * NX + SPLIT * (lane_out % STEPS) + lane_out // STEPS % SPLIT
    permute = one_hot(lane_in == wanted)
    lane = iota((depth, LANES), 1) // STEPS
    for t in range(width // LANES):
        lanes = slice(t * LANES, (t + 1) * LANES)
        tile = orb_ref[:, :, lanes].astype(jnp.float32).reshape(count * depth, LANES)
        tile = bf16_dot(tile.astype(jnp.bfloat16), permute)
        for g in range(groups):
            first = g * BATCH * depth
            regs = [tile[first + b * depth : first + (b + 1) * depth] for b in range(BATCH)]
            step = BATCH // 2
            while step:
                stays = lane // step % 2 == 0
                for b in range(BATCH):
                    if b & step == 0:
                        lo, hi = regs[b], regs[b + step]
                        regs[b] = jnp.where(stays, lo, pltpu.roll(hi, step * STEPS, 1))
                        regs[b + step] = jnp.where(
                            stays, pltpu.roll(lo, LANES - step * STEPS, 1), hi
                        )
                step //= 2
            for c in range(BATCH):
                y, m = 2 * t + c // SPLIT, c % SPLIT
                at = ((m * groups + g) * rows + y) * depth
                s_ref[at : at + depth] = regs[c]


def pack_kernel(v_ref, s_ref, own_ref, low_ref, high_ref, a_ref, b_ref):
    fields, depth, width = v_ref.shape
    rows = width // NX
    size = s_ref.shape[0] // (rows * depth)
    even = lax.rem(lax.axis_index("pot"), 2) == 0
    pot = jnp.transpose(v_ref[...], (1, 0, 2))
    left = lane_halves((fields, LANES))
    for z in range(depth):
        for y in range(rows):
            o = s_ref[pl.ds(y * depth + z, size, stride=rows * depth), :]
            value = pot[z, :, y // 2 * LANES : (y // 2 + 1) * LANES]
            upper = value.astype(jnp.bfloat16).astype(jnp.float32)
            lower = value - upper
            if y % 2:
                v = jnp.where(left, pltpu.roll(upper, NX, 1), lower)
            else:
                v = jnp.where(left, upper, pltpu.roll(lower, NX, 1))
            tile = jnp.concatenate([o, v], axis=0).astype(jnp.bfloat16)
            own_ref[z, y] = tile
            if z < HALO:
                low_ref[z, y] = tile
            if z >= depth - HALO:
                high_ref[z - (depth - HALO), y] = tile
    for at, (d, z) in enumerate(halo_cells(depth)[0]):
        a_ref[at] = own_ref[z, jnp.where(even, rows - d, d - 1)]
        b_ref[at] = own_ref[z, jnp.where(even, d - 1, rows - d)]


def corner_kernel(below_ref, above_ref, a_in, b_in, a_ref, b_ref, sem_ref):
    rows = below_ref.shape[1]
    even = lax.rem(lax.axis_index("pot"), 2) == 0
    inner, corners = halo_cells(rows_depth(a_ref))
    depth = rows_depth(a_ref)
    copies = []
    for number, (d, z) in enumerate(corners):
        source = below_ref.at[z + HALO] if z < 0 else above_ref.at[z - depth]
        top, bottom = rows - d, d - 1
        for side, (out_ref, y) in enumerate(
            ((a_ref, jnp.where(even, top, bottom)), (b_ref, jnp.where(even, bottom, top)))
        ):
            copies.append(
                pltpu.make_async_copy(
                    source.at[y], out_ref.at[len(inner) + number], sem_ref.at[2 * number + side]
                )
            )
    for copy in copies:
        copy.start()
    for copy in copies:
        copy.wait()


def rows_depth(edge_ref):
    total = sum(2 * (HALO - d) for d in range(1, HALO + 1))
    return (edge_ref.shape[0] - total) // HALO


def diagonal_kernel(energy_ref, lp_ref, r_ref, lp_ref2, *part_refs):
    planes_all, plane_cells = lp_ref.shape
    rows_all = plane_cells // NX
    region_z, region_y, size, _ = r_ref.shape
    depth, rows = region_z - 2 * HALO, region_y - 2 * HALO
    groups = size // SPLIT
    z_base = lax.axis_index("grid") * depth
    y_base = lax.axis_index("pot") * rows

    shift = jnp.zeros((size, LANES), jnp.float32)
    group_of = iota((size, LANES), 0) % groups
    member = iota((size, LANES), 1) // STEPS
    for g in range(groups):
        for b in range(BATCH):
            here = (group_of == g) & (member == b)
            shift = jnp.where(here, 3.0 - energy_ref[g * BATCH + b], shift)

    pairs = part_refs[0].shape[0]
    for p in range(pairs):
        at = jnp.clip((y_base - LEAD) // 2 + p, 0, rows_all // 2 - 1) * LANES
        rest = lp_ref[:, pl.ds(pl.multiple_of(at, LANES), LANES)]
        for part_ref in part_refs:
            part = rest.astype(jnp.bfloat16).astype(jnp.float32)
            part_ref[p] = part
            rest = rest - part
    from_lane, to_lane = iota((LANES, 2 * LANES), 0), iota((LANES, 2 * LANES), 1)
    pick = one_hot(
        (from_lane // NX == to_lane // LANES) & (from_lane % NX // SPLIT == to_lane % STEPS)
    )
    tile = (SUBLANES, LANES)
    keep = iota(tile, 1) % SPLIT == iota(tile, 0) % SPLIT
    per_tile = SUBLANES // SPLIT
    plane_of = iota(tile, 0) // SPLIT

    def clipped(zi):
        return jnp.clip(z_base + zi - HALO, 0, planes_all - 1)

    def chosen(index, values):
        out = jnp.broadcast_to(values[0], tile)
        for number, value in enumerate(values[1:], 1):
            out = jnp.where(index == number, jnp.broadcast_to(value, tile), out)
        return out

    for p in range(pairs):
        stacked = []
        for ref in part_refs:
            for zi in range(0, region_z, per_tile):
                values = [ref[p, pl.ds(clipped(zi + i), 1), :] for i in range(per_tile)]
                stacked.append(jnp.where(keep, chosen(plane_of, values), 0.0))
        parts = bf16_dot(jnp.concatenate(stacked, axis=0).astype(jnp.bfloat16), pick)
        length = region_z * SPLIT
        lp = (parts[:length] + parts[length : 2 * length]) + parts[2 * length :]
        lp_ref2[2 * p] = lp[:, :LANES]
        lp_ref2[2 * p + 1] = lp[:, LANES:]

    m_of = iota(tile, 0) // groups
    ms = SUBLANES // groups

    def plane(zi, carry):
        zg = z_base + zi - HALO
        z_inside = (zg >= 0) & (zg < planes_all)
        for y in range(-HALO, rows + HALO):
            yg = y_base + y
            inside = z_inside & (yg >= 0) & (yg < rows_all)
            scale = jnp.where(inside, 0.5 * DAMPING, 0.0)
            for part in range(size // SUBLANES):
                values = [
                    lp_ref2[y + LEAD, pl.ds(zi * SPLIT + part * ms + i, 1), :] for i in range(ms)
                ]
                at = slice(part * SUBLANES, (part + 1) * SUBLANES)
                r_ref[zi, y + HALO, at] = scale / (shift[at] + chosen(m_of, values))
        return carry

    lax.fori_loop(0, region_z, plane, 0)


def sweep_kernel(
    own_ref, below_ref, above_ref, got_a, got_b, r_ref, inverse_ref,
    out_ref, ro_ref, w_ref, v_ref, first_ref, x_ref, y_ref, acc_ref, m_ref, a_ref, b_ref, sem_ref,
):
    depth, rows = own_ref.shape[:2]
    fields = v_ref.shape[3]
    size = ro_ref.shape[2]
    groups = size // SPLIT
    count = groups * BATCH
    copies = [
        pltpu.make_async_copy(got_a, a_ref, sem_ref.at[0]),
        pltpu.make_async_copy(got_b, b_ref, sem_ref.at[1]),
    ]
    for copy in copies:
        copy.start()
    even = lax.rem(lax.axis_index("pot"), 2) == 0

    from_lane = iota((LANES, SPLIT * LANES), 0)
    to_lane = iota((LANES, SPLIT * LANES), 1)
    spread = one_hot(from_lane % NX == SPLIT * (to_lane % STEPS) + to_lane // LANES)

    def place(tiles, own=False):
        wide = [tile.astype(jnp.float32) for tile, _, _ in tiles]
        packed = jnp.concatenate([w[size:] for w in wide], axis=0).astype(jnp.bfloat16)
        values = bf16_dot(packed, spread)
        for number, (_, z, y) in enumerate(tiles):
            zi, yi = z + HALO, y + HALO
            o = -2.0 * wide[number][:size]
            ro = r_ref[zi, yi] * o
            ro_ref[zi, yi] = ro
            if own:
                weight = o * ro
                turn = groups // 2
                while turn:
                    weight = weight + pltpu.roll(weight, size - turn, 0)
                    turn //= 2
                w_ref[z, y] = weight
            for m in range(SPLIT):
                v_ref[zi, yi, m] = values[
                    number * fields : (number + 1) * fields, m * LANES : (m + 1) * LANES
                ]

    def plane(z, carry):
        place([(own_ref[z, y], z, y) for y in range(rows)], own=True)
        return carry

    lax.fori_loop(0, depth, plane, 0)

    def side(k, carry):
        place([(below_ref[k, y], k - HALO, y) for y in range(rows)])
        place([(above_ref[k, y], k + depth, y) for y in range(rows)])
        return carry

    lax.fori_loop(0, HALO, side, 0)
    for copy in copies:
        copy.wait()
    inner, corners = halo_cells(depth)
    for d in range(1, HALO + 1):
        y_a = jnp.where(even, rows - 1 + d, -d)
        y_b = jnp.where(even, -d, rows - 1 + d)
        tiles = []
        for at, (distance, z) in enumerate(inner + corners):
            if distance == d:
                tiles += [(a_ref[at], z, y_a), (b_ref[at], z, y_b)]
        place(tiles)

    step = iota((fields, LANES), 1) % STEPS
    first_k = step == 0
    last_k = step == STEPS - 1
    buffers = (first_ref, x_ref, y_ref)

    def begin(z, carry):
        for y in range(rows):
            for m in range(SPLIT):
                weight = jnp.broadcast_to(w_ref[z, y, pl.ds(m * groups, 1), :], (fields, LANES))
                acc_ref[z, y, m] = (COEFFS[0] * weight) * v_ref[z + HALO, y + HALO, m]
        return carry

    lax.fori_loop(0, depth, begin, 0)

    def group(g, carry):
        def stage(number, z, reach, deep):
            coeff = COEFFS[SWEEPS - 1 - number]
            target = buffers[min(number, SWEEPS - 2)]
            source = buffers[number - 1]

            def of_group(ref, i, y, m):
                return jnp.broadcast_to(ref[z + i, y, pl.ds(m * groups + g, 1), :], (fields, LANES))

            def row(i, y):
                return [source[z + i, y, m] for m in range(SPLIT)]

            ys = range(HALO - reach, HALO + rows + reach)
            if number == 0:
                for i in range(deep):
                    for y in ys:
                        for m in range(SPLIT):
                            target[z + i, y, m] = of_group(ro_ref, i, y, m) * v_ref[z + i, y, m]
                return
            before = [row(i, ys[0] - 1) for i in range(deep)]
            here = [row(i, ys[0]) for i in range(deep)]
            for y in ys:
                after = [row(i, y + 1) for i in range(deep)]
                under, over = row(-1, y), row(deep, y)
                for i in range(deep):
                    lower = here[i - 1] if i else under
                    upper = here[i + 1] if i + 1 < deep else over
                    mid = here[i]
                    for m in range(SPLIT):
                        if m:
                            left = mid[m - 1]
                        else:
                            left = jnp.where(first_k, 0.0, pltpu.roll(mid[SPLIT - 1], 1, 1))
                        if m + 1 < SPLIT:
                            right = mid[m + 1]
                        else:
                            right = jnp.where(last_k, 0.0, pltpu.roll(mid[0], LANES - 1, 1))
                        near = (before[i][m] + after[i][m]) + (lower[m] + upper[m])
                        near = near + (left + right)
                        if number == SWEEPS - 1:
                            term = of_group(ro_ref, i, y, m) * near
                            acc_ref[z + i - HALO, y - HALO, m] += term
                            continue
                        base = mid[m] if number == 1 else first_ref[z + i, y, m]
                        target[z + i, y, m] = of_group(r_ref, i, y, m) * near + coeff * base
                before, here = here, after

        for number in range(SWEEPS):
            reach = HALO - number

            def inner(pair, c, number=number, reach=reach):
                stage(number, HALO + 2 * pair, reach, 2)
                return c

            for d in range(1, reach + 1):
                stage(number, HALO - d, reach - d, 1)
                stage(number, HALO + depth - 1 + d, reach - d, 1)
            lax.fori_loop(0, depth // 2, inner, 0)
        return carry

    lax.fori_loop(0, groups, group, 0)

    lane_in, x_out = iota((SPLIT * LANES, LANES), 0), iota((SPLIT * LANES, LANES), 1) % NX
    gather = one_hot(x_out == SPLIT * (lane_in % STEPS) + lane_in // LANES)
    left = lane_halves((fields, LANES))
    factor = 4.0 / count * -0.5
    planes = []
    for z in range(depth):
        parts = [
            jnp.concatenate([acc_ref[z, y, m] for y in range(rows)], axis=0) for m in range(SPLIT)
        ]
        acc = jnp.concatenate(parts, axis=1)
        upper = acc.astype(jnp.bfloat16)
        lower = (acc - upper.astype(jnp.float32)).astype(jnp.bfloat16)
        total = bf16_dot(upper, gather) + bf16_dot(lower, gather)
        tiles = []
        for y in range(rows):
            packed = own_ref[z, y].astype(jnp.float32)[size:]
            value = packed + pltpu.roll(packed, NX, 1)
            tiles.append(value + factor * total[y * fields : (y + 1) * fields])
        pieces = [jnp.where(left, tiles[y], tiles[y + 1]) for y in range(0, rows, 2)]
        planes.append(jnp.concatenate(pieces, axis=1))
    stacked = jnp.concatenate(planes, axis=0).astype(jnp.bfloat16)
    all_rows = depth * fields

    pick = one_hot(iota((all_rows, fields), 0) // depth == iota((all_rows, fields), 1))
    tile = one_hot(iota((fields, all_rows), 1) % fields == iota((fields, all_rows), 0))
    wide = bf16_dot(bf16_dot(pick, inverse_ref[...]).astype(jnp.bfloat16), tile)
    square = (all_rows, all_rows)
    same = iota(square, 0) % depth == iota(square, 1) // fields
    wide = jnp.where(same, wide, 0.0).astype(jnp.bfloat16)
    updated = bf16_dot(wide, stacked)

    m_ref[...] = jnp.zeros_like(m_ref)
    gram = jnp.zeros((fields, fields), jnp.float32)
    for z in range(depth):
        one = planes[z].astype(jnp.bfloat16)
        gram = gram + lax.dot_general(
            one, one, (((1,), (1,)), ((), ())), preferred_element_type=jnp.float32
        )
    m_ref[:, :fields] = gram
    pieces = rows * NX // LANES
    for p in range(fields):
        for t in range(pieces):
            out_ref[p, t] = updated[p * depth : (p + 1) * depth, t * LANES : (t + 1) * LANES]
        out_ref[p, pieces] = jnp.broadcast_to(m_ref[p : p + 1, :], (depth, LANES))


VMEM = pl.BlockSpec(memory_space=pltpu.VMEM)
SMEM = pl.BlockSpec(memory_space=pltpu.SMEM)
ANY = pl.BlockSpec(memory_space=pl.ANY)


def rows_plan(potentials, orbitals, energies, local_potential, inverse_factor):
    pots = lax.axis_size("pot")
    grids = lax.axis_size("grid")
    depth = potentials.shape[1]
    count, _, width = orbitals.shape
    rows = width // NX
    fields = pots
    half = count // 2
    f32, bf16 = jnp.float32, jnp.bfloat16
    shape = jax.ShapeDtypeStruct
    tile = (half + fields, LANES)

    blocks = potentials.reshape(depth, pots, width).transpose(1, 0, 2)
    by_rows = lax.all_to_all(blocks, "pot", 0, 0, tiled=True)

    inner, corners = halo_cells(depth)
    edge = len(inner) + len(corners)
    by_groups = pl.pallas_call(
        orbital_kernel,
        out_shape=shape((half * rows * depth, LANES), f32),
        in_specs=[VMEM],
        out_specs=VMEM,
        name="orbitals",
    )(orbitals)
    own, low, high, part_a, part_b = pl.pallas_call(
        pack_kernel,
        out_shape=[
            shape((depth, rows) + tile, bf16),
            shape((HALO, rows) + tile, bf16),
            shape((HALO, rows) + tile, bf16),
            shape((edge,) + tile, bf16),
            shape((edge,) + tile, bf16),
        ],
        in_specs=[VMEM] * 2,
        out_specs=[VMEM] * 5,
        name="pack",
    )(by_rows, by_groups)

    forward = [(i, i + 1) for i in range(grids - 1)]
    below = lax.ppermute(high, "grid", forward)
    above = lax.ppermute(low, "grid", [(t, s) for s, t in forward])

    to_a, to_b = pl.pallas_call(
        corner_kernel,
        out_shape=[shape((edge,) + tile, bf16)] * 2,
        in_specs=[ANY] * 4,
        out_specs=[ANY] * 2,
        scratch_shapes=[pltpu.SemaphoreType.DMA((2 * len(corners),))],
        input_output_aliases={2: 0, 3: 1},
        name="corners",
    )(below, above, part_a, part_b)
    pairs_a = [(i, i ^ 1) for i in range(pots)]
    pairs_b = [(i, i + 1 if i % 2 else i - 1) for i in range(1, pots - 1)]
    got_a = lax.ppermute(to_a, "pot", pairs_a)
    got_b = lax.ppermute(to_b, "pot", pairs_b)

    region = (depth + 2 * HALO, rows + 2 * HALO)
    inverse_diagonal = pl.pallas_call(
        diagonal_kernel,
        out_shape=shape(region + (half, LANES), f32),
        in_specs=[SMEM, VMEM],
        out_specs=VMEM,
        scratch_shapes=[pltpu.VMEM((rows + 2 * LEAD, region[0] * SPLIT, LANES), f32)]
        + [pltpu.VMEM((rows // 2 + LEAD, local_potential.shape[0], LANES), f32)] * 3,
        name="diagonal",
    )(energies, local_potential)
    pieces = width // LANES
    sent = pl.pallas_call(
        sweep_kernel,
        out_shape=shape((fields, pieces + 1, depth, LANES), f32),
        in_specs=[VMEM] * 3 + [ANY] * 2 + [VMEM] * 2,
        out_specs=VMEM,
        scratch_shapes=[
            pltpu.VMEM(region + (half, LANES), f32),
            pltpu.VMEM((depth, rows, half, LANES), f32),
            pltpu.VMEM(region + (SPLIT, fields, LANES), f32),
            pltpu.VMEM(region + (SPLIT, fields, LANES), f32),
            pltpu.VMEM(region + (SPLIT, fields, LANES), f32),
            pltpu.VMEM(region + (SPLIT, fields, LANES), f32),
            pltpu.VMEM((depth, rows, SPLIT, fields, LANES), f32),
            pltpu.VMEM((fields, LANES), f32),
            pltpu.VMEM((edge,) + tile, bf16),
            pltpu.VMEM((edge,) + tile, bf16),
            pltpu.SemaphoreType.DMA((2,)),
        ],
        name="sweeps",
    )(own, below, above, got_a, got_b, inverse_diagonal, inverse_factor)

    back = lax.all_to_all(sent, "pot", 0, 0, tiled=True)
    updated = back[:, :pieces].reshape(pots * pieces, depth, LANES).transpose(1, 0, 2)
    updated = updated.reshape(1, depth, pots * width)
    margins = jnp.sum(back[:, pieces], axis=0)
    step = 1
    while step < grids:
        margins = margins + lax.ppermute(margins, "grid", [(i, i ^ step) for i in range(grids)])
        step *= 2
    margins = margins[:1, :fields] / local_potential.size
    return updated, margins


def local(potentials, orbitals, energies, local_potential, inverse_factor):
    pots = lax.axis_size("pot")
    grids = lax.axis_size("grid")
    depth = potentials.shape[1]
    count, _, width = orbitals.shape
    fits = (
        potentials.shape[0] == 1
        and pots == 8
        and width % LANES == 0
        and LANES == 2 * NX
        and width // NX >= HALO
        and depth == 8
        and count % (BATCH * SPLIT) == 0
        and count // BATCH in (2, 4)
        and grids & (grids - 1) == 0
    )
    plan = rows_plan if fits else gathered_plan
    return plan(potentials, orbitals, energies, local_potential, inverse_factor)


def solution(mesh):
    in_specs = (P("pot", "grid", None), P(None, "grid", "pot"), P(), P(), P())
    out_specs = (P("pot", "grid", None), P("pot", None))
    return jax.shard_map(local, mesh=mesh, in_specs=in_specs, out_specs=out_specs, check_vma=False)
```

```python
import math

import jax
import jax.numpy as jnp
from jax import lax
from jax.experimental import pallas as pl
from jax.experimental.pallas import tpu as pltpu
from jax.sharding import PartitionSpec as P

NX = 64
SWEEPS = 4
DAMPING = 0.8
COEFFS = tuple(
    sum(math.comb(n, m) * (1.0 - DAMPING) ** (n - m) for n in range(m, SWEEPS))
    for m in range(SWEEPS)
)
HALO = SWEEPS - 1
LEAD = HALO + HALO % 2
LANES = 128
SUBLANES = 8


def padded_2(block, sides, width):
    for axis, dim in sides:
        count = lax.axis_size(axis)
        forward = [(i, i + 1) for i in range(count - 1)]
        backward = [(target, source) for source, target in forward]
        low = lax.ppermute(
            lax.slice_in_dim(block, block.shape[dim] - width, None, axis=dim), axis, forward
        )
        high = lax.ppermute(lax.slice_in_dim(block, 0, width, axis=dim), axis, backward)
        block = jnp.concatenate([low, block, high], axis=dim)
    return block


def plane_neighbours(field, row_width):
    plane_size = field.shape[-1]
    widths = [(0, 0)] * (field.ndim - 1)
    padded = jnp.pad(field, widths + [(row_width, row_width)])
    along_y = padded[..., 2 * row_width :] + padded[..., :plane_size]
    column = jnp.arange(plane_size, dtype=jnp.int32) % row_width
    padded = jnp.pad(field, widths + [(1, 1)])
    right_side = jnp.where(column == row_width - 1, 0.0, padded[..., 2:])
    left_side = jnp.where(column == 0, 0.0, padded[..., :plane_size])
    return along_y + right_side + left_side


def across_slabs(answer):
    padded = padded_2(answer, (("grid", 2),), 1)
    return padded[:, :, 2:] + padded[:, :, :-2]


def absorb(orbital_block, energy_block, fields, local_here, along_planes):
    orbital = orbital_block.astype(jnp.float32)[:, None]
    diagonal = (3.0 + local_here[None] - energy_block[:, None, None])[:, None]
    source = -orbital * fields[None]
    answer = DAMPING * source / diagonal
    for sweep_index in range(SWEEPS - 1):
        nearby = along_planes(answer) + plane_neighbours(answer, NX)
        answer = answer + DAMPING * (source - diagonal * answer + 0.5 * nearby) / diagonal
    return jnp.sum(orbital * answer, axis=0)


def gathered_plan(potentials, orbitals, energies, local_potential, inverse_factor):
    slab_depth = potentials.shape[1]
    count = orbitals.shape[0]
    cells = local_potential.size
    grid_index = lax.axis_index("grid")
    local_here = lax.dynamic_slice_in_dim(local_potential, grid_index * slab_depth, slab_depth, 0)
    blocks = 4 if count % 4 == 0 else 1
    block_size = count // blocks
    response = jnp.zeros(potentials.shape, jnp.float32)
    for number in range(blocks):
        orbital_block = orbitals[number * block_size : (number + 1) * block_size]
        gathered = lax.all_gather(orbital_block, "pot", axis=2, tiled=True)
        energy_block = energies[number * block_size : (number + 1) * block_size]
        response = response + absorb(gathered, energy_block, potentials, local_here, across_slabs)
    trial_block = (potentials + 4.0 / count * response).astype(jnp.bfloat16)
    by_cells = lax.all_to_all(trial_block, "pot", split_axis=2, concat_axis=0, tiled=True)
    row_count = by_cells.shape[0]
    flattened = by_cells.reshape(row_count, -1)
    partial_margins = lax.dot_general(
        flattened, flattened, (((1,), (1,)), ((), ())), preferred_element_type=jnp.float32
    )
    combined = jnp.dot(inverse_factor, flattened, preferred_element_type=jnp.float32).reshape(
        by_cells.shape
    )
    updated = lax.all_to_all(combined, "pot", split_axis=0, concat_axis=2, tiled=True)
    scattered = lax.psum_scatter(partial_margins, "pot", scatter_dimension=0, tiled=True)
    own_rows = lax.psum(scattered, "grid")
    margins = own_rows / cells
    return (updated, margins)


def halo_cells(depth):
    reach = [(d, z) for d in range(1, HALO + 1) for z in range(d - HALO, depth + HALO - d)]
    inner = [(d, z) for d, z in reach if 0 <= z < depth]
    return inner, [(d, z) for d, z in reach if not 0 <= z < depth]


def iota(shape, dim):
    return lax.broadcasted_iota(jnp.int32, shape, dim)


def bf16_dot(a, b):
    return jnp.dot(a, b, preferred_element_type=jnp.float32)


def one_hot(mask):
    return mask.astype(jnp.float32).astype(jnp.bfloat16)


def lane_halves(shape):
    return iota(shape, len(shape) - 1) < NX


SPLIT = 4
STEPS = NX // SPLIT
BATCH = LANES // STEPS


def orbital_kernel(orb_ref, s_ref):
    count, depth, width = orb_ref.shape
    groups = count // BATCH
    rows = width // NX
    lane_in, lane_out = iota((LANES, LANES), 0), iota((LANES, LANES), 1)
    wanted = (lane_out // NX) * NX + SPLIT * (lane_out % STEPS) + lane_out // STEPS % SPLIT
    permute = one_hot(lane_in == wanted)
    lane = iota((depth, LANES), 1) // STEPS
    for t in range(width // LANES):
        lanes = slice(t * LANES, (t + 1) * LANES)
        tile = orb_ref[:, :, lanes].astype(jnp.float32).reshape(count * depth, LANES)
        tile = bf16_dot(tile.astype(jnp.bfloat16), permute)
        for g in range(groups):
            first = g * BATCH * depth
            regs = [tile[first + b * depth : first + (b + 1) * depth] for b in range(BATCH)]
            step = BATCH // 2
            while step:
                stays = lane // step % 2 == 0
                for b in range(BATCH):
                    if b & step == 0:
                        lo, hi = regs[b], regs[b + step]
                        regs[b] = jnp.where(stays, lo, pltpu.roll(hi, step * STEPS, 1))
                        regs[b + step] = jnp.where(
                            stays, pltpu.roll(lo, LANES - step * STEPS, 1), hi
                        )
                step //= 2
            for c in range(BATCH):
                y, m = 2 * t + c // SPLIT, c % SPLIT
                at = ((m * groups + g) * rows + y) * depth
                s_ref[at : at + depth] = regs[c]


def pack_kernel(v_ref, s_ref, own_ref, low_ref, high_ref, a_ref, b_ref):
    fields, depth, width = v_ref.shape
    rows = width // NX
    size = s_ref.shape[0] // (rows * depth)
    even = lax.rem(lax.axis_index("pot"), 2) == 0
    pot = jnp.transpose(v_ref[...], (1, 0, 2))
    left = lane_halves((fields, LANES))
    for z in range(depth):
        for y in range(rows):
            o = s_ref[pl.ds(y * depth + z, size, stride=rows * depth), :]
            value = pot[z, :, y // 2 * LANES : (y // 2 + 1) * LANES]
            upper = value.astype(jnp.bfloat16).astype(jnp.float32)
            lower = value - upper
            if y % 2:
                v = jnp.where(left, pltpu.roll(upper, NX, 1), lower)
            else:
                v = jnp.where(left, upper, pltpu.roll(lower, NX, 1))
            tile = jnp.concatenate([o, v], axis=0).astype(jnp.bfloat16)
            own_ref[z, y] = tile
            if z < HALO:
                low_ref[z, y] = tile
            if z >= depth - HALO:
                high_ref[z - (depth - HALO), y] = tile
    for at, (d, z) in enumerate(halo_cells(depth)[0]):
        a_ref[at] = own_ref[z, jnp.where(even, rows - d, d - 1)]
        b_ref[at] = own_ref[z, jnp.where(even, d - 1, rows - d)]


def corner_kernel(below_ref, above_ref, a_in, b_in, a_ref, b_ref):
    rows = below_ref.shape[1]
    depth = rows_depth(a_ref)
    even = lax.rem(lax.axis_index("pot"), 2) == 0
    inner, corners = halo_cells(depth)
    for at, (d, z) in enumerate(corners, len(inner)):
        source, plane = (below_ref, z + HALO) if z < 0 else (above_ref, z - depth)
        a_ref[at] = source[plane, jnp.where(even, rows - d, d - 1)]
        b_ref[at] = source[plane, jnp.where(even, d - 1, rows - d)]


def rows_depth(edge_ref):
    total = sum(2 * (HALO - d) for d in range(1, HALO + 1))
    return (edge_ref.shape[0] - total) // HALO


def diagonal_kernel(energy_ref, lp_ref, r_ref, lp_ref2, *part_refs):
    planes_all, plane_cells = lp_ref.shape
    rows_all = plane_cells // NX
    region_z, region_y, size, _ = r_ref.shape
    depth, rows = region_z - 2 * HALO, region_y - 2 * HALO
    groups = size // SPLIT
    z_base = lax.axis_index("grid") * depth
    y_base = lax.axis_index("pot") * rows

    shift = jnp.zeros((size, LANES), jnp.float32)
    group_of = iota((size, LANES), 0) % groups
    member = iota((size, LANES), 1) // STEPS
    for g in range(groups):
        for b in range(BATCH):
            here = (group_of == g) & (member == b)
            shift = jnp.where(here, 3.0 - energy_ref[g * BATCH + b], shift)

    pairs = part_refs[0].shape[0]
    for p in range(pairs):
        at = jnp.clip((y_base - LEAD) // 2 + p, 0, rows_all // 2 - 1) * LANES
        rest = lp_ref[:, pl.ds(pl.multiple_of(at, LANES), LANES)]
        for part_ref in part_refs:
            part = rest.astype(jnp.bfloat16).astype(jnp.float32)
            part_ref[p] = part
            rest = rest - part
    from_lane, to_lane = iota((LANES, 2 * LANES), 0), iota((LANES, 2 * LANES), 1)
    pick = one_hot(
        (from_lane // NX == to_lane // LANES) & (from_lane % NX // SPLIT == to_lane % STEPS)
    )
    tile = (SUBLANES, LANES)
    keep = iota(tile, 1) % SPLIT == iota(tile, 0) % SPLIT
    per_tile = SUBLANES // SPLIT
    plane_of = iota(tile, 0) // SPLIT

    def clipped(zi):
        return jnp.clip(z_base + zi - HALO, 0, planes_all - 1)

    def chosen(index, values):
        out = jnp.broadcast_to(values[0], tile)
        for number, value in enumerate(values[1:], 1):
            out = jnp.where(index == number, jnp.broadcast_to(value, tile), out)
        return out

    for p in range(pairs):
        stacked = []
        for ref in part_refs:
            for zi in range(0, region_z, per_tile):
                values = [ref[p, pl.ds(clipped(zi + i), 1), :] for i in range(per_tile)]
                stacked.append(jnp.where(keep, chosen(plane_of, values), 0.0))
        parts = bf16_dot(jnp.concatenate(stacked, axis=0).astype(jnp.bfloat16), pick)
        length = region_z * SPLIT
        lp = (parts[:length] + parts[length : 2 * length]) + parts[2 * length :]
        lp_ref2[2 * p] = lp[:, :LANES]
        lp_ref2[2 * p + 1] = lp[:, LANES:]

    m_of = iota(tile, 0) // groups
    ms = SUBLANES // groups

    def plane(zi, carry):
        zg = z_base + zi - HALO
        z_inside = (zg >= 0) & (zg < planes_all)
        for y in range(-HALO, rows + HALO):
            yg = y_base + y
            inside = z_inside & (yg >= 0) & (yg < rows_all)
            scale = jnp.where(inside, 0.5 * DAMPING, 0.0)
            for part in range(size // SUBLANES):
                values = [
                    lp_ref2[y + LEAD, pl.ds(zi * SPLIT + part * ms + i, 1), :] for i in range(ms)
                ]
                at = slice(part * SUBLANES, (part + 1) * SUBLANES)
                r_ref[zi, y + HALO, at] = scale / (shift[at] + chosen(m_of, values))
        return carry

    lax.fori_loop(0, region_z, plane, 0)


def sweep_kernel(
    own_ref, below_ref, above_ref, a_ref, b_ref, r_ref, inverse_ref,
    out_ref, ro_ref, w_ref, v_ref, first_ref, x_ref, y_ref, acc_ref, m_ref,
):
    depth, rows = own_ref.shape[:2]
    fields = v_ref.shape[3]
    size = ro_ref.shape[2]
    groups = size // SPLIT
    count = groups * BATCH
    even = lax.rem(lax.axis_index("pot"), 2) == 0

    from_lane = iota((LANES, SPLIT * LANES), 0)
    to_lane = iota((LANES, SPLIT * LANES), 1)
    spread = one_hot(from_lane % NX == SPLIT * (to_lane % STEPS) + to_lane // LANES)

    def place(tiles, own=False):
        wide = [tile.astype(jnp.float32) for tile, _, _ in tiles]
        packed = jnp.concatenate([w[size:] for w in wide], axis=0).astype(jnp.bfloat16)
        values = bf16_dot(packed, spread)
        for number, (_, z, y) in enumerate(tiles):
            zi, yi = z + HALO, y + HALO
            o = -2.0 * wide[number][:size]
            ro = r_ref[zi, yi] * o
            ro_ref[zi, yi] = ro
            if own:
                weight = o * ro
                turn = groups // 2
                while turn:
                    weight = weight + pltpu.roll(weight, size - turn, 0)
                    turn //= 2
                w_ref[z, y] = weight
            for m in range(SPLIT):
                v_ref[zi, yi, m] = values[
                    number * fields : (number + 1) * fields, m * LANES : (m + 1) * LANES
                ]

    def plane(z, carry):
        place([(own_ref[z, y], z, y) for y in range(rows)], own=True)
        return carry

    lax.fori_loop(0, depth, plane, 0)

    def side(k, carry):
        place([(below_ref[k, y], k - HALO, y) for y in range(rows)])
        place([(above_ref[k, y], k + depth, y) for y in range(rows)])
        return carry

    lax.fori_loop(0, HALO, side, 0)
    inner, corners = halo_cells(depth)
    for d in range(1, HALO + 1):
        y_a = jnp.where(even, rows - 1 + d, -d)
        y_b = jnp.where(even, -d, rows - 1 + d)
        tiles = []
        for at, (distance, z) in enumerate(inner + corners):
            if distance == d:
                tiles += [(a_ref[at], z, y_a), (b_ref[at], z, y_b)]
        place(tiles)

    step = iota((fields, LANES), 1) % STEPS
    first_k = step == 0
    last_k = step == STEPS - 1
    buffers = (first_ref, x_ref, y_ref)

    def begin(z, carry):
        for y in range(rows):
            for m in range(SPLIT):
                weight = jnp.broadcast_to(w_ref[z, y, pl.ds(m * groups, 1), :], (fields, LANES))
                acc_ref[z, y, m] = (COEFFS[0] * weight) * v_ref[z + HALO, y + HALO, m]
        return carry

    lax.fori_loop(0, depth, begin, 0)

    def group(g, carry):
        def stage(number, z, reach, deep):
            coeff = COEFFS[SWEEPS - 1 - number]
            target = buffers[min(number, SWEEPS - 2)]
            source = buffers[number - 1]

            def of_group(ref, i, y, m):
                return jnp.broadcast_to(ref[z + i, y, pl.ds(m * groups + g, 1), :], (fields, LANES))

            def row(i, y):
                return [source[z + i, y, m] for m in range(SPLIT)]

            ys = range(HALO - reach, HALO + rows + reach)
            if number == 0:
                for i in range(deep):
                    for y in ys:
                        for m in range(SPLIT):
                            target[z + i, y, m] = of_group(ro_ref, i, y, m) * v_ref[z + i, y, m]
                return
            before = [row(i, ys[0] - 1) for i in range(deep)]
            here = [row(i, ys[0]) for i in range(deep)]
            for y in ys:
                after = [row(i, y + 1) for i in range(deep)]
                under, over = row(-1, y), row(deep, y)
                for i in range(deep):
                    lower = here[i - 1] if i else under
                    upper = here[i + 1] if i + 1 < deep else over
                    mid = here[i]
                    for m in range(SPLIT):
                        if m:
                            left = mid[m - 1]
                        else:
                            left = jnp.where(first_k, 0.0, pltpu.roll(mid[SPLIT - 1], 1, 1))
                        if m + 1 < SPLIT:
                            right = mid[m + 1]
                        else:
                            right = jnp.where(last_k, 0.0, pltpu.roll(mid[0], LANES - 1, 1))
                        near = (before[i][m] + after[i][m]) + (lower[m] + upper[m])
                        near = near + (left + right)
                        if number == SWEEPS - 1:
                            term = of_group(ro_ref, i, y, m) * near
                            acc_ref[z + i - HALO, y - HALO, m] += term
                            continue
                        base = mid[m] if number == 1 else first_ref[z + i, y, m]
                        target[z + i, y, m] = of_group(r_ref, i, y, m) * near + coeff * base
                before, here = here, after

        for number in range(SWEEPS):
            reach = HALO - number

            def inner(pair, c, number=number, reach=reach):
                stage(number, HALO + 2 * pair, reach, 2)
                return c

            for d in range(1, reach + 1):
                stage(number, HALO - d, reach - d, 1)
                stage(number, HALO + depth - 1 + d, reach - d, 1)
            lax.fori_loop(0, depth // 2, inner, 0)
        return carry

    lax.fori_loop(0, groups, group, 0)

    lane_in, x_out = iota((SPLIT * LANES, LANES), 0), iota((SPLIT * LANES, LANES), 1) % NX
    gather = one_hot(x_out == SPLIT * (lane_in % STEPS) + lane_in // LANES)
    left = lane_halves((fields, LANES))
    factor = 4.0 / count * -0.5
    planes = []
    for z in range(depth):
        parts = [
            jnp.concatenate([acc_ref[z, y, m] for y in range(rows)], axis=0) for m in range(SPLIT)
        ]
        acc = jnp.concatenate(parts, axis=1)
        upper = acc.astype(jnp.bfloat16)
        lower = (acc - upper.astype(jnp.float32)).astype(jnp.bfloat16)
        total = bf16_dot(upper, gather) + bf16_dot(lower, gather)
        tiles = []
        for y in range(rows):
            packed = own_ref[z, y].astype(jnp.float32)[size:]
            value = packed + pltpu.roll(packed, NX, 1)
            tiles.append(value + factor * total[y * fields : (y + 1) * fields])
        pieces = [jnp.where(left, tiles[y], tiles[y + 1]) for y in range(0, rows, 2)]
        planes.append(jnp.concatenate(pieces, axis=1))
    stacked = jnp.concatenate(planes, axis=0).astype(jnp.bfloat16)
    all_rows = depth * fields

    pick = one_hot(iota((all_rows, fields), 0) // depth == iota((all_rows, fields), 1))
    tile = one_hot(iota((fields, all_rows), 1) % fields == iota((fields, all_rows), 0))
    wide = bf16_dot(bf16_dot(pick, inverse_ref[...]).astype(jnp.bfloat16), tile)
    square = (all_rows, all_rows)
    same = iota(square, 0) % depth == iota(square, 1) // fields
    wide = jnp.where(same, wide, 0.0).astype(jnp.bfloat16)
    updated = bf16_dot(wide, stacked)

    m_ref[...] = jnp.zeros_like(m_ref)
    gram = jnp.zeros((fields, fields), jnp.float32)
    for z in range(depth):
        one = planes[z].astype(jnp.bfloat16)
        gram = gram + lax.dot_general(
            one, one, (((1,), (1,)), ((), ())), preferred_element_type=jnp.float32
        )
    m_ref[:, :fields] = gram
    pieces = rows * NX // LANES
    for p in range(fields):
        for t in range(pieces):
            out_ref[p, t] = updated[p * depth : (p + 1) * depth, t * LANES : (t + 1) * LANES]
        out_ref[p, pieces] = jnp.broadcast_to(m_ref[p : p + 1, :], (depth, LANES))


VMEM = pl.BlockSpec(memory_space=pltpu.VMEM)
SMEM = pl.BlockSpec(memory_space=pltpu.SMEM)


def in_vmem(*arrays):
    return [pltpu.with_memory_space_constraint(array, pltpu.VMEM) for array in arrays]


def rows_plan(potentials, orbitals, energies, local_potential, inverse_factor):
    pots = lax.axis_size("pot")
    grids = lax.axis_size("grid")
    depth = potentials.shape[1]
    count, _, width = orbitals.shape
    rows = width // NX
    fields = pots
    half = count // 2
    f32, bf16 = jnp.float32, jnp.bfloat16
    shape = pltpu.VMEM
    tile = (half + fields, LANES)

    blocks = potentials.reshape(depth, pots, width).transpose(1, 0, 2)
    by_rows = lax.all_to_all(blocks, "pot", 0, 0, tiled=True)

    inner, corners = halo_cells(depth)
    edge = len(inner) + len(corners)
    by_groups = pl.pallas_call(
        orbital_kernel,
        out_shape=shape((half * rows * depth, LANES), f32),
        in_specs=[VMEM],
        out_specs=VMEM,
        name="orbitals",
    )(orbitals)
    own, low, high, part_a, part_b = pl.pallas_call(
        pack_kernel,
        out_shape=[
            shape((depth, rows) + tile, bf16),
            shape((HALO, rows) + tile, bf16),
            shape((HALO, rows) + tile, bf16),
            shape((edge,) + tile, bf16),
            shape((edge,) + tile, bf16),
        ],
        in_specs=[VMEM] * 2,
        out_specs=[VMEM] * 5,
        name="pack",
    )(*in_vmem(by_rows, by_groups))

    forward = [(i, i + 1) for i in range(grids - 1)]
    below = lax.ppermute(high, "grid", forward)
    above = lax.ppermute(low, "grid", [(t, s) for s, t in forward])

    to_a, to_b = pl.pallas_call(
        corner_kernel,
        out_shape=[shape((edge,) + tile, bf16)] * 2,
        in_specs=[VMEM] * 4,
        out_specs=[VMEM] * 2,
        input_output_aliases={2: 0, 3: 1},
        name="corners",
    )(*in_vmem(below, above, part_a, part_b))
    pairs_a = [(i, i ^ 1) for i in range(pots)]
    pairs_b = [(i, i + 1 if i % 2 else i - 1) for i in range(1, pots - 1)]
    got_a = lax.ppermute(to_a, "pot", pairs_a)
    got_b = lax.ppermute(to_b, "pot", pairs_b)

    region = (depth + 2 * HALO, rows + 2 * HALO)
    inverse_diagonal = pl.pallas_call(
        diagonal_kernel,
        out_shape=shape(region + (half, LANES), f32),
        in_specs=[SMEM, VMEM],
        out_specs=VMEM,
        scratch_shapes=[pltpu.VMEM((rows + 2 * LEAD, region[0] * SPLIT, LANES), f32)]
        + [pltpu.VMEM((rows // 2 + LEAD, local_potential.shape[0], LANES), f32)] * 3,
        name="diagonal",
    )(energies, local_potential)
    pieces = width // LANES
    sent = pl.pallas_call(
        sweep_kernel,
        out_shape=shape((fields, pieces + 1, depth, LANES), f32),
        in_specs=[VMEM] * 7,
        out_specs=VMEM,
        scratch_shapes=[
            pltpu.VMEM(region + (half, LANES), f32),
            pltpu.VMEM((depth, rows, half, LANES), f32),
            pltpu.VMEM(region + (SPLIT, fields, LANES), f32),
            pltpu.VMEM(region + (SPLIT, fields, LANES), f32),
            pltpu.VMEM(region + (SPLIT, fields, LANES), f32),
            pltpu.VMEM(region + (SPLIT, fields, LANES), f32),
            pltpu.VMEM((depth, rows, SPLIT, fields, LANES), f32),
            pltpu.VMEM((fields, LANES), f32),
        ],
        name="sweeps",
    )(*in_vmem(own, below, above, got_a, got_b, inverse_diagonal), inverse_factor)

    back = lax.all_to_all(sent, "pot", 0, 0, tiled=True)
    updated = back[:, :pieces].reshape(pots * pieces, depth, LANES).transpose(1, 0, 2)
    updated = updated.reshape(1, depth, pots * width)
    margins = jnp.sum(back[:, pieces], axis=0)
    step = 1
    while step < grids:
        margins = margins + lax.ppermute(margins, "grid", [(i, i ^ step) for i in range(grids)])
        step *= 2
    margins = margins[:1, :fields] / local_potential.size
    return updated, margins


def local(potentials, orbitals, energies, local_potential, inverse_factor):
    pots = lax.axis_size("pot")
    grids = lax.axis_size("grid")
    depth = potentials.shape[1]
    count, _, width = orbitals.shape
    fits = (
        potentials.shape[0] == 1
        and pots == 8
        and width % LANES == 0
        and LANES == 2 * NX
        and width // NX >= HALO
        and depth == 8
        and count % (BATCH * SPLIT) == 0
        and count // BATCH in (2, 4)
        and grids & (grids - 1) == 0
    )
    plan = rows_plan if fits else gathered_plan
    return plan(potentials, orbitals, energies, local_potential, inverse_factor)


def solution(mesh):
    in_specs = (P("pot", "grid", None), P(None, "grid", "pot"), P(), P(), P())
    out_specs = (P("pot", "grid", None), P("pot", None))
    return jax.shard_map(local, mesh=mesh, in_specs=in_specs, out_specs=out_specs, check_vma=False)
```

```python
import functools
import math

import jax
import jax.numpy as jnp
from jax import lax
from jax.experimental import pallas as pl
from jax.experimental.pallas import tpu as pltpu
from jax.sharding import PartitionSpec as P

NX = 64
SWEEPS = 4
DAMPING = 0.8
COEFFS = tuple(
    sum(math.comb(n, m) * (1.0 - DAMPING) ** (n - m) for n in range(m, SWEEPS))
    for m in range(SWEEPS)
)
HALO = SWEEPS - 1
LEAD = HALO + HALO % 2
LANES = 128
SUBLANES = 8
VMEM_LIMIT = 24 << 20


def padded_2(block, sides, width):
    for axis, dim in sides:
        count = lax.axis_size(axis)
        forward = [(i, i + 1) for i in range(count - 1)]
        backward = [(target, source) for source, target in forward]
        low = lax.ppermute(
            lax.slice_in_dim(block, block.shape[dim] - width, None, axis=dim), axis, forward
        )
        high = lax.ppermute(lax.slice_in_dim(block, 0, width, axis=dim), axis, backward)
        block = jnp.concatenate([low, block, high], axis=dim)
    return block


def plane_neighbours(field, row_width):
    plane_size = field.shape[-1]
    widths = [(0, 0)] * (field.ndim - 1)
    padded = jnp.pad(field, widths + [(row_width, row_width)])
    along_y = padded[..., 2 * row_width :] + padded[..., :plane_size]
    column = jnp.arange(plane_size, dtype=jnp.int32) % row_width
    padded = jnp.pad(field, widths + [(1, 1)])
    right_side = jnp.where(column == row_width - 1, 0.0, padded[..., 2:])
    left_side = jnp.where(column == 0, 0.0, padded[..., :plane_size])
    return along_y + right_side + left_side


def across_slabs(answer):
    padded = padded_2(answer, (("grid", 2),), 1)
    return padded[:, :, 2:] + padded[:, :, :-2]


def absorb(orbital_block, energy_block, fields, local_here, along_planes):
    orbital = orbital_block.astype(jnp.float32)[:, None]
    diagonal = (3.0 + local_here[None] - energy_block[:, None, None])[:, None]
    source = -orbital * fields[None]
    answer = DAMPING * source / diagonal
    for sweep_index in range(SWEEPS - 1):
        nearby = along_planes(answer) + plane_neighbours(answer, NX)
        answer = answer + DAMPING * (source - diagonal * answer + 0.5 * nearby) / diagonal
    return jnp.sum(orbital * answer, axis=0)


def gathered_plan(potentials, orbitals, energies, local_potential, inverse_factor):
    slab_depth = potentials.shape[1]
    count = orbitals.shape[0]
    cells = local_potential.size
    grid_index = lax.axis_index("grid")
    local_here = lax.dynamic_slice_in_dim(local_potential, grid_index * slab_depth, slab_depth, 0)
    blocks = 4 if count % 4 == 0 else 1
    block_size = count // blocks
    response = jnp.zeros(potentials.shape, jnp.float32)
    for number in range(blocks):
        orbital_block = orbitals[number * block_size : (number + 1) * block_size]
        gathered = lax.all_gather(orbital_block, "pot", axis=2, tiled=True)
        energy_block = energies[number * block_size : (number + 1) * block_size]
        response = response + absorb(gathered, energy_block, potentials, local_here, across_slabs)
    trial_block = (potentials + 4.0 / count * response).astype(jnp.bfloat16)
    by_cells = lax.all_to_all(trial_block, "pot", split_axis=2, concat_axis=0, tiled=True)
    row_count = by_cells.shape[0]
    flattened = by_cells.reshape(row_count, -1)
    partial_margins = lax.dot_general(
        flattened, flattened, (((1,), (1,)), ((), ())), preferred_element_type=jnp.float32
    )
    combined = jnp.dot(inverse_factor, flattened, preferred_element_type=jnp.float32).reshape(
        by_cells.shape
    )
    updated = lax.all_to_all(combined, "pot", split_axis=0, concat_axis=2, tiled=True)
    scattered = lax.psum_scatter(partial_margins, "pot", scatter_dimension=0, tiled=True)
    own_rows = lax.psum(scattered, "grid")
    margins = own_rows / cells
    return (updated, margins)


def row_cells(depth):
    return [(d, z) for d in range(1, HALO + 1) for z in range(depth)]


def plane_cells(rows):
    return [(d, y) for d in range(1, HALO + 1) for y in range(d - HALO, rows + HALO - d)]


def iota(shape, dim):
    return lax.broadcasted_iota(jnp.int32, shape, dim)


def bf16_dot(a, b):
    return jnp.dot(a, b, preferred_element_type=jnp.float32)


def one_hot(mask):
    return mask.astype(jnp.float32).astype(jnp.bfloat16)


def lane_halves(shape):
    return iota(shape, len(shape) - 1) < NX


SPLIT = 4
STEPS = NX // SPLIT
BATCH = LANES // STEPS


def orbital_kernel(orb_ref, own_ref, a_ref, b_ref, s_ref):
    count, depth, width = orb_ref.shape
    groups = count // BATCH
    rows = width // NX
    lane_in, lane_out = iota((LANES, LANES), 0), iota((LANES, LANES), 1)
    wanted = (lane_out // NX) * NX + SPLIT * (lane_out % STEPS) + lane_out // STEPS % SPLIT
    permute = one_hot(lane_in == wanted)
    lane = iota((depth, LANES), 1) // STEPS
    for t in range(width // LANES):
        lanes = slice(t * LANES, (t + 1) * LANES)
        tile = orb_ref[:, :, lanes].astype(jnp.float32).reshape(count * depth, LANES)
        tile = bf16_dot(tile.astype(jnp.bfloat16), permute)
        for g in range(groups):
            first = g * BATCH * depth
            regs = [tile[first + b * depth : first + (b + 1) * depth] for b in range(BATCH)]
            step = BATCH // 2
            while step:
                stays = lane // step % 2 == 0
                for b in range(BATCH):
                    if b & step == 0:
                        lo, hi = regs[b], regs[b + step]
                        regs[b] = jnp.where(stays, lo, pltpu.roll(hi, step * STEPS, 1))
                        regs[b + step] = jnp.where(
                            stays, pltpu.roll(lo, LANES - step * STEPS, 1), hi
                        )
                step //= 2
            for c in range(BATCH):
                y, m = 2 * t + c // SPLIT, c % SPLIT
                at = ((m * groups + g) * rows + y) * depth
                s_ref[at : at + depth] = regs[c]
    for z in range(depth):
        for y in range(rows):
            tile = s_ref[pl.ds(y * depth + z, SPLIT * groups, stride=rows * depth), :]
            own_ref[z, y] = tile.astype(jnp.bfloat16)
    even = lax.rem(lax.axis_index("pot"), 2) == 0
    for at, (d, z) in enumerate(row_cells(depth)):
        a_ref[at] = own_ref[z, jnp.where(even, rows - d, d - 1)]
        b_ref[at] = own_ref[z, jnp.where(even, d - 1, rows - d)]


def window_kernel(v_ref, out_ref):
    receivers, pieces = out_ref.shape[:2]
    total = v_ref.shape[2] // LANES
    stride = total // receivers
    ahead = LEAD * NX // LANES
    for p in range(receivers):
        for t in range(pieces):
            at = p * stride + t - ahead
            if 0 <= at < total:
                out_ref[p, t] = v_ref[0, :, at * LANES : (at + 1) * LANES]
            else:
                out_ref[p, t] = jnp.zeros(out_ref.shape[2:], out_ref.dtype)


def two_parts(value, y):
    left = lane_halves(value.shape)
    upper = value.astype(jnp.bfloat16).astype(jnp.float32)
    lower = value - upper
    if y % 2:
        return jnp.where(left, pltpu.roll(upper, NX, 1), lower)
    return jnp.where(left, upper, pltpu.roll(lower, NX, 1))


def row_tile(own_ref, a_ref, b_ref, z, y):
    depth, rows = own_ref.shape[:2]
    even = lax.rem(lax.axis_index("pot"), 2) == 0
    if 0 <= y < rows:
        return own_ref[z, y]
    at = (-y - 1 if y < 0 else y - rows) * depth + z
    a, b = a_ref[at].astype(jnp.float32), b_ref[at].astype(jnp.float32)
    return jnp.where(even == (y < 0), b, a).astype(jnp.bfloat16)


def send_kernel(v_ref, own_ref, a_ref, b_ref, to_a_ref, to_b_ref):
    depth, rows = own_ref.shape[:2]
    pieces = rows * NX // LANES + 2 * (LEAD * NX // LANES)
    fields = v_ref.shape[0] // (pieces * depth)
    even = lax.rem(lax.axis_index("grid"), 2) == 0

    def tile_of(z, y):
        start = (y + LEAD) // 2 * depth + z
        value = v_ref[pl.ds(start, fields, stride=pieces * depth), :]
        orbitals = row_tile(own_ref, a_ref, b_ref, z, y).astype(jnp.float32)
        return jnp.concatenate([orbitals, two_parts(value, y)], axis=0)

    for at, (d, y) in enumerate(plane_cells(rows)):
        top, bottom = tile_of(depth - d, y), tile_of(d - 1, y)
        to_a_ref[at] = jnp.where(even, top, bottom).astype(jnp.bfloat16)
        to_b_ref[at] = jnp.where(even, bottom, top).astype(jnp.bfloat16)


def diagonal_kernel(energy_ref, lp_ref, r_ref, lp_ref2, *part_refs):
    planes_all, plane_cells = lp_ref.shape
    rows_all = plane_cells // NX
    region_z, region_y, size, _ = r_ref.shape
    depth, rows = region_z - 2 * HALO, region_y - 2 * HALO
    groups = size // SPLIT
    z_base = lax.axis_index("grid") * depth
    y_base = lax.axis_index("pot") * rows

    shift = jnp.zeros((size, LANES), jnp.float32)
    group_of = iota((size, LANES), 0) % groups
    member = iota((size, LANES), 1) // STEPS
    for g in range(groups):
        for b in range(BATCH):
            here = (group_of == g) & (member == b)
            shift = jnp.where(here, 3.0 - energy_ref[g * BATCH + b], shift)

    pairs = part_refs[0].shape[0]
    for p in range(pairs):
        at = jnp.clip((y_base - LEAD) // 2 + p, 0, rows_all // 2 - 1) * LANES
        rest = lp_ref[:, pl.ds(pl.multiple_of(at, LANES), LANES)]
        for part_ref in part_refs:
            part = rest.astype(jnp.bfloat16).astype(jnp.float32)
            part_ref[p] = part
            rest = rest - part
    from_lane, to_lane = iota((LANES, 2 * LANES), 0), iota((LANES, 2 * LANES), 1)
    pick = one_hot(
        (from_lane // NX == to_lane // LANES) & (from_lane % NX // SPLIT == to_lane % STEPS)
    )
    tile = (SUBLANES, LANES)
    keep = iota(tile, 1) % SPLIT == iota(tile, 0) % SPLIT
    per_tile = SUBLANES // SPLIT
    plane_of = iota(tile, 0) // SPLIT

    def clipped(zi):
        return jnp.clip(z_base + zi - HALO, 0, planes_all - 1)

    def chosen(index, values):
        out = jnp.broadcast_to(values[0], tile)
        for number, value in enumerate(values[1:], 1):
            out = jnp.where(index == number, jnp.broadcast_to(value, tile), out)
        return out

    for p in range(pairs):
        stacked = []
        for ref in part_refs:
            for zi in range(0, region_z, per_tile):
                values = [ref[p, pl.ds(clipped(zi + i), 1), :] for i in range(per_tile)]
                stacked.append(jnp.where(keep, chosen(plane_of, values), 0.0))
        parts = bf16_dot(jnp.concatenate(stacked, axis=0).astype(jnp.bfloat16), pick)
        length = region_z * SPLIT
        lp = (parts[:length] + parts[length : 2 * length]) + parts[2 * length :]
        lp_ref2[2 * p] = lp[:, :LANES]
        lp_ref2[2 * p + 1] = lp[:, LANES:]

    m_of = iota(tile, 0) // groups
    ms = SUBLANES // groups

    def plane(zi, carry):
        zg = z_base + zi - HALO
        z_inside = (zg >= 0) & (zg < planes_all)
        for y in range(-HALO, rows + HALO):
            yg = y_base + y
            inside = z_inside & (yg >= 0) & (yg < rows_all)
            scale = jnp.where(inside, 0.5 * DAMPING, 0.0)
            for part in range(size // SUBLANES):
                values = [
                    lp_ref2[y + LEAD, pl.ds(zi * SPLIT + part * ms + i, 1), :] for i in range(ms)
                ]
                at = slice(part * SUBLANES, (part + 1) * SUBLANES)
                r_ref[zi, y + HALO, at] = scale / (shift[at] + chosen(m_of, values))
        return carry

    lax.fori_loop(0, region_z, plane, 0)


def spread_matrix():
    from_lane = iota((LANES, SPLIT * LANES), 0)
    to_lane = iota((LANES, SPLIT * LANES), 1)
    return one_hot(from_lane % NX == SPLIT * (to_lane % STEPS) + to_lane // LANES)


def place(cells, r_ref, ro_ref, v_ref, then=None):
    fields = v_ref.shape[3]
    packed = jnp.concatenate([parts for _, parts, _, _ in cells], axis=0).astype(jnp.bfloat16)
    values = bf16_dot(packed, spread_matrix())
    for number, (orbitals, _, z, y) in enumerate(cells):
        zi, yi = z + HALO, y + HALO
        o = -2.0 * orbitals.astype(jnp.float32)
        ro = r_ref[zi, yi] * o
        ro_ref[zi, yi] = ro
        own = [
            values[number * fields : (number + 1) * fields, m * LANES : (m + 1) * LANES]
            for m in range(SPLIT)
        ]
        for m in range(SPLIT):
            v_ref[zi, yi, m] = own[m]
        if then is not None:
            then(z, y, o * ro, own)


def prepare_kernel(
    parts_ref, own_ref, a_ref, b_ref, r_ref, ro_ref, v_ref, acc_ref, w_ref
):
    depth, rows = own_ref.shape[:2]
    fields = v_ref.shape[3]
    size = ro_ref.shape[2]
    groups = size // SPLIT
    pieces = parts_ref.shape[0] // (depth * fields)

    def first_term(z, y, weight, values):
        if not 0 <= y < rows:
            return
        turn = groups // 2
        while turn:
            weight = weight + pltpu.roll(weight, size - turn, 0)
            turn //= 2
        w_ref[y] = COEFFS[0] * weight
        for m in range(SPLIT):
            at = m * groups
            w = jnp.broadcast_to(w_ref[y, at : at + 1], (fields, LANES))
            acc_ref[z, y, m] = w * values[m]

    def plane(z, carry):
        cells = []
        for y in range(-HALO, rows + HALO):
            start = (y + LEAD) // 2 * depth + z
            value = parts_ref[pl.ds(start, fields, stride=pieces * depth), :]
            cells.append((row_tile(own_ref, a_ref, b_ref, z, y), two_parts(value, y), z, y))
        place(cells, r_ref, ro_ref, v_ref, first_term)
        return carry

    lax.fori_loop(0, depth, plane, 0)


def sweep_kernel(
    parts_ref, a_ref, b_ref, r_ref, inverse_ref, ro_in, v_in, acc_in,
    out_ref, ro_ref, v_ref, acc_ref, first_ref, x_ref, y_ref, m_ref,
):
    depth, rows = acc_ref.shape[:2]
    fields = v_ref.shape[3]
    size = ro_ref.shape[2]
    groups = size // SPLIT
    count = groups * BATCH
    even = lax.rem(lax.axis_index("grid"), 2) == 0
    all_cells = list(enumerate(plane_cells(rows)))
    for d in range(1, HALO + 1):
        z_a = jnp.where(even, depth - 1 + d, -d)
        z_b = jnp.where(even, -d, depth - 1 + d)
        cells = []
        for at, (distance, y) in all_cells:
            if distance == d:
                for ref, z in ((a_ref, z_a), (b_ref, z_b)):
                    tile = ref[at].astype(jnp.float32)
                    cells.append((tile[:size], tile[size:], z, y))
        place(cells, r_ref, ro_ref, v_ref)

    step = iota((fields, LANES), 1) % STEPS
    first_k = step == 0
    last_k = step == STEPS - 1
    buffers = (first_ref, x_ref, y_ref)

    def group(g, carry):
        def stage(number, z, reach, deep):
            coeff = COEFFS[SWEEPS - 1 - number]
            target = buffers[min(number, SWEEPS - 2)]
            source = buffers[number - 1]

            def of_group(ref, i, y, m):
                return jnp.broadcast_to(ref[z + i, y, pl.ds(m * groups + g, 1), :], (fields, LANES))

            def row(i, y):
                return [source[z + i, y, m] for m in range(SPLIT)]

            ys = range(HALO - reach, HALO + rows + reach)
            if number == 0:
                for i in range(deep):
                    for y in ys:
                        for m in range(SPLIT):
                            target[z + i, y, m] = of_group(ro_ref, i, y, m) * v_ref[z + i, y, m]
                return
            before = [row(i, ys[0] - 1) for i in range(deep)]
            here = [row(i, ys[0]) for i in range(deep)]
            for y in ys:
                after = [row(i, y + 1) for i in range(deep)]
                under, over = row(-1, y), row(deep, y)
                for i in range(deep):
                    lower = here[i - 1] if i else under
                    upper = here[i + 1] if i + 1 < deep else over
                    mid = here[i]
                    for m in range(SPLIT):
                        if m:
                            left = mid[m - 1]
                        else:
                            left = jnp.where(first_k, 0.0, pltpu.roll(mid[SPLIT - 1], 1, 1))
                        if m + 1 < SPLIT:
                            right = mid[m + 1]
                        else:
                            right = jnp.where(last_k, 0.0, pltpu.roll(mid[0], LANES - 1, 1))
                        near = (before[i][m] + after[i][m]) + (lower[m] + upper[m])
                        near = near + (left + right)
                        if number == SWEEPS - 1:
                            term = of_group(ro_ref, i, y, m) * near
                            acc_ref[z + i - HALO, y - HALO, m] += term
                            continue
                        base = mid[m] if number == 1 else first_ref[z + i, y, m]
                        target[z + i, y, m] = of_group(r_ref, i, y, m) * near + coeff * base
                before, here = here, after

        for number in range(SWEEPS):
            reach = HALO - number

            def inner(pair, c, number=number, reach=reach):
                stage(number, HALO + 2 * pair, reach, 2)
                return c

            for d in range(1, reach + 1):
                stage(number, HALO - d, reach - d, 1)
                stage(number, HALO + depth - 1 + d, reach - d, 1)
            lax.fori_loop(0, depth // 2, inner, 0)
        return carry

    lax.fori_loop(0, groups, group, 0)

    lane_in, x_out = iota((SPLIT * LANES, LANES), 0), iota((SPLIT * LANES, LANES), 1) % NX
    gather = one_hot(x_out == SPLIT * (lane_in % STEPS) + lane_in // LANES)
    left = lane_halves((fields, LANES))
    factor = 4.0 / count * -0.5
    planes = []
    for z in range(depth):
        parts = [
            jnp.concatenate([acc_ref[z, y, m] for y in range(rows)], axis=0) for m in range(SPLIT)
        ]
        acc = jnp.concatenate(parts, axis=1)
        upper = acc.astype(jnp.bfloat16)
        lower = (acc - upper.astype(jnp.float32)).astype(jnp.bfloat16)
        total = bf16_dot(upper, gather) + bf16_dot(lower, gather)
        tiles = []
        for y in range(rows):
            tiles.append(total[y * fields : (y + 1) * fields])
        pieces = []
        for y in range(0, rows, 2):
            start = (y + LEAD) // 2 * depth + z
            value = parts_ref[pl.ds(start, fields, stride=parts_ref.shape[0] // fields), :]
            pieces.append(value + factor * jnp.where(left, tiles[y], tiles[y + 1]))
        planes.append(jnp.concatenate(pieces, axis=1))
    stacked = jnp.concatenate(planes, axis=0).astype(jnp.bfloat16)
    all_rows = depth * fields

    pick = one_hot(iota((all_rows, fields), 0) // depth == iota((all_rows, fields), 1))
    tile = one_hot(iota((fields, all_rows), 1) % fields == iota((fields, all_rows), 0))
    wide = bf16_dot(bf16_dot(pick, inverse_ref[...]).astype(jnp.bfloat16), tile)
    square = (all_rows, all_rows)
    same = iota(square, 0) % depth == iota(square, 1) // fields
    wide = jnp.where(same, wide, 0.0).astype(jnp.bfloat16)
    updated = bf16_dot(wide, stacked)

    m_ref[...] = jnp.zeros_like(m_ref)
    gram = jnp.zeros((fields, fields), jnp.float32)
    for z in range(depth):
        one = planes[z].astype(jnp.bfloat16)
        gram = gram + lax.dot_general(
            one, one, (((1,), (1,)), ((), ())), preferred_element_type=jnp.float32
        )
    m_ref[:, :fields] = gram
    pieces = rows * NX // LANES
    for p in range(fields):
        for t in range(pieces):
            out_ref[p, t] = updated[p * depth : (p + 1) * depth, t * LANES : (t + 1) * LANES]
        out_ref[p, pieces] = jnp.broadcast_to(m_ref[p : p + 1, :], (depth, LANES))


VMEM = pl.BlockSpec(memory_space=pltpu.VMEM)
SMEM = pl.BlockSpec(memory_space=pltpu.SMEM)


def in_vmem(*arrays):
    return [pltpu.with_memory_space_constraint(array, pltpu.VMEM) for array in arrays]


def swapped(to_a, to_b, axis):
    count = lax.axis_size(axis)
    pairs_a = [(i, i ^ 1) for i in range(count)]
    pairs_b = [(i, i + 1 if i % 2 else i - 1) for i in range(1, count - 1)]
    return lax.ppermute(to_a, axis, pairs_a), lax.ppermute(to_b, axis, pairs_b)


def rows_plan(potentials, orbitals, energies, local_potential, inverse_factor):
    pots = lax.axis_size("pot")
    grids = lax.axis_size("grid")
    depth = potentials.shape[1]
    count, _, width = orbitals.shape
    rows = width // NX
    fields = pots
    half = count // 2
    f32, bf16 = jnp.float32, jnp.bfloat16
    shape = pltpu.VMEM
    tile = (half + fields, LANES)

    region = (depth + 2 * HALO, rows + 2 * HALO)
    pieces = width // LANES
    window = pieces + 2 * (LEAD * NX // LANES)
    limit = pltpu.CompilerParams(vmem_limit_bytes=VMEM_LIMIT)
    call = functools.partial(pl.pallas_call, compiler_params=limit)
    windows = call(
        window_kernel,
        out_shape=shape((pots, window, depth, LANES), f32),
        in_specs=[VMEM],
        out_specs=VMEM,
        name="windows",
    )(potentials)
    parts = lax.all_to_all(windows, "pot", 0, 0, tiled=True)
    parts = parts.reshape(pots * window * depth, LANES)

    side = len(row_cells(depth))
    own, to_a, to_b = call(
        orbital_kernel,
        out_shape=[
            shape((depth, rows, half, LANES), bf16),
            shape((side, half, LANES), bf16),
            shape((side, half, LANES), bf16),
        ],
        in_specs=[VMEM],
        out_specs=[VMEM] * 3,
        scratch_shapes=[pltpu.VMEM((half * rows * depth, LANES), f32)],
        name="orbitals",
    )(orbitals)
    got_a, got_b = swapped(to_a, to_b, "pot")

    inverse_diagonal = call(
        diagonal_kernel,
        out_shape=shape(region + (half, LANES), f32),
        in_specs=[SMEM, VMEM],
        out_specs=VMEM,
        scratch_shapes=[pltpu.VMEM((rows + 2 * LEAD, region[0] * SPLIT, LANES), f32)]
        + [pltpu.VMEM((rows // 2 + LEAD, local_potential.shape[0], LANES), f32)] * 3,
        name="diagonal",
    )(energies, local_potential)

    edge = len(plane_cells(rows))
    up, down = call(
        send_kernel,
        out_shape=[shape((edge,) + tile, bf16)] * 2,
        in_specs=[VMEM] * 4,
        out_specs=[VMEM] * 2,
        name="sends",
    )(*in_vmem(parts, own, got_a, got_b))
    z_a, z_b = swapped(up, down, "grid")

    own_values = [
        shape(region + (half, LANES), f32),
        shape(region + (SPLIT, fields, LANES), f32),
        shape((depth, rows, SPLIT, fields, LANES), f32),
    ]
    prepared = call(
        prepare_kernel,
        out_shape=own_values,
        in_specs=[VMEM] * 5,
        out_specs=[VMEM] * 3,
        scratch_shapes=[pltpu.VMEM((rows, half, LANES), f32)],
        name="prepare",
    )(*in_vmem(parts, own, got_a, got_b, inverse_diagonal))
    sent, *_ = call(
        sweep_kernel,
        out_shape=[shape((fields, pieces + 1, depth, LANES), f32)] + own_values,
        in_specs=[VMEM] * 8,
        out_specs=[VMEM] * 4,
        scratch_shapes=[
            pltpu.VMEM(region + (SPLIT, fields, LANES), f32),
            pltpu.VMEM(region + (SPLIT, fields, LANES), f32),
            pltpu.VMEM(region + (SPLIT, fields, LANES), f32),
            pltpu.VMEM((fields, LANES), f32),
        ],
        input_output_aliases={5: 1, 6: 2, 7: 3},
        name="sweeps",
    )(*in_vmem(parts, z_a, z_b, inverse_diagonal), inverse_factor, *in_vmem(*prepared))

    back = lax.all_to_all(sent, "pot", 0, 0, tiled=True)
    updated = back[:, :pieces].reshape(pots * pieces, depth, LANES).transpose(1, 0, 2)
    updated = updated.reshape(1, depth, pots * width)
    margins = jnp.sum(back[:, pieces], axis=0)
    step = 1
    while step < grids:
        margins = margins + lax.ppermute(margins, "grid", [(i, i ^ step) for i in range(grids)])
        step *= 2
    margins = margins[:1, :fields] / local_potential.size
    return updated, margins


def local(potentials, orbitals, energies, local_potential, inverse_factor):
    pots = lax.axis_size("pot")
    grids = lax.axis_size("grid")
    depth = potentials.shape[1]
    count, _, width = orbitals.shape
    fits = (
        potentials.shape[0] == 1
        and pots == 8
        and width % LANES == 0
        and LANES == 2 * NX
        and width // NX >= HALO
        and depth == 8
        and count % (BATCH * SPLIT) == 0
        and count // BATCH in (2, 4)
        and grids & (grids - 1) == 0
    )
    plan = rows_plan if fits else gathered_plan
    return plan(potentials, orbitals, energies, local_potential, inverse_factor)


def solution(mesh):
    in_specs = (P("pot", "grid", None), P(None, "grid", "pot"), P(), P(), P())
    out_specs = (P("pot", "grid", None), P("pot", None))
    return jax.shard_map(local, mesh=mesh, in_specs=in_specs, out_specs=out_specs, check_vma=False)
```

```python
import functools
import math

import jax
import jax.numpy as jnp
from jax import lax
from jax.experimental import pallas as pl
from jax.experimental.pallas import tpu as pltpu
from jax.sharding import PartitionSpec as P


NX = 64
SWEEPS = 4
DAMPING = 0.8
COEFFS = tuple(
    sum(math.comb(n, m) * (1.0 - DAMPING) ** (n - m) for n in range(m, SWEEPS))
    for m in range(SWEEPS)
)
HALO = SWEEPS - 1
LEAD = HALO + HALO % 2
LANES = 128
SUBLANES = 8
VMEM_LIMIT = 24 << 20


def padded_2(block, sides, width):
    for axis, dim in sides:
        count = lax.axis_size(axis)
        forward = [(i, i + 1) for i in range(count - 1)]
        backward = [(target, source) for source, target in forward]
        low = lax.ppermute(
            lax.slice_in_dim(block, block.shape[dim] - width, None, axis=dim), axis, forward
        )
        high = lax.ppermute(lax.slice_in_dim(block, 0, width, axis=dim), axis, backward)
        block = jnp.concatenate([low, block, high], axis=dim)
    return block


def plane_neighbours(field, row_width):
    plane_size = field.shape[-1]
    widths = [(0, 0)] * (field.ndim - 1)
    padded = jnp.pad(field, widths + [(row_width, row_width)])
    along_y = padded[..., 2 * row_width :] + padded[..., :plane_size]
    column = jnp.arange(plane_size, dtype=jnp.int32) % row_width
    padded = jnp.pad(field, widths + [(1, 1)])
    right_side = jnp.where(column == row_width - 1, 0.0, padded[..., 2:])
    left_side = jnp.where(column == 0, 0.0, padded[..., :plane_size])
    return along_y + right_side + left_side


def across_slabs(answer):
    padded = padded_2(answer, (("grid", 2),), 1)
    return padded[:, :, 2:] + padded[:, :, :-2]


def absorb(orbital_block, energy_block, fields, local_here, along_planes):
    orbital = orbital_block.astype(jnp.float32)[:, None]
    diagonal = (3.0 + local_here[None] - energy_block[:, None, None])[:, None]
    source = -orbital * fields[None]
    answer = DAMPING * source / diagonal
    for _ in range(SWEEPS - 1):
        nearby = along_planes(answer) + plane_neighbours(answer, NX)
        answer = answer + DAMPING * (source - diagonal * answer + 0.5 * nearby) / diagonal
    return jnp.sum(orbital * answer, axis=0)


def gathered_plan(potentials, orbitals, energies, local_potential, inverse_factor):
    slab_depth = potentials.shape[1]
    count = orbitals.shape[0]
    cells = local_potential.size
    grid_index = lax.axis_index("grid")
    local_here = lax.dynamic_slice_in_dim(local_potential, grid_index * slab_depth, slab_depth, 0)
    blocks = 4 if count % 4 == 0 else 1
    block_size = count // blocks
    response = jnp.zeros(potentials.shape, jnp.float32)
    for number in range(blocks):
        orbital_block = orbitals[number * block_size : (number + 1) * block_size]
        gathered = lax.all_gather(orbital_block, "pot", axis=2, tiled=True)
        energy_block = energies[number * block_size : (number + 1) * block_size]
        response = response + absorb(gathered, energy_block, potentials, local_here, across_slabs)
    trial_block = (potentials + 4.0 / count * response).astype(jnp.bfloat16)
    by_cells = lax.all_to_all(trial_block, "pot", split_axis=2, concat_axis=0, tiled=True)
    row_count = by_cells.shape[0]
    flattened = by_cells.reshape(row_count, -1)
    partial_margins = lax.dot_general(
        flattened, flattened, (((1,), (1,)), ((), ())), preferred_element_type=jnp.float32
    )
    combined = jnp.dot(inverse_factor, flattened, preferred_element_type=jnp.float32).reshape(
        by_cells.shape
    )
    updated = lax.all_to_all(combined, "pot", split_axis=0, concat_axis=2, tiled=True)
    scattered = lax.psum_scatter(partial_margins, "pot", scatter_dimension=0, tiled=True)
    own_rows = lax.psum(scattered, "grid")
    margins = own_rows / cells
    return (updated, margins)


def row_cells(depth):
    return [(d, z) for d in range(1, HALO + 1) for z in range(depth)]


def plane_cells(rows):
    return [(d, y) for d in range(1, HALO + 1) for y in range(d - HALO, rows + HALO - d)]


def iota(shape, dim):
    return lax.broadcasted_iota(jnp.int32, shape, dim)


def bf16_dot(a, b):
    return jnp.dot(a, b, preferred_element_type=jnp.float32)


def one_hot(mask):
    return mask.astype(jnp.float32).astype(jnp.bfloat16)


def lane_halves(shape):
    return iota(shape, len(shape) - 1) < NX


SPLIT = 4
STEPS = NX // SPLIT
BATCH = LANES // STEPS


def orbital_kernel(orb_ref, own_ref, a_ref, b_ref, s_ref):
    count, depth, width = orb_ref.shape
    groups = count // BATCH
    rows = width // NX
    lane_in, lane_out = iota((LANES, LANES), 0), iota((LANES, LANES), 1)
    wanted = (lane_out // NX) * NX + SPLIT * (lane_out % STEPS) + lane_out // STEPS % SPLIT
    permute = one_hot(lane_in == wanted)
    lane = iota((depth, LANES), 1) // STEPS
    for t in range(width // LANES):
        lanes = slice(t * LANES, (t + 1) * LANES)
        tile = orb_ref[:, :, lanes].astype(jnp.float32).reshape(count * depth, LANES)
        tile = bf16_dot(tile.astype(jnp.bfloat16), permute)
        for g in range(groups):
            first = g * BATCH * depth
            regs = [tile[first + b * depth : first + (b + 1) * depth] for b in range(BATCH)]
            step = BATCH // 2
            while step:
                stays = lane // step % 2 == 0
                for b in range(BATCH):
                    if b & step == 0:
                        lo, hi = regs[b], regs[b + step]
                        regs[b] = jnp.where(stays, lo, pltpu.roll(hi, step * STEPS, 1))
                        regs[b + step] = jnp.where(
                            stays, pltpu.roll(lo, LANES - step * STEPS, 1), hi
                        )
                step //= 2
            for c in range(BATCH):
                y, m = 2 * t + c // SPLIT, c % SPLIT
                at = ((m * groups + g) * rows + y) * depth
                s_ref[at : at + depth] = regs[c]
    for z in range(depth):
        for y in range(rows):
            tile = s_ref[pl.ds(y * depth + z, SPLIT * groups, stride=rows * depth), :]
            own_ref[z, y] = tile.astype(jnp.bfloat16)
    even = lax.rem(lax.axis_index("pot"), 2) == 0
    for at, (d, z) in enumerate(row_cells(depth)):
        a_ref[at] = own_ref[z, jnp.where(even, rows - d, d - 1)]
        b_ref[at] = own_ref[z, jnp.where(even, d - 1, rows - d)]


def window_kernel(v_ref, out_ref):
    receivers, pieces = out_ref.shape[:2]
    total = v_ref.shape[2] // LANES
    stride = total // receivers
    ahead = LEAD * NX // LANES
    for p in range(receivers):
        for t in range(pieces):
            at = p * stride + t - ahead
            if 0 <= at < total:
                out_ref[p, t] = v_ref[0, :, at * LANES : (at + 1) * LANES]
            else:
                out_ref[p, t] = jnp.zeros(out_ref.shape[2:], out_ref.dtype)


def two_parts(value, y):
    left = lane_halves(value.shape)
    upper = value.astype(jnp.bfloat16).astype(jnp.float32)
    lower = value - upper
    if y % 2:
        return jnp.where(left, pltpu.roll(upper, NX, 1), lower)
    return jnp.where(left, upper, pltpu.roll(lower, NX, 1))


def row_tile(own_ref, a_ref, b_ref, z, y):
    depth, rows = own_ref.shape[:2]
    even = lax.rem(lax.axis_index("pot"), 2) == 0
    if 0 <= y < rows:
        return own_ref[z, y]
    at = (-y - 1 if y < 0 else y - rows) * depth + z
    a, b = a_ref[at].astype(jnp.float32), b_ref[at].astype(jnp.float32)
    return jnp.where(even == (y < 0), b, a).astype(jnp.bfloat16)


def send_kernel(v_ref, own_ref, a_ref, b_ref, to_a_ref, to_b_ref):
    depth, rows = own_ref.shape[:2]
    pieces = rows * NX // LANES + 2 * (LEAD * NX // LANES)
    fields = v_ref.shape[0] // (pieces * depth)
    even = lax.rem(lax.axis_index("grid"), 2) == 0

    def tile_of(z, y):
        start = (y + LEAD) // 2 * depth + z
        value = v_ref[pl.ds(start, fields, stride=pieces * depth), :]
        orbitals = row_tile(own_ref, a_ref, b_ref, z, y).astype(jnp.float32)
        return jnp.concatenate([orbitals, two_parts(value, y)], axis=0)

    for at, (d, y) in enumerate(plane_cells(rows)):
        top, bottom = tile_of(depth - d, y), tile_of(d - 1, y)
        to_a_ref[at] = jnp.where(even, top, bottom).astype(jnp.bfloat16)
        to_b_ref[at] = jnp.where(even, bottom, top).astype(jnp.bfloat16)


def diagonal_kernel(energy_ref, lp_ref, r_ref, lp_ref2, *part_refs):
    planes_all, plane_cells = lp_ref.shape
    rows_all = plane_cells // NX
    region_z, region_y, size, _ = r_ref.shape
    depth, rows = region_z - 2 * HALO, region_y - 2 * HALO
    groups = size // SPLIT
    z_base = lax.axis_index("grid") * depth
    y_base = lax.axis_index("pot") * rows

    shift = jnp.zeros((size, LANES), jnp.float32)
    group_of = iota((size, LANES), 0) % groups
    member = iota((size, LANES), 1) // STEPS
    for g in range(groups):
        for b in range(BATCH):
            here = (group_of == g) & (member == b)
            shift = jnp.where(here, 3.0 - energy_ref[g * BATCH + b], shift)

    pairs = part_refs[0].shape[0]
    for p in range(pairs):
        at = jnp.clip((y_base - LEAD) // 2 + p, 0, rows_all // 2 - 1) * LANES
        rest = lp_ref[:, pl.ds(pl.multiple_of(at, LANES), LANES)]
        for part_ref in part_refs:
            part = rest.astype(jnp.bfloat16).astype(jnp.float32)
            part_ref[p] = part
            rest = rest - part
    from_lane, to_lane = iota((LANES, 2 * LANES), 0), iota((LANES, 2 * LANES), 1)
    pick = one_hot(
        (from_lane // NX == to_lane // LANES) & (from_lane % NX // SPLIT == to_lane % STEPS)
    )
    tile = (SUBLANES, LANES)
    keep = iota(tile, 1) % SPLIT == iota(tile, 0) % SPLIT
    per_tile = SUBLANES // SPLIT
    plane_of = iota(tile, 0) // SPLIT

    def clipped(zi):
        return jnp.clip(z_base + zi - HALO, 0, planes_all - 1)

    def chosen(index, values):
        out = jnp.broadcast_to(values[0], tile)
        for number, value in enumerate(values[1:], 1):
            out = jnp.where(index == number, jnp.broadcast_to(value, tile), out)
        return out

    for p in range(pairs):
        stacked = []
        for ref in part_refs:
            for zi in range(0, region_z, per_tile):
                values = [ref[p, pl.ds(clipped(zi + i), 1), :] for i in range(per_tile)]
                stacked.append(jnp.where(keep, chosen(plane_of, values), 0.0))
        parts = bf16_dot(jnp.concatenate(stacked, axis=0).astype(jnp.bfloat16), pick)
        length = region_z * SPLIT
        lp = (parts[:length] + parts[length : 2 * length]) + parts[2 * length :]
        lp_ref2[2 * p] = lp[:, :LANES]
        lp_ref2[2 * p + 1] = lp[:, LANES:]

    m_of = iota(tile, 0) // groups
    ms = SUBLANES // groups

    def plane(zi, carry):
        zg = z_base + zi - HALO
        z_inside = (zg >= 0) & (zg < planes_all)
        for y in range(-HALO, rows + HALO):
            yg = y_base + y
            inside = z_inside & (yg >= 0) & (yg < rows_all)
            scale = jnp.where(inside, 0.5 * DAMPING, 0.0)
            for part in range(size // SUBLANES):
                values = [
                    lp_ref2[y + LEAD, pl.ds(zi * SPLIT + part * ms + i, 1), :] for i in range(ms)
                ]
                at = slice(part * SUBLANES, (part + 1) * SUBLANES)
                r_ref[zi, y + HALO, at] = scale / (shift[at] + chosen(m_of, values))
        return carry

    lax.fori_loop(0, region_z, plane, 0)


def spread_matrix():
    from_lane = iota((LANES, SPLIT * LANES), 0)
    to_lane = iota((LANES, SPLIT * LANES), 1)
    return one_hot(from_lane % NX == SPLIT * (to_lane % STEPS) + to_lane // LANES)


def place(cells, r_ref, ro_ref, first_ref, then=None):
    fields = first_ref.shape[4]
    packed = jnp.concatenate([parts for _, parts, _, _ in cells], axis=0).astype(jnp.bfloat16)
    values = bf16_dot(packed, spread_matrix())
    for number, (orbitals, _, z, y) in enumerate(cells):
        zi, yi = z + HALO, y + HALO
        o = -2.0 * orbitals.astype(jnp.float32)
        ro = r_ref[zi, yi] * o
        ro_ref[zi, yi] = ro
        own = [
            values[number * fields : (number + 1) * fields, m * LANES : (m + 1) * LANES]
            for m in range(SPLIT)
        ]
        first_sweep(ro_ref, first_ref, z, y, own)
        if then is not None:
            then(z, y, o * ro, own)


def first_sweep(ro_ref, first_ref, z, y, values):
    groups = first_ref.shape[0]
    zi, yi = z + HALO, y + HALO
    for g in range(groups):
        for m in range(SPLIT):
            at = m * groups + g
            ro = jnp.broadcast_to(ro_ref[zi, yi, at : at + 1], values[m].shape)
            first_ref[g, zi, yi, m] = ro * values[m]


def prepare_kernel(
    parts_ref, own_ref, a_ref, b_ref, r_ref, ro_ref, first_ref, acc_ref, w_ref
):
    depth, rows = own_ref.shape[:2]
    fields = first_ref.shape[4]
    size = ro_ref.shape[2]
    groups = size // SPLIT
    pieces = parts_ref.shape[0] // (depth * fields)

    def first_term(z, y, weight, values):
        if not 0 <= y < rows:
            return
        turn = groups // 2
        while turn:
            weight = weight + pltpu.roll(weight, size - turn, 0)
            turn //= 2
        w_ref[y] = COEFFS[0] * weight
        for m in range(SPLIT):
            at = m * groups
            w = jnp.broadcast_to(w_ref[y, at : at + 1], (fields, LANES))
            acc_ref[z, y, m] = w * values[m]

    def plane(z, carry):
        cells = []
        for y in range(-HALO, rows + HALO):
            start = (y + LEAD) // 2 * depth + z
            value = parts_ref[pl.ds(start, fields, stride=pieces * depth), :]
            cells.append((row_tile(own_ref, a_ref, b_ref, z, y), two_parts(value, y), z, y))
        place(cells, r_ref, ro_ref, first_ref, first_term)
        return carry

    lax.fori_loop(0, depth, plane, 0)


def sweep_kernel(
    parts_ref, a_ref, b_ref, r_ref, inverse_ref, ro_in, first_in, acc_in,
    out_ref, ro_ref, first_ref, acc_ref, x_ref, y_ref, m_ref,
):
    depth, rows = acc_ref.shape[:2]
    fields = first_ref.shape[4]
    size = ro_ref.shape[2]
    groups = size // SPLIT
    count = groups * BATCH
    even = lax.rem(lax.axis_index("grid"), 2) == 0
    all_cells = list(enumerate(plane_cells(rows)))
    for d in range(1, HALO + 1):
        z_a = jnp.where(even, depth - 1 + d, -d)
        z_b = jnp.where(even, -d, depth - 1 + d)
        cells = []
        for at, (distance, y) in all_cells:
            if distance == d:
                for ref, z in ((a_ref, z_a), (b_ref, z_b)):
                    tile = ref[at].astype(jnp.float32)
                    cells.append((tile[:size], tile[size:], z, y))
        place(cells, r_ref, ro_ref, first_ref)

    step = iota((fields, LANES), 1) % STEPS
    first_k = step == 0
    last_k = step == STEPS - 1

    def group(g, carry):
        buffers = (first_ref.at[g], x_ref, y_ref)

        def stage(number, z, reach, deep):
            coeff = COEFFS[SWEEPS - 1 - number]
            target = buffers[min(number, SWEEPS - 2)]
            source = buffers[number - 1]

            def of_group(ref, i, y, m):
                return jnp.broadcast_to(ref[z + i, y, pl.ds(m * groups + g, 1), :], (fields, LANES))

            def row(i, y):
                return [source[z + i, y, m] for m in range(SPLIT)]

            ys = range(HALO - reach, HALO + rows + reach)
            before = [row(i, ys[0] - 1) for i in range(deep)]
            here = [row(i, ys[0]) for i in range(deep)]
            for y in ys:
                after = [row(i, y + 1) for i in range(deep)]
                under, over = row(-1, y), row(deep, y)
                for i in range(deep):
                    lower = here[i - 1] if i else under
                    upper = here[i + 1] if i + 1 < deep else over
                    mid = here[i]
                    for m in range(SPLIT):
                        if m:
                            left = mid[m - 1]
                        else:
                            left = jnp.where(first_k, 0.0, pltpu.roll(mid[SPLIT - 1], 1, 1))
                        if m + 1 < SPLIT:
                            right = mid[m + 1]
                        else:
                            right = jnp.where(last_k, 0.0, pltpu.roll(mid[0], LANES - 1, 1))
                        near = (before[i][m] + after[i][m]) + (lower[m] + upper[m])
                        near = near + (left + right)
                        if number == SWEEPS - 1:
                            term = of_group(ro_ref, i, y, m) * near
                            acc_ref[z + i - HALO, y - HALO, m] += term
                            continue
                        base = mid[m] if number == 1 else buffers[0][z + i, y, m]
                        target[z + i, y, m] = of_group(r_ref, i, y, m) * near + coeff * base
                before, here = here, after

        for number in range(1, SWEEPS):
            reach = HALO - number

            def inner(pair, c, number=number, reach=reach):
                stage(number, HALO + 2 * pair, reach, 2)
                return c

            for d in range(1, reach + 1):
                stage(number, HALO - d, reach - d, 1)
                stage(number, HALO + depth - 1 + d, reach - d, 1)
            lax.fori_loop(0, depth // 2, inner, 0)
        return carry

    lax.fori_loop(0, groups, group, 0)

    lane_in, x_out = iota((SPLIT * LANES, LANES), 0), iota((SPLIT * LANES, LANES), 1) % NX
    gather = one_hot(x_out == SPLIT * (lane_in % STEPS) + lane_in // LANES)
    left = lane_halves((fields, LANES))
    factor = 4.0 / count * -0.5
    planes = []
    for z in range(depth):
        parts = [
            jnp.concatenate([acc_ref[z, y, m] for y in range(rows)], axis=0) for m in range(SPLIT)
        ]
        acc = jnp.concatenate(parts, axis=1)
        upper = acc.astype(jnp.bfloat16)
        lower = (acc - upper.astype(jnp.float32)).astype(jnp.bfloat16)
        total = bf16_dot(upper, gather) + bf16_dot(lower, gather)
        tiles = []
        for y in range(rows):
            tiles.append(total[y * fields : (y + 1) * fields])
        pieces = []
        for y in range(0, rows, 2):
            start = (y + LEAD) // 2 * depth + z
            value = parts_ref[pl.ds(start, fields, stride=parts_ref.shape[0] // fields), :]
            pieces.append(value + factor * jnp.where(left, tiles[y], tiles[y + 1]))
        planes.append(jnp.concatenate(pieces, axis=1))
    stacked = jnp.concatenate(planes, axis=0).astype(jnp.bfloat16)
    all_rows = depth * fields

    pick = one_hot(iota((all_rows, fields), 0) // depth == iota((all_rows, fields), 1))
    tile = one_hot(iota((fields, all_rows), 1) % fields == iota((fields, all_rows), 0))
    wide = bf16_dot(bf16_dot(pick, inverse_ref[...]).astype(jnp.bfloat16), tile)
    square = (all_rows, all_rows)
    same = iota(square, 0) % depth == iota(square, 1) // fields
    wide = jnp.where(same, wide, 0.0).astype(jnp.bfloat16)
    updated = bf16_dot(wide, stacked)

    m_ref[...] = jnp.zeros_like(m_ref)
    gram = jnp.zeros((fields, fields), jnp.float32)
    for z in range(depth):
        one = planes[z].astype(jnp.bfloat16)
        gram = gram + lax.dot_general(
            one, one, (((1,), (1,)), ((), ())), preferred_element_type=jnp.float32
        )
    m_ref[:, :fields] = gram
    pieces = rows * NX // LANES
    for p in range(fields):
        for t in range(pieces):
            out_ref[p, t] = updated[p * depth : (p + 1) * depth, t * LANES : (t + 1) * LANES]
        out_ref[p, pieces] = jnp.broadcast_to(m_ref[p : p + 1, :], (depth, LANES))


VMEM = pl.BlockSpec(memory_space=pltpu.VMEM)
SMEM = pl.BlockSpec(memory_space=pltpu.SMEM)


def in_vmem(*arrays):
    return [pltpu.with_memory_space_constraint(array, pltpu.VMEM) for array in arrays]


def in_hbm(array):
    return pltpu.with_memory_space_constraint(array, pltpu.HBM)


def swapped(to_a, to_b, axis):
    count = lax.axis_size(axis)
    pairs_a = [(i, i ^ 1) for i in range(count)]
    pairs_b = [(i, i + 1 if i % 2 else i - 1) for i in range(1, count - 1)]
    got_a = lax.ppermute(to_a, axis, pairs_a)
    got_b = lax.ppermute(to_b, axis, pairs_b)
    return got_a, got_b


def rows_plan(potentials, orbitals, energies, local_potential, inverse_factor):
    pots = lax.axis_size("pot")
    grids = lax.axis_size("grid")
    depth = potentials.shape[1]
    count, _, width = orbitals.shape
    rows = width // NX
    fields = pots
    half = count // 2
    f32, bf16 = jnp.float32, jnp.bfloat16
    shape = pltpu.VMEM
    tile = (half + fields, LANES)

    region = (depth + 2 * HALO, rows + 2 * HALO)
    pieces = width // LANES
    window = pieces + 2 * (LEAD * NX // LANES)
    limit = pltpu.CompilerParams(vmem_limit_bytes=VMEM_LIMIT)
    call = functools.partial(pl.pallas_call, compiler_params=limit)
    side = len(row_cells(depth))
    own, to_a, to_b = call(
        orbital_kernel,
        out_shape=[
            shape((depth, rows, half, LANES), bf16),
            shape((side, half, LANES), bf16),
            shape((side, half, LANES), bf16),
        ],
        in_specs=[VMEM],
        out_specs=[VMEM] * 3,
        scratch_shapes=[pltpu.VMEM((half * rows * depth, LANES), f32)],
        name="orbitals",
    )(in_hbm(orbitals))
    got_a, got_b = swapped(to_a, to_b, "pot")

    windows = call(
        window_kernel,
        out_shape=shape((pots, window, depth, LANES), f32),
        in_specs=[VMEM],
        out_specs=VMEM,
        name="windows",
    )(in_hbm(potentials))
    parts = lax.all_to_all(windows, "pot", 0, 0, tiled=True)
    parts = parts.reshape(pots * window * depth, LANES)

    inverse_diagonal = call(
        diagonal_kernel,
        out_shape=shape(region + (half, LANES), f32),
        in_specs=[SMEM, VMEM],
        out_specs=VMEM,
        scratch_shapes=[pltpu.VMEM((rows + 2 * LEAD, region[0] * SPLIT, LANES), f32)]
        + [pltpu.VMEM((rows // 2 + LEAD, local_potential.shape[0], LANES), f32)] * 3,
        name="diagonal",
    )(energies, local_potential)

    parts, inverse_diagonal = lax.optimization_barrier((parts, inverse_diagonal))
    edge = len(plane_cells(rows))
    up, down = call(
        send_kernel,
        out_shape=[shape((edge,) + tile, bf16)] * 2,
        in_specs=[VMEM] * 4,
        out_specs=[VMEM] * 2,
        name="sends",
    )(*in_vmem(parts, own, got_a, got_b))
    z_a, z_b = swapped(up, down, "grid")

    own_values = [
        shape(region + (half, LANES), f32),
        shape((half // SPLIT,) + region + (SPLIT, fields, LANES), f32),
        shape((depth, rows, SPLIT, fields, LANES), f32),
    ]
    prepared = call(
        prepare_kernel,
        out_shape=own_values,
        in_specs=[VMEM] * 5,
        out_specs=[VMEM] * 3,
        scratch_shapes=[pltpu.VMEM((rows, half, LANES), f32)],
        name="prepare",
    )(*in_vmem(parts, own, got_a, got_b, inverse_diagonal))
    sent, *_ = call(
        sweep_kernel,
        out_shape=[shape((fields, pieces + 1, depth, LANES), f32)] + own_values,
        in_specs=[VMEM] * 8,
        out_specs=[VMEM] * 4,
        scratch_shapes=[
            pltpu.VMEM(region + (SPLIT, fields, LANES), f32),
            pltpu.VMEM(region + (SPLIT, fields, LANES), f32),
            pltpu.VMEM((fields, LANES), f32),
        ],
        input_output_aliases={5: 1, 6: 2, 7: 3},
        name="sweeps",
    )(*in_vmem(parts, z_a, z_b, inverse_diagonal), inverse_factor, *in_vmem(*prepared))

    back = lax.all_to_all(sent, "pot", 0, 0, tiled=True)
    updated = back[:, :pieces].reshape(pots * pieces, depth, LANES).transpose(1, 0, 2)
    updated = updated.reshape(1, depth, pots * width)
    margins = jnp.sum(back[:, pieces], axis=0)
    step = 1
    while step < grids:
        margins = margins + lax.ppermute(margins, "grid", [(i, i ^ step) for i in range(grids)])
        step *= 2
    margins = margins[:1, :fields] / local_potential.size
    return updated, margins


def local(potentials, orbitals, energies, local_potential, inverse_factor):
    pots = lax.axis_size("pot")
    grids = lax.axis_size("grid")
    depth = potentials.shape[1]
    count, _, width = orbitals.shape
    fits = (
        potentials.shape[0] == 1
        and pots == 8
        and width % LANES == 0
        and LANES == 2 * NX
        and width // NX >= HALO
        and depth == 8
        and count % (BATCH * SPLIT) == 0
        and count // BATCH in (2, 4)
        and grids & (grids - 1) == 0
    )
    plan = rows_plan if fits else gathered_plan
    return plan(potentials, orbitals, energies, local_potential, inverse_factor)


def solution(mesh):
    in_specs = (P("pot", "grid", None), P(None, "grid", "pot"), P(), P(), P())
    out_specs = (P("pot", "grid", None), P("pot", None))
    return jax.shard_map(local, mesh=mesh, in_specs=in_specs, out_specs=out_specs, check_vma=False)
```

```python
import functools
import math

import jax
import jax.numpy as jnp
from jax import lax
from jax.experimental import pallas as pl
from jax.experimental.pallas import tpu as pltpu
from jax.sharding import PartitionSpec as P


NX = 64
SWEEPS = 4
DAMPING = 0.8
COEFFS = tuple(
    sum(math.comb(n, m) * (1.0 - DAMPING) ** (n - m) for n in range(m, SWEEPS))
    for m in range(SWEEPS)
)
START = COEFFS[SWEEPS - 2]
WEIGHTS = [COEFFS[SWEEPS - 2 - n] / START for n in range(SWEEPS - 2)]
INNER = tuple(
    ((1.0 / START) if n == 0 else WEIGHTS[n - 1]) / WEIGHTS[n] for n in range(SWEEPS - 2)
)
LAST = WEIGHTS[-1]
HALO = SWEEPS - 1
LEAD = HALO + HALO % 2
LANES = 128
SUBLANES = 8
VMEM_LIMIT = 24 << 20


def padded_2(block, sides, width):
    for axis, dim in sides:
        count = lax.axis_size(axis)
        forward = [(i, i + 1) for i in range(count - 1)]
        backward = [(target, source) for source, target in forward]
        low = lax.ppermute(
            lax.slice_in_dim(block, block.shape[dim] - width, None, axis=dim), axis, forward
        )
        high = lax.ppermute(lax.slice_in_dim(block, 0, width, axis=dim), axis, backward)
        block = jnp.concatenate([low, block, high], axis=dim)
    return block


def plane_neighbours(field, row_width):
    plane_size = field.shape[-1]
    widths = [(0, 0)] * (field.ndim - 1)
    padded = jnp.pad(field, widths + [(row_width, row_width)])
    along_y = padded[..., 2 * row_width :] + padded[..., :plane_size]
    column = jnp.arange(plane_size, dtype=jnp.int32) % row_width
    padded = jnp.pad(field, widths + [(1, 1)])
    right_side = jnp.where(column == row_width - 1, 0.0, padded[..., 2:])
    left_side = jnp.where(column == 0, 0.0, padded[..., :plane_size])
    return along_y + right_side + left_side


def across_slabs(answer):
    padded = padded_2(answer, (("grid", 2),), 1)
    return padded[:, :, 2:] + padded[:, :, :-2]


def absorb(orbital_block, energy_block, fields, local_here, along_planes):
    orbital = orbital_block.astype(jnp.float32)[:, None]
    diagonal = (3.0 + local_here[None] - energy_block[:, None, None])[:, None]
    source = -orbital * fields[None]
    answer = DAMPING * source / diagonal
    for _ in range(SWEEPS - 1):
        nearby = along_planes(answer) + plane_neighbours(answer, NX)
        answer = answer + DAMPING * (source - diagonal * answer + 0.5 * nearby) / diagonal
    return jnp.sum(orbital * answer, axis=0)


def gathered_plan(potentials, orbitals, energies, local_potential, inverse_factor):
    slab_depth = potentials.shape[1]
    count = orbitals.shape[0]
    cells = local_potential.size
    grid_index = lax.axis_index("grid")
    local_here = lax.dynamic_slice_in_dim(local_potential, grid_index * slab_depth, slab_depth, 0)
    blocks = 4 if count % 4 == 0 else 1
    block_size = count // blocks
    response = jnp.zeros(potentials.shape, jnp.float32)
    for number in range(blocks):
        orbital_block = orbitals[number * block_size : (number + 1) * block_size]
        gathered = lax.all_gather(orbital_block, "pot", axis=2, tiled=True)
        energy_block = energies[number * block_size : (number + 1) * block_size]
        response = response + absorb(gathered, energy_block, potentials, local_here, across_slabs)
    trial_block = (potentials + 4.0 / count * response).astype(jnp.bfloat16)
    by_cells = lax.all_to_all(trial_block, "pot", split_axis=2, concat_axis=0, tiled=True)
    row_count = by_cells.shape[0]
    flattened = by_cells.reshape(row_count, -1)
    partial_margins = lax.dot_general(
        flattened, flattened, (((1,), (1,)), ((), ())), preferred_element_type=jnp.float32
    )
    combined = jnp.dot(inverse_factor, flattened, preferred_element_type=jnp.float32).reshape(
        by_cells.shape
    )
    updated = lax.all_to_all(combined, "pot", split_axis=0, concat_axis=2, tiled=True)
    scattered = lax.psum_scatter(partial_margins, "pot", scatter_dimension=0, tiled=True)
    own_rows = lax.psum(scattered, "grid")
    margins = own_rows / cells
    return (updated, margins)


def row_cells(depth):
    return [(d, z) for d in range(1, HALO + 1) for z in range(depth)]


def plane_cells(rows):
    return [(d, y) for d in range(1, HALO + 1) for y in range(d - HALO, rows + HALO - d)]


def iota(shape, dim):
    return lax.broadcasted_iota(jnp.int32, shape, dim)


def bf16_dot(a, b):
    return jnp.dot(a, b, preferred_element_type=jnp.float32)


def one_hot(mask):
    return mask.astype(jnp.float32).astype(jnp.bfloat16)


def lane_halves(shape):
    return iota(shape, len(shape) - 1) < NX


SPLIT = 4
STEPS = NX // SPLIT
BATCH = LANES // STEPS


def first_kernel(
    fields_ref, orbitals_ref, windows_ref, own_ref, a_ref, b_ref, wide_ref, orb_ref, s_ref, sem_ref
):
    receivers, window = windows_ref.shape[:2]
    total = fields_ref.shape[0]
    ahead = LEAD * NX // LANES
    fetch = pltpu.make_async_copy(fields_ref, wide_ref.at[pl.ds(ahead, total)], sem_ref.at[0])
    fetch_orbitals = pltpu.make_async_copy(orbitals_ref, orb_ref, sem_ref.at[1])
    fetch.start()
    fetch_orbitals.start()
    for t in range(ahead):
        wide_ref[t] = jnp.zeros(wide_ref.shape[1:], wide_ref.dtype)
        wide_ref[ahead + total + t] = jnp.zeros(wide_ref.shape[1:], wide_ref.dtype)
    fetch.wait()
    copies = [
        pltpu.make_async_copy(
            wide_ref.at[pl.ds(p * (total // receivers), window)], windows_ref.at[p], sem_ref.at[2 + p]
        )
        for p in range(receivers)
    ]
    for copy in copies:
        copy.start()
    fetch_orbitals.wait()
    relayout(orb_ref, own_ref, a_ref, b_ref, s_ref)
    for copy in copies:
        copy.wait()


def relayout(orb_ref, own_ref, a_ref, b_ref, s_ref):
    count, depth, width = orb_ref.shape
    groups = count // BATCH
    rows = width // NX
    lane_in, lane_out = iota((LANES, LANES), 0), iota((LANES, LANES), 1)
    wanted = (lane_out // NX) * NX + SPLIT * (lane_out % STEPS) + lane_out // STEPS % SPLIT
    permute = one_hot(lane_in == wanted)
    lane = iota((depth, LANES), 1) // STEPS
    for t in range(width // LANES):
        lanes = slice(t * LANES, (t + 1) * LANES)
        tile = orb_ref[:, :, lanes].astype(jnp.float32).reshape(count * depth, LANES)
        tile = bf16_dot(tile.astype(jnp.bfloat16), permute)
        for g in range(groups):
            first = g * BATCH * depth
            regs = [tile[first + b * depth : first + (b + 1) * depth] for b in range(BATCH)]
            step = BATCH // 2
            while step:
                stays = lane // step % 2 == 0
                for b in range(BATCH):
                    if b & step == 0:
                        lo, hi = regs[b], regs[b + step]
                        regs[b] = jnp.where(stays, lo, pltpu.roll(hi, step * STEPS, 1))
                        regs[b + step] = jnp.where(
                            stays, pltpu.roll(lo, LANES - step * STEPS, 1), hi
                        )
                step //= 2
            for c in range(BATCH):
                y, m = 2 * t + c // SPLIT, c % SPLIT
                at = ((m * groups + g) * rows + y) * depth
                s_ref[at : at + depth] = regs[c]
    for z in range(depth):
        for y in range(rows):
            tile = s_ref[pl.ds(y * depth + z, SPLIT * groups, stride=rows * depth), :]
            own_ref[z, y] = tile.astype(jnp.bfloat16)
    even = lax.rem(lax.axis_index("pot"), 2) == 0
    for at, (d, z) in enumerate(row_cells(depth)):
        a_ref[at] = own_ref[z, jnp.where(even, rows - d, d - 1)]
        b_ref[at] = own_ref[z, jnp.where(even, d - 1, rows - d)]


def two_parts(value, y):
    left = lane_halves(value.shape)
    upper = value.astype(jnp.bfloat16).astype(jnp.float32)
    lower = value - upper
    if y % 2:
        return jnp.where(left, pltpu.roll(upper, NX, 1), lower)
    return jnp.where(left, upper, pltpu.roll(lower, NX, 1))


def row_tile(own_ref, a_ref, b_ref, z, y):
    depth, rows = own_ref.shape[:2]
    even = lax.rem(lax.axis_index("pot"), 2) == 0
    if 0 <= y < rows:
        return own_ref[z, y]
    at = (-y - 1 if y < 0 else y - rows) * depth + z
    a, b = a_ref[at].astype(jnp.float32), b_ref[at].astype(jnp.float32)
    return jnp.where(even == (y < 0), b, a).astype(jnp.bfloat16)


def send_kernel(v_ref, own_ref, a_ref, b_ref, to_a_ref, to_b_ref):
    depth, rows = own_ref.shape[:2]
    pieces = rows * NX // LANES + 2 * (LEAD * NX // LANES)
    fields = v_ref.shape[0] // (pieces * depth)
    even = lax.rem(lax.axis_index("grid"), 2) == 0

    def tile_of(z, y):
        start = (y + LEAD) // 2 * depth + z
        value = v_ref[pl.ds(start, fields, stride=pieces * depth), :]
        orbitals = row_tile(own_ref, a_ref, b_ref, z, y).astype(jnp.float32)
        return jnp.concatenate([orbitals, two_parts(value, y)], axis=0)

    for at, (d, y) in enumerate(plane_cells(rows)):
        top, bottom = tile_of(depth - d, y), tile_of(d - 1, y)
        to_a_ref[at] = jnp.where(even, top, bottom).astype(jnp.bfloat16)
        to_b_ref[at] = jnp.where(even, bottom, top).astype(jnp.bfloat16)


def diagonal_kernel(energy_ref, lp_ref, r_ref, lp_ref2, *part_refs):
    planes_all, plane_cells = lp_ref.shape
    rows_all = plane_cells // NX
    region_z, region_y, size, _ = r_ref.shape
    depth, rows = region_z - 2 * HALO, region_y - 2 * HALO
    groups = size // SPLIT
    z_base = lax.axis_index("grid") * depth
    y_base = lax.axis_index("pot") * rows

    shift = jnp.zeros((size, LANES), jnp.float32)
    group_of = iota((size, LANES), 0) % groups
    member = iota((size, LANES), 1) // STEPS
    for g in range(groups):
        for b in range(BATCH):
            here = (group_of == g) & (member == b)
            shift = jnp.where(here, 3.0 - energy_ref[g * BATCH + b], shift)

    pairs = part_refs[0].shape[0]
    for p in range(pairs):
        at = jnp.clip((y_base - LEAD) // 2 + p, 0, rows_all // 2 - 1) * LANES
        rest = lp_ref[:, pl.ds(pl.multiple_of(at, LANES), LANES)]
        for part_ref in part_refs:
            part = rest.astype(jnp.bfloat16).astype(jnp.float32)
            part_ref[p] = part
            rest = rest - part
    from_lane, to_lane = iota((LANES, 2 * LANES), 0), iota((LANES, 2 * LANES), 1)
    pick = one_hot(
        (from_lane // NX == to_lane // LANES) & (from_lane % NX // SPLIT == to_lane % STEPS)
    )
    tile = (SUBLANES, LANES)
    keep = iota(tile, 1) % SPLIT == iota(tile, 0) % SPLIT
    per_tile = SUBLANES // SPLIT
    plane_of = iota(tile, 0) // SPLIT

    def clipped(zi):
        return jnp.clip(z_base + zi - HALO, 0, planes_all - 1)

    def chosen(index, values):
        out = jnp.broadcast_to(values[0], tile)
        for number, value in enumerate(values[1:], 1):
            out = jnp.where(index == number, jnp.broadcast_to(value, tile), out)
        return out

    for p in range(pairs):
        stacked = []
        for ref in part_refs:
            for zi in range(0, region_z, per_tile):
                values = [ref[p, pl.ds(clipped(zi + i), 1), :] for i in range(per_tile)]
                stacked.append(jnp.where(keep, chosen(plane_of, values), 0.0))
        parts = bf16_dot(jnp.concatenate(stacked, axis=0).astype(jnp.bfloat16), pick)
        length = region_z * SPLIT
        lp = (parts[:length] + parts[length : 2 * length]) + parts[2 * length :]
        lp_ref2[2 * p] = lp[:, :LANES]
        lp_ref2[2 * p + 1] = lp[:, LANES:]

    m_of = iota(tile, 0) // groups
    ms = SUBLANES // groups

    def plane(zi, carry):
        zg = z_base + zi - HALO
        z_inside = (zg >= 0) & (zg < planes_all)
        for y in range(-HALO, rows + HALO):
            yg = y_base + y
            inside = z_inside & (yg >= 0) & (yg < rows_all)
            scale = jnp.where(inside, INNER[0] * 0.5 * DAMPING, 0.0)
            for part in range(size // SUBLANES):
                values = [
                    lp_ref2[y + LEAD, pl.ds(zi * SPLIT + part * ms + i, 1), :] for i in range(ms)
                ]
                at = slice(part * SUBLANES, (part + 1) * SUBLANES)
                r_ref[zi, y + HALO, at] = scale / (shift[at] + chosen(m_of, values))
        return carry

    lax.fori_loop(0, region_z, plane, 0)


def spread_matrix():
    from_lane = iota((LANES, SPLIT * LANES), 0)
    to_lane = iota((LANES, SPLIT * LANES), 1)
    return one_hot(from_lane % NX == SPLIT * (to_lane % STEPS) + to_lane // LANES)


def place(cells, r_ref, ro_ref, first_ref, then=None):
    fields = first_ref.shape[4]
    packed = jnp.concatenate([parts for _, parts, _, _ in cells], axis=0).astype(jnp.bfloat16)
    values = (START / LAST) * bf16_dot(packed, spread_matrix())
    for number, (orbitals, _, z, y) in enumerate(cells):
        zi, yi = z + HALO, y + HALO
        o = (-2.0 * START * LAST) * orbitals.astype(jnp.float32)
        ro = r_ref[zi, yi] * o
        ro_ref[zi, yi] = ro
        own = [
            values[number * fields : (number + 1) * fields, m * LANES : (m + 1) * LANES]
            for m in range(SPLIT)
        ]
        first_sweep(ro_ref, first_ref, z, y, own)
        if then is not None:
            then(z, y, o * ro, own)


def first_sweep(ro_ref, first_ref, z, y, values):
    groups = first_ref.shape[0]
    zi, yi = z + HALO, y + HALO
    for g in range(groups):
        for m in range(SPLIT):
            at = m * groups + g
            ro = jnp.broadcast_to(ro_ref[zi, yi, at : at + 1], values[m].shape)
            first_ref[g, zi, yi, m] = ro * values[m]


def prepare_kernel(
    parts_ref, own_ref, a_ref, b_ref, r_ref, ro_ref, first_ref, acc_ref, later_ref, w_ref
):
    depth, rows = own_ref.shape[:2]
    fields = first_ref.shape[4]
    size = ro_ref.shape[2]
    groups = size // SPLIT
    pieces = parts_ref.shape[0] // (depth * fields)

    def first_term(z, y, weight, values):
        if not 0 <= y < rows:
            return
        turn = groups // 2
        while turn:
            weight = weight + pltpu.roll(weight, size - turn, 0)
            turn //= 2
        w_ref[y] = (COEFFS[0] / (START * START * LAST)) * weight
        for m in range(SPLIT):
            at = m * groups
            w = jnp.broadcast_to(w_ref[y, at : at + 1], (fields, LANES))
            acc_ref[z, y, m] = w * values[m]

    def plane(z, carry):
        cells = []
        for y in range(-HALO, rows + HALO):
            start = (y + LEAD) // 2 * depth + z
            value = parts_ref[pl.ds(start, fields, stride=pieces * depth), :]
            cells.append((row_tile(own_ref, a_ref, b_ref, z, y), two_parts(value, y), z, y))
        place(cells, r_ref, ro_ref, first_ref, first_term)
        return carry

    lax.fori_loop(0, depth, plane, 0)

    def scaled(z, carry):
        later_ref[z] = (INNER[-1] / INNER[0]) * r_ref[z]
        return carry

    lax.fori_loop(0, r_ref.shape[0], scaled, 0)


def sweep_kernel(
    parts_ref, a_ref, b_ref, r_ref, later_ref, inverse_ref, ro_in, first_in, acc_in,
    out_ref, ro_ref, first_ref, acc_ref, x_ref, y_ref, m_ref,
):
    depth, rows = acc_ref.shape[:2]
    fields = first_ref.shape[4]
    size = ro_ref.shape[2]
    groups = size // SPLIT
    count = groups * BATCH
    even = lax.rem(lax.axis_index("grid"), 2) == 0
    all_cells = list(enumerate(plane_cells(rows)))
    for d in range(1, HALO + 1):
        z_a = jnp.where(even, depth - 1 + d, -d)
        z_b = jnp.where(even, -d, depth - 1 + d)
        cells = []
        for at, (distance, y) in all_cells:
            if distance == d:
                for ref, z in ((a_ref, z_a), (b_ref, z_b)):
                    tile = ref[at].astype(jnp.float32)
                    cells.append((tile[:size], tile[size:], z, y))
        place(cells, r_ref, ro_ref, first_ref)

    step = iota((fields, LANES), 1) % STEPS
    first_k = step == 0
    last_k = step == STEPS - 1

    def group(g, carry):
        buffers = (first_ref.at[g], x_ref, y_ref)
        scales = (r_ref, later_ref)

        def stage(number, z, reach, deep):
            target = buffers[min(number, SWEEPS - 2)]
            source = buffers[number - 1]

            def of_group(ref, i, y, m):
                return jnp.broadcast_to(ref[z + i, y, pl.ds(m * groups + g, 1), :], (fields, LANES))

            def row(i, y):
                return [source[z + i, y, m] for m in range(SPLIT)]

            ys = range(HALO - reach, HALO + rows + reach)
            before = [row(i, ys[0] - 1) for i in range(deep)]
            here = [row(i, ys[0]) for i in range(deep)]
            for y in ys:
                after = [row(i, y + 1) for i in range(deep)]
                under, over = row(-1, y), row(deep, y)
                for i in range(deep):
                    lower = here[i - 1] if i else under
                    upper = here[i + 1] if i + 1 < deep else over
                    mid = here[i]
                    for m in range(SPLIT):
                        if m:
                            left = mid[m - 1]
                        else:
                            left = jnp.where(first_k, 0.0, pltpu.roll(mid[SPLIT - 1], 1, 1))
                        if m + 1 < SPLIT:
                            right = mid[m + 1]
                        else:
                            right = jnp.where(last_k, 0.0, pltpu.roll(mid[0], LANES - 1, 1))
                        near = (before[i][m] + after[i][m]) + (lower[m] + upper[m])
                        near = near + (left + right)
                        if number == SWEEPS - 1:
                            term = of_group(ro_ref, i, y, m) * near
                            acc_ref[z + i - HALO, y - HALO, m] += term
                            continue
                        base = mid[m] if number == 1 else buffers[0][z + i, y, m]
                        target[z + i, y, m] = of_group(scales[number - 1], i, y, m) * near + base
                before, here = here, after

        for number in range(1, SWEEPS):
            reach = HALO - number

            def inner(pair, c, number=number, reach=reach):
                stage(number, HALO + 2 * pair, reach, 2)
                return c

            for d in range(1, reach + 1):
                stage(number, HALO - d, reach - d, 1)
                stage(number, HALO + depth - 1 + d, reach - d, 1)
            lax.fori_loop(0, depth // 2, inner, 0, unroll=2)
        return carry

    lax.fori_loop(0, groups, group, 0)

    lane_in, x_out = iota((SPLIT * LANES, LANES), 0), iota((SPLIT * LANES, LANES), 1) % NX
    gather = one_hot(x_out == SPLIT * (lane_in % STEPS) + lane_in // LANES)
    left = lane_halves((fields, LANES))
    factor = 4.0 / count * -0.5
    planes = []
    for z in range(depth):
        parts = [
            jnp.concatenate([acc_ref[z, y, m] for y in range(rows)], axis=0) for m in range(SPLIT)
        ]
        acc = jnp.concatenate(parts, axis=1)
        upper = acc.astype(jnp.bfloat16)
        lower = (acc - upper.astype(jnp.float32)).astype(jnp.bfloat16)
        total = bf16_dot(upper, gather) + bf16_dot(lower, gather)
        tiles = []
        for y in range(rows):
            tiles.append(total[y * fields : (y + 1) * fields])
        pieces = []
        for y in range(0, rows, 2):
            start = (y + LEAD) // 2 * depth + z
            value = parts_ref[pl.ds(start, fields, stride=parts_ref.shape[0] // fields), :]
            pieces.append(value + factor * jnp.where(left, tiles[y], tiles[y + 1]))
        planes.append(jnp.concatenate(pieces, axis=1))
    stacked = jnp.concatenate(planes, axis=0).astype(jnp.bfloat16)
    all_rows = depth * fields

    pick = one_hot(iota((all_rows, fields), 0) // depth == iota((all_rows, fields), 1))
    tile = one_hot(iota((fields, all_rows), 1) % fields == iota((fields, all_rows), 0))
    wide = bf16_dot(bf16_dot(pick, inverse_ref[...]).astype(jnp.bfloat16), tile)
    square = (all_rows, all_rows)
    same = iota(square, 0) % depth == iota(square, 1) // fields
    wide = jnp.where(same, wide, 0.0).astype(jnp.bfloat16)
    updated = bf16_dot(wide, stacked)

    m_ref[...] = jnp.zeros_like(m_ref)
    gram = jnp.zeros((fields, fields), jnp.float32)
    for z in range(depth):
        one = planes[z].astype(jnp.bfloat16)
        gram = gram + lax.dot_general(
            one, one, (((1,), (1,)), ((), ())), preferred_element_type=jnp.float32
        )
    m_ref[:, :fields] = gram
    pieces = rows * NX // LANES
    for p in range(fields):
        for t in range(pieces):
            out_ref[p, t] = updated[p * depth : (p + 1) * depth, t * LANES : (t + 1) * LANES]
        out_ref[p, pieces] = jnp.broadcast_to(m_ref[p : p + 1, :], (depth, LANES))


VMEM = pl.BlockSpec(memory_space=pltpu.VMEM)
SMEM = pl.BlockSpec(memory_space=pltpu.SMEM)
ANY = pl.BlockSpec(memory_space=pl.ANY)


def in_vmem(*arrays):
    return [pltpu.with_memory_space_constraint(array, pltpu.VMEM) for array in arrays]


def in_hbm(array):
    return pltpu.with_memory_space_constraint(array, pltpu.HBM)


def swapped(to_a, to_b, axis):
    count = lax.axis_size(axis)
    pairs_a = [(i, i ^ 1) for i in range(count)]
    pairs_b = [(i, i + 1 if i % 2 else i - 1) for i in range(1, count - 1)]
    got_a = lax.ppermute(to_a, axis, pairs_a)
    got_b = lax.ppermute(to_b, axis, pairs_b)
    return got_a, got_b


def rows_plan(potentials, orbitals, energies, local_potential, inverse_factor):
    pots = lax.axis_size("pot")
    grids = lax.axis_size("grid")
    depth = potentials.shape[1]
    count, _, width = orbitals.shape
    rows = width // NX
    fields = pots
    half = count // 2
    f32, bf16 = jnp.float32, jnp.bfloat16
    shape = pltpu.VMEM
    tile = (half + fields, LANES)

    region = (depth + 2 * HALO, rows + 2 * HALO)
    pieces = width // LANES
    window = pieces + 2 * (LEAD * NX // LANES)
    limit = pltpu.CompilerParams(vmem_limit_bytes=VMEM_LIMIT)
    call = functools.partial(pl.pallas_call, compiler_params=limit)
    side = len(row_cells(depth))
    fields_tiles = potentials.reshape(depth, pots * pieces, LANES).transpose(1, 0, 2)
    windows, own, to_a, to_b = call(
        first_kernel,
        out_shape=[
            pltpu.HBM((pots, window, depth, LANES), f32),
            shape((depth, rows, half, LANES), bf16),
            shape((side, half, LANES), bf16),
            shape((side, half, LANES), bf16),
        ],
        in_specs=[ANY] * 2,
        out_specs=[ANY] + [VMEM] * 3,
        scratch_shapes=[
            pltpu.VMEM((pots * pieces + window - pieces, depth, LANES), f32),
            pltpu.VMEM(orbitals.shape, bf16),
            pltpu.VMEM((half * rows * depth, LANES), f32),
            pltpu.SemaphoreType.DMA((2 + pots,)),
        ],
        name="first",
    )(in_hbm(fields_tiles), in_hbm(orbitals))
    got_a, got_b = swapped(to_a, to_b, "pot")
    parts = lax.all_to_all(windows, "pot", 0, 0, tiled=True)
    parts = parts.reshape(pots * window * depth, LANES)

    inverse_diagonal = call(
        diagonal_kernel,
        out_shape=shape(region + (half, LANES), f32),
        in_specs=[SMEM, VMEM],
        out_specs=VMEM,
        scratch_shapes=[pltpu.VMEM((rows + 2 * LEAD, region[0] * SPLIT, LANES), f32)]
        + [pltpu.VMEM((rows // 2 + LEAD, local_potential.shape[0], LANES), f32)] * 3,
        name="diagonal",
    )(energies, local_potential)

    parts, inverse_diagonal = lax.optimization_barrier((parts, inverse_diagonal))
    edge = len(plane_cells(rows))
    up, down = call(
        send_kernel,
        out_shape=[shape((edge,) + tile, bf16)] * 2,
        in_specs=[VMEM] * 4,
        out_specs=[VMEM] * 2,
        name="sends",
    )(*in_vmem(parts, own, got_a, got_b))
    z_a, z_b = swapped(up, down, "grid")

    own_values = [
        shape(region + (half, LANES), f32),
        shape((half // SPLIT,) + region + (SPLIT, fields, LANES), f32),
        shape((depth, rows, SPLIT, fields, LANES), f32),
    ]
    *prepared, later = call(
        prepare_kernel,
        out_shape=own_values + own_values[:1],
        in_specs=[VMEM] * 5,
        out_specs=[VMEM] * 4,
        scratch_shapes=[pltpu.VMEM((rows, half, LANES), f32)],
        name="prepare",
    )(*in_vmem(parts, own, got_a, got_b, inverse_diagonal))
    sent, *_ = call(
        sweep_kernel,
        out_shape=[shape((fields, pieces + 1, depth, LANES), f32)] + own_values,
        in_specs=[VMEM] * 9,
        out_specs=[VMEM] * 4,
        scratch_shapes=[
            pltpu.VMEM(region + (SPLIT, fields, LANES), f32),
            pltpu.VMEM(region + (SPLIT, fields, LANES), f32),
            pltpu.VMEM((fields, LANES), f32),
        ],
        input_output_aliases={6: 1, 7: 2, 8: 3},
        name="sweeps",
    )(*in_vmem(parts, z_a, z_b, inverse_diagonal, later), inverse_factor, *in_vmem(*prepared))

    back = lax.all_to_all(sent, "pot", 0, 0, tiled=True)
    updated = back[:, :pieces].reshape(pots * pieces, depth, LANES).transpose(1, 0, 2)
    updated = updated.reshape(1, depth, pots * width)
    margins = jnp.sum(back[:, pieces], axis=0)
    step = 1
    while step < grids:
        margins = margins + lax.ppermute(margins, "grid", [(i, i ^ step) for i in range(grids)])
        step *= 2
    margins = margins[:1, :fields] / local_potential.size
    return updated, margins


def local(potentials, orbitals, energies, local_potential, inverse_factor):
    pots = lax.axis_size("pot")
    grids = lax.axis_size("grid")
    depth = potentials.shape[1]
    count, _, width = orbitals.shape
    fits = (
        potentials.shape[0] == 1
        and pots == 8
        and width % LANES == 0
        and LANES == 2 * NX
        and width // NX >= HALO
        and depth == 8
        and count % (BATCH * SPLIT) == 0
        and count // BATCH in (2, 4)
        and grids & (grids - 1) == 0
    )
    plan = rows_plan if fits else gathered_plan
    return plan(potentials, orbitals, energies, local_potential, inverse_factor)


def solution(mesh):
    in_specs = (P("pot", "grid", None), P(None, "grid", "pot"), P(), P(), P())
    out_specs = (P("pot", "grid", None), P("pot", None))
    return jax.shard_map(local, mesh=mesh, in_specs=in_specs, out_specs=out_specs, check_vma=False)
```

```python
import functools
import math

import jax
import jax.numpy as jnp
from jax import lax
from jax.experimental import pallas as pl
from jax.experimental.pallas import tpu as pltpu
from jax.sharding import PartitionSpec as P


NX = 64
SWEEPS = 4
DAMPING = 0.8
COEFFS = tuple(
    sum(math.comb(n, m) * (1.0 - DAMPING) ** (n - m) for n in range(m, SWEEPS))
    for m in range(SWEEPS)
)
START = COEFFS[SWEEPS - 2]
WEIGHTS = [COEFFS[SWEEPS - 2 - n] / START for n in range(SWEEPS - 2)]
INNER = tuple(
    ((1.0 / START) if n == 0 else WEIGHTS[n - 1]) / WEIGHTS[n] for n in range(SWEEPS - 2)
)
LAST = WEIGHTS[-1]
assert SWEEPS == 4
HALO = SWEEPS - 1
LEAD = HALO + HALO % 2
LANES = 128
SUBLANES = 8
VMEM_LIMIT = 8 << 20


def padded_2(block, sides, width):
    for axis, dim in sides:
        count = lax.axis_size(axis)
        forward = [(i, i + 1) for i in range(count - 1)]
        backward = [(target, source) for source, target in forward]
        low = lax.ppermute(
            lax.slice_in_dim(block, block.shape[dim] - width, None, axis=dim), axis, forward
        )
        high = lax.ppermute(lax.slice_in_dim(block, 0, width, axis=dim), axis, backward)
        block = jnp.concatenate([low, block, high], axis=dim)
    return block


def plane_neighbours(field, row_width):
    plane_size = field.shape[-1]
    widths = [(0, 0)] * (field.ndim - 1)
    padded = jnp.pad(field, widths + [(row_width, row_width)])
    along_y = padded[..., 2 * row_width :] + padded[..., :plane_size]
    column = jnp.arange(plane_size, dtype=jnp.int32) % row_width
    padded = jnp.pad(field, widths + [(1, 1)])
    right_side = jnp.where(column == row_width - 1, 0.0, padded[..., 2:])
    left_side = jnp.where(column == 0, 0.0, padded[..., :plane_size])
    return along_y + right_side + left_side


def across_slabs(answer):
    padded = padded_2(answer, (("grid", 2),), 1)
    return padded[:, :, 2:] + padded[:, :, :-2]


def absorb(orbital_block, energy_block, fields, local_here, along_planes):
    orbital = orbital_block.astype(jnp.float32)[:, None]
    diagonal = (3.0 + local_here[None] - energy_block[:, None, None])[:, None]
    source = -orbital * fields[None]
    answer = DAMPING * source / diagonal
    for _ in range(SWEEPS - 1):
        nearby = along_planes(answer) + plane_neighbours(answer, NX)
        answer = answer + DAMPING * (source - diagonal * answer + 0.5 * nearby) / diagonal
    return jnp.sum(orbital * answer, axis=0)


def gathered_plan(potentials, orbitals, energies, local_potential, inverse_factor):
    slab_depth = potentials.shape[1]
    count = orbitals.shape[0]
    cells = local_potential.size
    grid_index = lax.axis_index("grid")
    local_here = lax.dynamic_slice_in_dim(local_potential, grid_index * slab_depth, slab_depth, 0)
    blocks = 4 if count % 4 == 0 else 1
    block_size = count // blocks
    response = jnp.zeros(potentials.shape, jnp.float32)
    for number in range(blocks):
        orbital_block = orbitals[number * block_size : (number + 1) * block_size]
        gathered = lax.all_gather(orbital_block, "pot", axis=2, tiled=True)
        energy_block = energies[number * block_size : (number + 1) * block_size]
        response = response + absorb(gathered, energy_block, potentials, local_here, across_slabs)
    trial_block = (potentials + 4.0 / count * response).astype(jnp.bfloat16)
    by_cells = lax.all_to_all(trial_block, "pot", split_axis=2, concat_axis=0, tiled=True)
    row_count = by_cells.shape[0]
    flattened = by_cells.reshape(row_count, -1)
    partial_margins = lax.dot_general(
        flattened, flattened, (((1,), (1,)), ((), ())), preferred_element_type=jnp.float32
    )
    combined = jnp.dot(inverse_factor, flattened, preferred_element_type=jnp.float32).reshape(
        by_cells.shape
    )
    updated = lax.all_to_all(combined, "pot", split_axis=0, concat_axis=2, tiled=True)
    scattered = lax.psum_scatter(partial_margins, "pot", scatter_dimension=0, tiled=True)
    own_rows = lax.psum(scattered, "grid")
    margins = own_rows / cells
    return (updated, margins)


def row_cells(depth):
    return [(d, z) for d in range(1, HALO + 1) for z in range(depth)]


def plane_cells(rows):
    return [(d, y) for d in range(1, HALO + 1) for y in range(d - HALO, rows + HALO - d)]


def iota(shape, dim):
    return lax.broadcasted_iota(jnp.int32, shape, dim)


def bf16_dot(a, b):
    return jnp.dot(a, b, preferred_element_type=jnp.float32)


def one_hot(mask):
    return mask.astype(jnp.float32).astype(jnp.bfloat16)


def lane_halves(shape):
    return iota(shape, len(shape) - 1) < NX


SPLIT = 4
STEPS = NX // SPLIT
BATCH = LANES // STEPS


def first_kernel(
    fields_ref, orbitals_ref, windows_ref, own_ref, a_ref, b_ref,
    wide_ref, outer_ref, orb_ref, s_ref, sem_ref,
):
    receivers, window = windows_ref.shape[:2]
    total = fields_ref.shape[0]
    ahead = LEAD * NX // LANES
    fetch = pltpu.make_async_copy(fields_ref, wide_ref.at[pl.ds(ahead, total)], sem_ref.at[0])
    fetch_orbitals = pltpu.make_async_copy(orbitals_ref, orb_ref, sem_ref.at[1])
    fetch.start()
    fetch_orbitals.start()
    for t in range(ahead):
        wide_ref[t] = jnp.zeros(wide_ref.shape[1:], wide_ref.dtype)
        wide_ref[ahead + total + t] = jnp.zeros(wide_ref.shape[1:], wide_ref.dtype)
    fetch.wait()
    copies = []
    for p in range(receivers):
        at = p * (total // receivers)
        left = lane_halves(outer_ref.shape[1:])
        outer_ref[p] = jnp.where(left, wide_ref[at + window], wide_ref[at])
        inner = wide_ref.at[pl.ds(at + 1, window - 1)]
        for source, target in (
            (outer_ref.at[pl.ds(p, 1)], windows_ref.at[p, pl.ds(0, 1)]),
            (inner, windows_ref.at[p, pl.ds(1, window - 1)]),
        ):
            copies.append(pltpu.make_async_copy(source, target, sem_ref.at[2 + len(copies)]))
    for copy in copies:
        copy.start()
    fetch_orbitals.wait()
    relayout(orb_ref, own_ref, a_ref, b_ref, s_ref)
    for copy in copies:
        copy.wait()


def relayout(orb_ref, own_ref, a_ref, b_ref, s_ref):
    count, depth, width = orb_ref.shape
    groups = count // BATCH
    rows = width // NX
    lane_in, lane_out = iota((LANES, LANES), 0), iota((LANES, LANES), 1)
    wanted = (lane_out // NX) * NX + SPLIT * (lane_out % STEPS) + lane_out // STEPS % SPLIT
    permute = one_hot(lane_in == wanted)
    lane = iota((depth, LANES), 1) // STEPS
    for t in range(width // LANES):
        lanes = slice(t * LANES, (t + 1) * LANES)
        tile = orb_ref[:, :, lanes].astype(jnp.float32).reshape(count * depth, LANES)
        tile = bf16_dot(tile.astype(jnp.bfloat16), permute)
        for g in range(groups):
            first = g * BATCH * depth
            regs = [tile[first + b * depth : first + (b + 1) * depth] for b in range(BATCH)]
            step = BATCH // 2
            while step:
                stays = lane // step % 2 == 0
                for b in range(BATCH):
                    if b & step == 0:
                        lo, hi = regs[b], regs[b + step]
                        regs[b] = jnp.where(stays, lo, pltpu.roll(hi, step * STEPS, 1))
                        regs[b + step] = jnp.where(
                            stays, pltpu.roll(lo, LANES - step * STEPS, 1), hi
                        )
                step //= 2
            for c in range(BATCH):
                y, m = 2 * t + c // SPLIT, c % SPLIT
                at = ((m * groups + g) * rows + y) * depth
                s_ref[at : at + depth] = regs[c]
    for z in range(depth):
        for y in range(rows):
            tile = s_ref[pl.ds(y * depth + z, SPLIT * groups, stride=rows * depth), :]
            own_ref[z, y] = tile.astype(jnp.bfloat16)
    even = lax.rem(lax.axis_index("pot"), 2) == 0
    for at, (d, z) in enumerate(row_cells(depth)):
        a_ref[at] = own_ref[z, jnp.where(even, rows - d, d - 1)]
        b_ref[at] = own_ref[z, jnp.where(even, d - 1, rows - d)]


def of_fields(parts_ref, fields, depth, z, y):
    pieces = parts_ref.shape[0] // (fields * depth)
    start = (y + LEAD) // 2 % pieces * depth + z
    return parts_ref[pl.ds(start, fields, stride=pieces * depth), :]


def two_parts(value, y):
    left = lane_halves(value.shape)
    upper = value.astype(jnp.bfloat16).astype(jnp.float32)
    lower = value - upper
    if y % 2:
        return jnp.where(left, pltpu.roll(upper, NX, 1), lower)
    return jnp.where(left, upper, pltpu.roll(lower, NX, 1))


def row_tile(own_ref, a_ref, b_ref, z, y):
    depth, rows = own_ref.shape[:2]
    even = lax.rem(lax.axis_index("pot"), 2) == 0
    if 0 <= y < rows:
        return own_ref[z, y]
    at = (-y - 1 if y < 0 else y - rows) * depth + z
    a, b = a_ref[at].astype(jnp.float32), b_ref[at].astype(jnp.float32)
    return jnp.where(even == (y < 0), b, a).astype(jnp.bfloat16)


def send_kernel(v_ref, own_ref, a_ref, b_ref, to_a_ref, to_b_ref):
    depth, rows = own_ref.shape[:2]
    fields = lax.axis_size("pot")
    even = lax.rem(lax.axis_index("grid"), 2) == 0

    def tile_of(z, y):
        value = of_fields(v_ref, fields, depth, z, y)
        orbitals = row_tile(own_ref, a_ref, b_ref, z, y).astype(jnp.float32)
        return jnp.concatenate([orbitals, two_parts(value, y)], axis=0)

    for at, (d, y) in enumerate(plane_cells(rows)):
        top, bottom = tile_of(depth - d, y), tile_of(d - 1, y)
        to_a_ref[at] = jnp.where(even, top, bottom).astype(jnp.bfloat16)
        to_b_ref[at] = jnp.where(even, bottom, top).astype(jnp.bfloat16)


def diagonal_kernel(energy_ref, lp_ref, r_ref, lp_ref2, *part_refs):
    planes_all, plane_cells = lp_ref.shape
    rows_all = plane_cells // NX
    region_z, region_y, size, _ = r_ref.shape
    depth, rows = region_z - 2 * HALO, region_y - 2 * HALO
    groups = size // SPLIT
    z_base = lax.axis_index("grid") * depth
    y_base = lax.axis_index("pot") * rows

    shift = jnp.zeros((size, LANES), jnp.float32)
    group_of = iota((size, LANES), 0) % groups
    member = iota((size, LANES), 1) // STEPS
    for g in range(groups):
        for b in range(BATCH):
            here = (group_of == g) & (member == b)
            shift = jnp.where(here, 3.0 - energy_ref[g * BATCH + b], shift)

    pairs = part_refs[0].shape[0]
    for p in range(pairs):
        at = jnp.clip((y_base - LEAD) // 2 + p, 0, rows_all // 2 - 1) * LANES
        rest = lp_ref[:, pl.ds(pl.multiple_of(at, LANES), LANES)]
        for part_ref in part_refs:
            part = rest.astype(jnp.bfloat16).astype(jnp.float32)
            part_ref[p] = part
            rest = rest - part
    from_lane, to_lane = iota((LANES, 2 * LANES), 0), iota((LANES, 2 * LANES), 1)
    pick = one_hot(
        (from_lane // NX == to_lane // LANES) & (from_lane % NX // SPLIT == to_lane % STEPS)
    )
    tile = (SUBLANES, LANES)
    keep = iota(tile, 1) % SPLIT == iota(tile, 0) % SPLIT
    per_tile = SUBLANES // SPLIT
    plane_of = iota(tile, 0) // SPLIT

    def clipped(zi):
        return jnp.clip(z_base + zi - HALO, 0, planes_all - 1)

    def chosen(index, values):
        out = jnp.broadcast_to(values[0], tile)
        for number, value in enumerate(values[1:], 1):
            out = jnp.where(index == number, jnp.broadcast_to(value, tile), out)
        return out

    for p in range(pairs):
        stacked = []
        for ref in part_refs:
            for zi in range(0, region_z, per_tile):
                values = [ref[p, pl.ds(clipped(zi + i), 1), :] for i in range(per_tile)]
                stacked.append(jnp.where(keep, chosen(plane_of, values), 0.0))
        parts = bf16_dot(jnp.concatenate(stacked, axis=0).astype(jnp.bfloat16), pick)
        length = region_z * SPLIT
        lp = (parts[:length] + parts[length : 2 * length]) + parts[2 * length :]
        lp_ref2[2 * p] = lp[:, :LANES]
        lp_ref2[2 * p + 1] = lp[:, LANES:]

    m_of = iota(tile, 0) // groups
    ms = SUBLANES // groups

    def plane(zi, carry):
        zg = z_base + zi - HALO
        z_inside = (zg >= 0) & (zg < planes_all)
        for y in range(-HALO, rows + HALO):
            yg = y_base + y
            inside = z_inside & (yg >= 0) & (yg < rows_all)
            scale = jnp.where(inside, INNER[0] * 0.5 * DAMPING, 0.0)
            for part in range(size // SUBLANES):
                values = [
                    lp_ref2[y + LEAD, pl.ds(zi * SPLIT + part * ms + i, 1), :] for i in range(ms)
                ]
                at = slice(part * SUBLANES, (part + 1) * SUBLANES)
                r_ref[zi, y + HALO, at] = scale / (shift[at] + chosen(m_of, values))
        return carry

    lax.fori_loop(0, region_z, plane, 0)


def spread_matrix():
    from_lane = iota((LANES, SPLIT * LANES), 0)
    to_lane = iota((LANES, SPLIT * LANES), 1)
    return one_hot(from_lane % NX == SPLIT * (to_lane % STEPS) + to_lane // LANES)


def place(cells, r_ref, ro_ref, first_ref, then=None):
    fields = first_ref.shape[4]
    packed = jnp.concatenate([parts for _, parts, _, _ in cells], axis=0).astype(jnp.bfloat16)
    values = (START / LAST) * bf16_dot(packed, spread_matrix())
    for number, (orbitals, _, z, y) in enumerate(cells):
        zi, yi = z + HALO, y + HALO
        o = (-2.0 * START * LAST) * orbitals.astype(jnp.float32)
        ro = r_ref[zi, yi] * o
        ro_ref[zi, yi] = ro
        own = [
            values[number * fields : (number + 1) * fields, m * LANES : (m + 1) * LANES]
            for m in range(SPLIT)
        ]
        first_sweep(ro_ref, first_ref, z, y, own)
        if then is not None:
            then(z, y, o * ro, own)


def sweep(number, g, z, reaches, rows, scale_ref, first_ref, source_ref, target_ref):
    groups, fields = first_ref.shape[0], first_ref.shape[4]
    deep = len(reaches)
    before_number = number - 1
    last = number == SWEEPS - 1
    step = iota((fields, LANES), 1) % STEPS
    first_k = step == 0
    last_k = step == STEPS - 1

    def row(i, y):
        return [source_ref[g, z + i - before_number, y - before_number, m] for m in range(SPLIT)]

    most = max(reaches)
    ys = range(HALO - most, HALO + rows + most)
    before = [row(i, ys[0] - 1) for i in range(deep)]
    here = [row(i, ys[0]) for i in range(deep)]
    for y in ys:
        after = [row(i, y + 1) for i in range(deep)]
        under, over = row(-1, y), row(deep, y)
        for i in range(deep):
            if not -reaches[i] <= y - HALO < rows + reaches[i]:
                continue
            lower = here[i - 1] if i else under
            upper = here[i + 1] if i + 1 < deep else over
            mid = here[i]
            for m in range(SPLIT):
                if m:
                    left = mid[m - 1]
                else:
                    left = jnp.where(first_k, 0.0, pltpu.roll(mid[SPLIT - 1], 1, 1))
                if m + 1 < SPLIT:
                    right = mid[m + 1]
                else:
                    right = jnp.where(last_k, 0.0, pltpu.roll(mid[0], LANES - 1, 1))
                near = (before[i][m] + after[i][m]) + (lower[m] + upper[m])
                near = near + (left + right)
                scale = scale_ref[z + i, y, pl.ds(m * groups + g, 1), :]
                near = jnp.broadcast_to(scale, (fields, LANES)) * near
                if last:
                    target_ref[z + i - HALO, y - HALO, m] += near
                else:
                    base = mid[m] if number == 1 else first_ref[g, z + i, y, m]
                    target_ref[g, z + i - number, y - number, m] = near + base
        before, here = here, after


def first_sweep(ro_ref, first_ref, z, y, values):
    groups = first_ref.shape[0]
    zi, yi = z + HALO, y + HALO
    for g in range(groups):
        for m in range(SPLIT):
            at = m * groups + g
            ro = jnp.broadcast_to(ro_ref[zi, yi, at : at + 1], values[m].shape)
            first_ref[g, zi, yi, m] = ro * values[m]


def prepare_kernel(
    parts_ref, own_ref, a_ref, b_ref, r_ref, inverse_ref,
    ro_ref, first_ref, x_ref, y_ref, acc_ref, later_ref, wide_ref, w_ref,
):
    depth, rows = own_ref.shape[:2]
    fields = first_ref.shape[4]
    size = ro_ref.shape[2]
    groups = size // SPLIT

    def first_term(z, y, weight, values):
        if not 0 <= y < rows:
            return
        turn = groups // 2
        while turn:
            weight = weight + pltpu.roll(weight, size - turn, 0)
            turn //= 2
        w_ref[y] = (COEFFS[0] / (START * START * LAST)) * weight
        for m in range(SPLIT):
            at = m * groups
            w = jnp.broadcast_to(w_ref[y, at : at + 1], (fields, LANES))
            acc_ref[z, y, m] = w * values[m]

    def plane(z, carry):
        cells = []
        for y in range(-HALO, rows + HALO):
            value = of_fields(parts_ref, fields, depth, z, y)
            cells.append((row_tile(own_ref, a_ref, b_ref, z, y), two_parts(value, y), z, y))
        place(cells, r_ref, ro_ref, first_ref, first_term)
        return carry

    lax.fori_loop(0, depth, plane, 0)

    def scaled(z, carry):
        later_ref[z] = (INNER[-1] / INNER[0]) * r_ref[z]
        return carry

    lax.fori_loop(0, r_ref.shape[0], scaled, 0)

    all_rows = depth * fields

    pick = one_hot(iota((all_rows, fields), 0) // depth == iota((all_rows, fields), 1))
    tile = one_hot(iota((fields, all_rows), 1) % fields == iota((fields, all_rows), 0))
    wide = bf16_dot(bf16_dot(pick, inverse_ref[...]).astype(jnp.bfloat16), tile)
    square = (all_rows, all_rows)
    same = iota(square, 0) % depth == iota(square, 1) // fields
    wide_ref[...] = jnp.where(same, wide, 0.0).astype(jnp.bfloat16)

    def group(g, carry):
        for z in range(1, depth - 1, 2):
            sweep(1, g, HALO + z, (HALO - 1,) * 2, rows, r_ref, first_ref, first_ref, x_ref)
        for z in range(2, depth - 2, 2):
            sweep(2, g, HALO + z, (HALO - 2,) * 2, rows, later_ref, first_ref, x_ref, y_ref)
        return carry

    lax.fori_loop(0, groups, group, 0)


def sweep_kernel(
    parts_ref, a_ref, b_ref, r_ref, later_ref, wide_ref, ro_in, first_in, x_in, y_in, acc_in,
    out_ref, ro_ref, first_ref, x_ref, y_ref, acc_ref, m_ref,
):
    depth, rows = acc_ref.shape[:2]
    fields = first_ref.shape[4]
    size = ro_ref.shape[2]
    groups = size // SPLIT
    count = groups * BATCH
    even = lax.rem(lax.axis_index("grid"), 2) == 0
    all_cells = list(enumerate(plane_cells(rows)))
    for d in range(1, HALO + 1):
        z_a = jnp.where(even, depth - 1 + d, -d)
        z_b = jnp.where(even, -d, depth - 1 + d)
        cells = []
        for at, (distance, y) in all_cells:
            if distance == d:
                for ref, z in ((a_ref, z_a), (b_ref, z_b)):
                    tile = ref[at].astype(jnp.float32)
                    cells.append((tile[:size], tile[size:], z, y))
        place(cells, r_ref, ro_ref, first_ref)

    top = HALO + depth

    def group(g, carry):
        for z, reaches in (
            (HALO - 2, (0,)),
            (HALO - 1, (1, 2)),
            (top - 1, (2, 1)),
            (top + 1, (0,)),
        ):
            sweep(1, g, z, reaches, rows, r_ref, first_ref, first_ref, x_ref)
        for z, reaches in ((HALO - 1, (0,)), (HALO, (1, 1)), (top - 2, (1, 1)), (top, (0,))):
            sweep(2, g, z, reaches, rows, later_ref, first_ref, x_ref, y_ref)

        def inner(pair, c):
            sweep(3, g, HALO + 2 * pair, (0, 0), rows, ro_ref, first_ref, y_ref, acc_ref)
            return c

        lax.fori_loop(0, depth // 2, inner, 0, unroll=2)
        return carry

    lax.fori_loop(0, groups, group, 0)

    lane_in, x_out = iota((SPLIT * LANES, LANES), 0), iota((SPLIT * LANES, LANES), 1) % NX
    gather = one_hot(x_out == SPLIT * (lane_in % STEPS) + lane_in // LANES)
    left = lane_halves((fields, LANES))
    factor = 4.0 / count * -0.5
    planes = []
    for z in range(depth):
        parts = [
            jnp.concatenate([acc_ref[z, y, m] for y in range(rows)], axis=0) for m in range(SPLIT)
        ]
        acc = jnp.concatenate(parts, axis=1)
        upper = acc.astype(jnp.bfloat16)
        lower = (acc - upper.astype(jnp.float32)).astype(jnp.bfloat16)
        total = bf16_dot(upper, gather) + bf16_dot(lower, gather)
        tiles = []
        for y in range(rows):
            tiles.append(total[y * fields : (y + 1) * fields])
        pieces = []
        for y in range(0, rows, 2):
            value = of_fields(parts_ref, fields, depth, z, y)
            pieces.append(value + factor * jnp.where(left, tiles[y], tiles[y + 1]))
        planes.append(jnp.concatenate(pieces, axis=1))
    stacked = jnp.concatenate(planes, axis=0).astype(jnp.bfloat16)
    updated = bf16_dot(wide_ref[...], stacked)

    m_ref[...] = jnp.zeros_like(m_ref)
    gram = jnp.zeros((fields, fields), jnp.float32)
    for z in range(depth):
        one = planes[z].astype(jnp.bfloat16)
        gram = gram + lax.dot_general(
            one, one, (((1,), (1,)), ((), ())), preferred_element_type=jnp.float32
        )
    m_ref[:, :fields] = gram
    pieces = rows * NX // LANES
    for p in range(fields):
        for t in range(pieces):
            out_ref[p, t] = updated[p * depth : (p + 1) * depth, t * LANES : (t + 1) * LANES]
        out_ref[p, pieces] = jnp.broadcast_to(m_ref[p : p + 1, :], (depth, LANES))


VMEM = pl.BlockSpec(memory_space=pltpu.VMEM)
SMEM = pl.BlockSpec(memory_space=pltpu.SMEM)
ANY = pl.BlockSpec(memory_space=pl.ANY)


def in_vmem(*arrays):
    return [pltpu.with_memory_space_constraint(array, pltpu.VMEM) for array in arrays]


def in_hbm(array):
    return pltpu.with_memory_space_constraint(array, pltpu.HBM)


def swapped(to_a, to_b, axis):
    count = lax.axis_size(axis)
    pairs_a = [(i, i ^ 1) for i in range(count)]
    pairs_b = [(i, i + 1 if i % 2 else i - 1) for i in range(1, count - 1)]
    got_a = lax.ppermute(to_a, axis, pairs_a)
    got_b = lax.ppermute(to_b, axis, pairs_b)
    return got_a, got_b


def rows_plan(potentials, orbitals, energies, local_potential, inverse_factor):
    pots = lax.axis_size("pot")
    grids = lax.axis_size("grid")
    depth = potentials.shape[1]
    count, _, width = orbitals.shape
    rows = width // NX
    fields = pots
    half = count // 2
    f32, bf16 = jnp.float32, jnp.bfloat16
    shape = pltpu.VMEM
    tile = (half + fields, LANES)

    region = (depth + 2 * HALO, rows + 2 * HALO)
    pieces = width // LANES
    window = pieces + 2 * (LEAD * NX // LANES) - 1
    limit = pltpu.CompilerParams(vmem_limit_bytes=VMEM_LIMIT)
    call = functools.partial(pl.pallas_call, compiler_params=limit)
    side = len(row_cells(depth))
    fields_tiles = potentials.reshape(depth, pots * pieces, LANES).transpose(1, 0, 2)
    windows, own, to_a, to_b = call(
        first_kernel,
        out_shape=[
            pltpu.HBM((pots, window, depth, LANES), f32),
            shape((depth, rows, half, LANES), bf16),
            shape((side, half, LANES), bf16),
            shape((side, half, LANES), bf16),
        ],
        in_specs=[ANY] * 2,
        out_specs=[ANY] + [VMEM] * 3,
        scratch_shapes=[
            pltpu.VMEM((pots * pieces + window + 1 - pieces, depth, LANES), f32),
            pltpu.VMEM((pots, depth, LANES), f32),
            pltpu.VMEM(orbitals.shape, bf16),
            pltpu.VMEM((half * rows * depth, LANES), f32),
            pltpu.SemaphoreType.DMA((2 + 2 * pots,)),
        ],
        name="first",
    )(in_hbm(fields_tiles), in_hbm(orbitals))
    got_a, got_b = swapped(to_a, to_b, "pot")
    parts = lax.all_to_all(windows, "pot", 0, 0, tiled=True)
    parts = parts.reshape(pots * window * depth, LANES)

    inverse_diagonal = call(
        diagonal_kernel,
        out_shape=shape(region + (half, LANES), f32),
        in_specs=[SMEM, VMEM],
        out_specs=VMEM,
        scratch_shapes=[pltpu.VMEM((rows + 2 * LEAD, region[0] * SPLIT, LANES), f32)]
        + [pltpu.VMEM((rows // 2 + LEAD, local_potential.shape[0], LANES), f32)] * 3,
        name="diagonal",
    )(energies, local_potential)

    parts, inverse_diagonal = lax.optimization_barrier((parts, inverse_diagonal))
    edge = len(plane_cells(rows))
    up, down = call(
        send_kernel,
        out_shape=[shape((edge,) + tile, bf16)] * 2,
        in_specs=[VMEM] * 4,
        out_specs=[VMEM] * 2,
        name="sends",
    )(*in_vmem(parts, own, got_a, got_b))
    z_a, z_b = swapped(up, down, "grid")

    own_values = [
        shape(region + (half, LANES), f32),
        *(
            shape((half // SPLIT, region[0] - 2 * n, region[1] - 2 * n, SPLIT, fields, LANES), f32)
            for n in range(SWEEPS - 1)
        ),
        shape((depth, rows, SPLIT, fields, LANES), f32),
    ]
    *prepared, later, wide = call(
        prepare_kernel,
        out_shape=own_values + own_values[:1] + [shape((depth * fields,) * 2, bf16)],
        in_specs=[VMEM] * 6,
        out_specs=[VMEM] * 7,
        scratch_shapes=[pltpu.VMEM((rows, half, LANES), f32)],
        name="prepare",
    )(*in_vmem(parts, own, got_a, got_b, inverse_diagonal), in_hbm(inverse_factor))
    sent, *_ = call(
        sweep_kernel,
        out_shape=[shape((fields, pieces + 1, depth, LANES), f32)] + own_values,
        in_specs=[VMEM] * 11,
        out_specs=[VMEM] * 6,
        scratch_shapes=[pltpu.VMEM((fields, LANES), f32)],
        input_output_aliases={6 + i: 1 + i for i in range(5)},
        name="sweeps",
    )(*in_vmem(parts, z_a, z_b, inverse_diagonal, later, wide, *prepared))

    back = lax.all_to_all(sent, "pot", 0, 0, tiled=True)
    updated = back[:, :pieces].reshape(pots * pieces, depth, LANES).transpose(1, 0, 2)
    updated = updated.reshape(1, depth, pots * width)
    margins = jnp.sum(back[:, pieces], axis=0)
    step = 1
    while step < grids:
        margins = margins + lax.ppermute(margins, "grid", [(i, i ^ step) for i in range(grids)])
        step *= 2
    margins = margins[:1, :fields] / local_potential.size
    return updated, margins


def local(potentials, orbitals, energies, local_potential, inverse_factor):
    pots = lax.axis_size("pot")
    grids = lax.axis_size("grid")
    depth = potentials.shape[1]
    count, _, width = orbitals.shape
    fits = (
        potentials.shape[0] == 1
        and pots == 8
        and width % LANES == 0
        and LANES == 2 * NX
        and width // NX >= HALO
        and depth == 8
        and count % (BATCH * SPLIT) == 0
        and count // BATCH in (2, 4)
        and grids & (grids - 1) == 0
    )
    plan = rows_plan if fits else gathered_plan
    return plan(potentials, orbitals, energies, local_potential, inverse_factor)


def solution(mesh):
    in_specs = (P("pot", "grid", None), P(None, "grid", "pot"), P(), P(), P())
    out_specs = (P("pot", "grid", None), P("pot", None))
    return jax.shard_map(local, mesh=mesh, in_specs=in_specs, out_specs=out_specs, check_vma=False)
```

```python
import functools
import math

import jax
import jax.numpy as jnp
from jax import lax
from jax.experimental import pallas as pl
from jax.experimental.pallas import tpu as pltpu
from jax.sharding import PartitionSpec as P


NX = 64
SWEEPS = 4
DAMPING = 0.8
COEFFS = tuple(
    sum(math.comb(n, m) * (1.0 - DAMPING) ** (n - m) for n in range(m, SWEEPS))
    for m in range(SWEEPS)
)
START = COEFFS[SWEEPS - 2]
WEIGHTS = [COEFFS[SWEEPS - 2 - n] / START for n in range(SWEEPS - 2)]
INNER = tuple(
    ((1.0 / START) if n == 0 else WEIGHTS[n - 1]) / WEIGHTS[n] for n in range(SWEEPS - 2)
)
LAST = WEIGHTS[-1]
assert SWEEPS == 4
HALO = SWEEPS - 1
LEAD = HALO + HALO % 2
LANES = 128
SUBLANES = 8
VMEM_LIMIT = 8 << 20


def padded_2(block, sides, width):
    for axis, dim in sides:
        count = lax.axis_size(axis)
        forward = [(i, i + 1) for i in range(count - 1)]
        backward = [(target, source) for source, target in forward]
        low = lax.ppermute(
            lax.slice_in_dim(block, block.shape[dim] - width, None, axis=dim), axis, forward
        )
        high = lax.ppermute(lax.slice_in_dim(block, 0, width, axis=dim), axis, backward)
        block = jnp.concatenate([low, block, high], axis=dim)
    return block


def plane_neighbours(field, row_width):
    plane_size = field.shape[-1]
    widths = [(0, 0)] * (field.ndim - 1)
    padded = jnp.pad(field, widths + [(row_width, row_width)])
    along_y = padded[..., 2 * row_width :] + padded[..., :plane_size]
    column = jnp.arange(plane_size, dtype=jnp.int32) % row_width
    padded = jnp.pad(field, widths + [(1, 1)])
    right_side = jnp.where(column == row_width - 1, 0.0, padded[..., 2:])
    left_side = jnp.where(column == 0, 0.0, padded[..., :plane_size])
    return along_y + right_side + left_side


def across_slabs(answer):
    padded = padded_2(answer, (("grid", 2),), 1)
    return padded[:, :, 2:] + padded[:, :, :-2]


def absorb(orbital_block, energy_block, fields, local_here, along_planes):
    orbital = orbital_block.astype(jnp.float32)[:, None]
    diagonal = (3.0 + local_here[None] - energy_block[:, None, None])[:, None]
    source = -orbital * fields[None]
    answer = DAMPING * source / diagonal
    for _ in range(SWEEPS - 1):
        nearby = along_planes(answer) + plane_neighbours(answer, NX)
        answer = answer + DAMPING * (source - diagonal * answer + 0.5 * nearby) / diagonal
    return jnp.sum(orbital * answer, axis=0)


def gathered_plan(potentials, orbitals, energies, local_potential, inverse_factor):
    slab_depth = potentials.shape[1]
    count = orbitals.shape[0]
    cells = local_potential.size
    grid_index = lax.axis_index("grid")
    local_here = lax.dynamic_slice_in_dim(local_potential, grid_index * slab_depth, slab_depth, 0)
    blocks = 4 if count % 4 == 0 else 1
    block_size = count // blocks
    response = jnp.zeros(potentials.shape, jnp.float32)
    for number in range(blocks):
        orbital_block = orbitals[number * block_size : (number + 1) * block_size]
        gathered = lax.all_gather(orbital_block, "pot", axis=2, tiled=True)
        energy_block = energies[number * block_size : (number + 1) * block_size]
        response = response + absorb(gathered, energy_block, potentials, local_here, across_slabs)
    trial_block = (potentials + 4.0 / count * response).astype(jnp.bfloat16)
    by_cells = lax.all_to_all(trial_block, "pot", split_axis=2, concat_axis=0, tiled=True)
    row_count = by_cells.shape[0]
    flattened = by_cells.reshape(row_count, -1)
    partial_margins = lax.dot_general(
        flattened, flattened, (((1,), (1,)), ((), ())), preferred_element_type=jnp.float32
    )
    combined = jnp.dot(inverse_factor, flattened, preferred_element_type=jnp.float32).reshape(
        by_cells.shape
    )
    updated = lax.all_to_all(combined, "pot", split_axis=0, concat_axis=2, tiled=True)
    scattered = lax.psum_scatter(partial_margins, "pot", scatter_dimension=0, tiled=True)
    own_rows = lax.psum(scattered, "grid")
    margins = own_rows / cells
    return (updated, margins)


def row_cells(depth):
    return [(d, z) for d in range(1, HALO + 1) for z in range(depth)]


def plane_cells(rows):
    return [(d, y) for d in range(1, HALO + 1) for y in range(d - HALO, rows + HALO - d)]


def iota(shape, dim):
    return lax.broadcasted_iota(jnp.int32, shape, dim)


def bf16_dot(a, b):
    return jnp.dot(a, b, preferred_element_type=jnp.float32)


def one_hot(mask):
    return mask.astype(jnp.float32).astype(jnp.bfloat16)


def lane_halves(shape):
    return iota(shape, len(shape) - 1) < NX


SPLIT = 4
STEPS = NX // SPLIT
BATCH = LANES // STEPS


def first_kernel(
    fields_ref, orbitals_ref, potential_ref, windows_ref, own_ref, a_ref, b_ref, lp_ref,
    wide_ref, outer_ref, orb_ref, s_ref, sem_ref, lp_sem_ref,
):
    receivers, window = windows_ref.shape[:2]
    total = fields_ref.shape[0]
    ahead = LEAD * NX // LANES
    fetch = pltpu.make_async_copy(fields_ref, wide_ref.at[pl.ds(ahead, total)], sem_ref.at[0])
    fetch_orbitals = pltpu.make_async_copy(orbitals_ref, orb_ref, sem_ref.at[1])
    fetch.start()
    fetch_orbitals.start()
    first_pair = (lax.axis_index("pot") * own_ref.shape[1] - LEAD) // 2
    last_pair = potential_ref.shape[1] // LANES - 1
    fetches = []
    for p in range(lp_ref.shape[0]):
        at = pl.multiple_of(jnp.clip(first_pair + p, 0, last_pair) * LANES, LANES)
        source = potential_ref.at[:, pl.ds(at, LANES)]
        fetches.append(pltpu.make_async_copy(source, lp_ref.at[p], lp_sem_ref.at[p]))
    for copy in fetches:
        copy.start()
    for t in range(ahead):
        wide_ref[t] = jnp.zeros(wide_ref.shape[1:], wide_ref.dtype)
        wide_ref[ahead + total + t] = jnp.zeros(wide_ref.shape[1:], wide_ref.dtype)
    fetch.wait()
    copies = []
    for p in range(receivers):
        at = p * (total // receivers)
        left = lane_halves(outer_ref.shape[1:])
        outer_ref[p] = jnp.where(left, wide_ref[at + window], wide_ref[at])
        inner = wide_ref.at[pl.ds(at + 1, window - 1)]
        for source, target in (
            (outer_ref.at[pl.ds(p, 1)], windows_ref.at[p, pl.ds(0, 1)]),
            (inner, windows_ref.at[p, pl.ds(1, window - 1)]),
        ):
            copies.append(pltpu.make_async_copy(source, target, sem_ref.at[2 + len(copies)]))
    for copy in copies:
        copy.start()
    fetch_orbitals.wait()
    relayout(orb_ref, own_ref, a_ref, b_ref, s_ref)
    for copy in fetches + copies:
        copy.wait()


def relayout(orb_ref, own_ref, a_ref, b_ref, s_ref):
    count, depth, width = orb_ref.shape
    groups = count // BATCH
    rows = width // NX
    lane_in, lane_out = iota((LANES, LANES), 0), iota((LANES, LANES), 1)
    wanted = (lane_out // NX) * NX + SPLIT * (lane_out % STEPS) + lane_out // STEPS % SPLIT
    permute = one_hot(lane_in == wanted)
    lane = iota((depth, LANES), 1) // STEPS
    for t in range(width // LANES):
        lanes = slice(t * LANES, (t + 1) * LANES)
        tile = orb_ref[:, :, lanes].astype(jnp.float32).reshape(count * depth, LANES)
        tile = bf16_dot(tile.astype(jnp.bfloat16), permute)
        for g in range(groups):
            first = g * BATCH * depth
            regs = [tile[first + b * depth : first + (b + 1) * depth] for b in range(BATCH)]
            step = BATCH // 2
            while step:
                stays = lane // step % 2 == 0
                for b in range(BATCH):
                    if b & step == 0:
                        lo, hi = regs[b], regs[b + step]
                        regs[b] = jnp.where(stays, lo, pltpu.roll(hi, step * STEPS, 1))
                        regs[b + step] = jnp.where(
                            stays, pltpu.roll(lo, LANES - step * STEPS, 1), hi
                        )
                step //= 2
            for c in range(BATCH):
                y, m = 2 * t + c // SPLIT, c % SPLIT
                at = ((m * groups + g) * rows + y) * depth
                s_ref[at : at + depth] = regs[c]
    for z in range(depth):
        for y in range(rows):
            tile = s_ref[pl.ds(y * depth + z, SPLIT * groups, stride=rows * depth), :]
            own_ref[z, y] = tile.astype(jnp.bfloat16)
    even = lax.rem(lax.axis_index("pot"), 2) == 0
    for at, (d, z) in enumerate(row_cells(depth)):
        a_ref[at] = own_ref[z, jnp.where(even, rows - d, d - 1)]
        b_ref[at] = own_ref[z, jnp.where(even, d - 1, rows - d)]


def of_fields(parts_ref, fields, depth, z, y):
    pieces = parts_ref.shape[0] // (fields * depth)
    start = (y + LEAD) // 2 % pieces * depth + z
    return parts_ref[pl.ds(start, fields, stride=pieces * depth), :]


def two_parts(value, y):
    left = lane_halves(value.shape)
    upper = value.astype(jnp.bfloat16).astype(jnp.float32)
    lower = value - upper
    if y % 2:
        return jnp.where(left, pltpu.roll(upper, NX, 1), lower)
    return jnp.where(left, upper, pltpu.roll(lower, NX, 1))


def row_tile(own_ref, a_ref, b_ref, z, y):
    depth, rows = own_ref.shape[:2]
    even = lax.rem(lax.axis_index("pot"), 2) == 0
    if 0 <= y < rows:
        return own_ref[z, y]
    at = (-y - 1 if y < 0 else y - rows) * depth + z
    a, b = a_ref[at].astype(jnp.float32), b_ref[at].astype(jnp.float32)
    return jnp.where(even == (y < 0), b, a).astype(jnp.bfloat16)


def send_kernel(v_ref, own_ref, a_ref, b_ref, to_a_ref, to_b_ref):
    depth, rows = own_ref.shape[:2]
    fields = lax.axis_size("pot")
    even = lax.rem(lax.axis_index("grid"), 2) == 0

    def tile_of(z, y):
        value = of_fields(v_ref, fields, depth, z, y)
        orbitals = row_tile(own_ref, a_ref, b_ref, z, y).astype(jnp.float32)
        return jnp.concatenate([orbitals, two_parts(value, y)], axis=0)

    for at, (d, y) in enumerate(plane_cells(rows)):
        top, bottom = tile_of(depth - d, y), tile_of(d - 1, y)
        to_a_ref[at] = jnp.where(even, top, bottom).astype(jnp.bfloat16)
        to_b_ref[at] = jnp.where(even, bottom, top).astype(jnp.bfloat16)


def diagonal_kernel(energy_ref, lp_ref, r_ref, lp_ref2, *part_refs):
    pairs, planes_all, _ = lp_ref.shape
    region_z, region_y, size, _ = r_ref.shape
    depth, rows = region_z - 2 * HALO, region_y - 2 * HALO
    groups = size // SPLIT
    z_base = lax.axis_index("grid") * depth
    y_base = lax.axis_index("pot") * rows
    rows_all = lax.axis_size("pot") * rows

    shift = jnp.zeros((size, LANES), jnp.float32)
    group_of = iota((size, LANES), 0) % groups
    member = iota((size, LANES), 1) // STEPS
    for g in range(groups):
        for b in range(BATCH):
            here = (group_of == g) & (member == b)
            shift = jnp.where(here, 3.0 - energy_ref[g * BATCH + b], shift)

    for p in range(pairs):
        rest = lp_ref[p]
        for part_ref in part_refs:
            part = rest.astype(jnp.bfloat16).astype(jnp.float32)
            part_ref[p] = part
            rest = rest - part
    from_lane, to_lane = iota((LANES, 2 * LANES), 0), iota((LANES, 2 * LANES), 1)
    pick = one_hot(
        (from_lane // NX == to_lane // LANES) & (from_lane % NX // SPLIT == to_lane % STEPS)
    )
    tile = (SUBLANES, LANES)
    keep = iota(tile, 1) % SPLIT == iota(tile, 0) % SPLIT
    per_tile = SUBLANES // SPLIT
    plane_of = iota(tile, 0) // SPLIT

    def clipped(zi):
        return jnp.clip(z_base + zi - HALO, 0, planes_all - 1)

    def chosen(index, values):
        out = jnp.broadcast_to(values[0], tile)
        for number, value in enumerate(values[1:], 1):
            out = jnp.where(index == number, jnp.broadcast_to(value, tile), out)
        return out

    for p in range(pairs):
        stacked = []
        for ref in part_refs:
            for zi in range(0, region_z, per_tile):
                values = [ref[p, pl.ds(clipped(zi + i), 1), :] for i in range(per_tile)]
                stacked.append(jnp.where(keep, chosen(plane_of, values), 0.0))
        parts = bf16_dot(jnp.concatenate(stacked, axis=0).astype(jnp.bfloat16), pick)
        length = region_z * SPLIT
        lp = (parts[:length] + parts[length : 2 * length]) + parts[2 * length :]
        lp_ref2[2 * p] = lp[:, :LANES]
        lp_ref2[2 * p + 1] = lp[:, LANES:]

    m_of = iota(tile, 0) // groups
    ms = SUBLANES // groups

    def plane(zi, carry):
        zg = z_base + zi - HALO
        z_inside = (zg >= 0) & (zg < planes_all)
        for y in range(-HALO, rows + HALO):
            yg = y_base + y
            inside = z_inside & (yg >= 0) & (yg < rows_all)
            scale = jnp.where(inside, INNER[0] * 0.5 * DAMPING, 0.0)
            for part in range(size // SUBLANES):
                values = [
                    lp_ref2[y + LEAD, pl.ds(zi * SPLIT + part * ms + i, 1), :] for i in range(ms)
                ]
                at = slice(part * SUBLANES, (part + 1) * SUBLANES)
                r_ref[zi, y + HALO, at] = scale / (shift[at] + chosen(m_of, values))
        return carry

    lax.fori_loop(0, region_z, plane, 0)


def spread_matrix():
    from_lane = iota((LANES, SPLIT * LANES), 0)
    to_lane = iota((LANES, SPLIT * LANES), 1)
    return one_hot(from_lane % NX == SPLIT * (to_lane % STEPS) + to_lane // LANES)


def place(cells, r_ref, ro_ref, first_ref, then=None):
    fields = first_ref.shape[4]
    packed = jnp.concatenate([parts for _, parts, _, _ in cells], axis=0).astype(jnp.bfloat16)
    values = (START / LAST) * bf16_dot(packed, spread_matrix())
    for number, (orbitals, _, z, y) in enumerate(cells):
        zi, yi = z + HALO, y + HALO
        o = (-2.0 * START * LAST) * orbitals.astype(jnp.float32)
        ro = r_ref[zi, yi] * o
        ro_ref[zi, yi] = ro
        own = [
            values[number * fields : (number + 1) * fields, m * LANES : (m + 1) * LANES]
            for m in range(SPLIT)
        ]
        first_sweep(ro_ref, first_ref, z, y, own)
        if then is not None:
            then(z, y, o * ro, own)


def sweep(number, g, z, reaches, rows, scale_ref, first_ref, source_ref, target_ref):
    groups, fields = first_ref.shape[0], first_ref.shape[4]
    deep = len(reaches)
    before_number = number - 1
    last = number == SWEEPS - 1
    step = iota((fields, LANES), 1) % STEPS
    first_k = step == 0
    last_k = step == STEPS - 1

    def row(i, y):
        return [source_ref[g, z + i - before_number, y - before_number, m] for m in range(SPLIT)]

    most = max(reaches)
    ys = range(HALO - most, HALO + rows + most)
    before = [row(i, ys[0] - 1) for i in range(deep)]
    here = [row(i, ys[0]) for i in range(deep)]
    for y in ys:
        after = [row(i, y + 1) for i in range(deep)]
        under, over = row(-1, y), row(deep, y)
        for i in range(deep):
            if not -reaches[i] <= y - HALO < rows + reaches[i]:
                continue
            lower = here[i - 1] if i else under
            upper = here[i + 1] if i + 1 < deep else over
            mid = here[i]
            for m in range(SPLIT):
                if m:
                    left = mid[m - 1]
                else:
                    left = jnp.where(first_k, 0.0, pltpu.roll(mid[SPLIT - 1], 1, 1))
                if m + 1 < SPLIT:
                    right = mid[m + 1]
                else:
                    right = jnp.where(last_k, 0.0, pltpu.roll(mid[0], LANES - 1, 1))
                near = (before[i][m] + after[i][m]) + (lower[m] + upper[m])
                near = near + (left + right)
                scale = scale_ref[z + i, y, pl.ds(m * groups + g, 1), :]
                near = jnp.broadcast_to(scale, (fields, LANES)) * near
                if last:
                    target_ref[z + i - HALO, y - HALO, m] += near
                else:
                    base = mid[m] if number == 1 else first_ref[g, z + i, y, m]
                    target_ref[g, z + i - number, y - number, m] = near + base
        before, here = here, after


def first_sweep(ro_ref, first_ref, z, y, values):
    groups = first_ref.shape[0]
    zi, yi = z + HALO, y + HALO
    for g in range(groups):
        for m in range(SPLIT):
            at = m * groups + g
            ro = jnp.broadcast_to(ro_ref[zi, yi, at : at + 1], values[m].shape)
            first_ref[g, zi, yi, m] = ro * values[m]


def prepare_kernel(
    parts_ref, own_ref, a_ref, b_ref, r_ref, ro_ref, first_ref, acc_ref, later_ref, w_ref
):
    depth, rows = own_ref.shape[:2]
    fields = first_ref.shape[4]
    size = ro_ref.shape[2]
    groups = size // SPLIT

    def first_term(z, y, weight, values):
        if not 0 <= y < rows:
            return
        turn = groups // 2
        while turn:
            weight = weight + pltpu.roll(weight, size - turn, 0)
            turn //= 2
        w_ref[y] = (COEFFS[0] / (START * START * LAST)) * weight
        for m in range(SPLIT):
            at = m * groups
            w = jnp.broadcast_to(w_ref[y, at : at + 1], (fields, LANES))
            acc_ref[z, y, m] = w * values[m]

    def plane(z, carry):
        cells = []
        for y in range(-HALO, rows + HALO):
            value = of_fields(parts_ref, fields, depth, z, y)
            cells.append((row_tile(own_ref, a_ref, b_ref, z, y), two_parts(value, y), z, y))
        place(cells, r_ref, ro_ref, first_ref, first_term)
        return carry

    lax.fori_loop(0, depth, plane, 0)

    def scaled(z, carry):
        later_ref[z] = (INNER[-1] / INNER[0]) * r_ref[z]
        return carry

    lax.fori_loop(0, r_ref.shape[0], scaled, 0)


def inner_kernel(first_ref, r_ref, later_ref, inverse_ref, x_ref, y_ref, wide_ref):
    groups, region_z, region_y, _, fields = first_ref.shape[:5]
    depth, rows = region_z - 2 * HALO, region_y - 2 * HALO
    all_rows = depth * fields

    pick = one_hot(iota((all_rows, fields), 0) // depth == iota((all_rows, fields), 1))
    tile = one_hot(iota((fields, all_rows), 1) % fields == iota((fields, all_rows), 0))
    wide = bf16_dot(bf16_dot(pick, inverse_ref[...]).astype(jnp.bfloat16), tile)
    square = (all_rows, all_rows)
    same = iota(square, 0) % depth == iota(square, 1) // fields
    wide_ref[...] = jnp.where(same, wide, 0.0).astype(jnp.bfloat16)

    def group(g, carry):
        for z in range(1, depth - 1, 2):
            sweep(1, g, HALO + z, (HALO - 1,) * 2, rows, r_ref, first_ref, first_ref, x_ref)
        for z in range(2, depth - 2, 2):
            sweep(2, g, HALO + z, (HALO - 2,) * 2, rows, later_ref, first_ref, x_ref, y_ref)
        return carry

    lax.fori_loop(0, groups, group, 0)


def sweep_kernel(
    parts_ref, a_ref, b_ref, r_ref, later_ref, wide_ref, ro_in, first_in, x_in, y_in, acc_in,
    out_ref, ro_ref, first_ref, x_ref, y_ref, acc_ref, m_ref,
):
    depth, rows = acc_ref.shape[:2]
    fields = first_ref.shape[4]
    size = ro_ref.shape[2]
    groups = size // SPLIT
    count = groups * BATCH
    even = lax.rem(lax.axis_index("grid"), 2) == 0
    all_cells = list(enumerate(plane_cells(rows)))
    for d in range(1, HALO + 1):
        z_a = jnp.where(even, depth - 1 + d, -d)
        z_b = jnp.where(even, -d, depth - 1 + d)
        cells = []
        for at, (distance, y) in all_cells:
            if distance == d:
                for ref, z in ((a_ref, z_a), (b_ref, z_b)):
                    tile = ref[at].astype(jnp.float32)
                    cells.append((tile[:size], tile[size:], z, y))
        place(cells, r_ref, ro_ref, first_ref)

    top = HALO + depth

    def group(g, carry):
        for z, reaches in (
            (HALO - 2, (0,)),
            (HALO - 1, (1, 2)),
            (top - 1, (2, 1)),
            (top + 1, (0,)),
        ):
            sweep(1, g, z, reaches, rows, r_ref, first_ref, first_ref, x_ref)
        for z, reaches in ((HALO - 1, (0,)), (HALO, (1, 1)), (top - 2, (1, 1)), (top, (0,))):
            sweep(2, g, z, reaches, rows, later_ref, first_ref, x_ref, y_ref)

        def inner(pair, c):
            sweep(3, g, HALO + 2 * pair, (0, 0), rows, ro_ref, first_ref, y_ref, acc_ref)
            return c

        lax.fori_loop(0, depth // 2, inner, 0, unroll=2)
        return carry

    lax.fori_loop(0, groups, group, 0)

    lane_in, x_out = iota((SPLIT * LANES, LANES), 0), iota((SPLIT * LANES, LANES), 1) % NX
    gather = one_hot(x_out == SPLIT * (lane_in % STEPS) + lane_in // LANES)
    left = lane_halves((fields, LANES))
    factor = 4.0 / count * -0.5
    planes = []
    for z in range(depth):
        parts = [
            jnp.concatenate([acc_ref[z, y, m] for y in range(rows)], axis=0) for m in range(SPLIT)
        ]
        acc = jnp.concatenate(parts, axis=1)
        upper = acc.astype(jnp.bfloat16)
        lower = (acc - upper.astype(jnp.float32)).astype(jnp.bfloat16)
        total = bf16_dot(upper, gather) + bf16_dot(lower, gather)
        tiles = []
        for y in range(rows):
            tiles.append(total[y * fields : (y + 1) * fields])
        pieces = []
        for y in range(0, rows, 2):
            value = of_fields(parts_ref, fields, depth, z, y)
            pieces.append(value + factor * jnp.where(left, tiles[y], tiles[y + 1]))
        planes.append(jnp.concatenate(pieces, axis=1))
    stacked = jnp.concatenate(planes, axis=0).astype(jnp.bfloat16)
    updated = bf16_dot(wide_ref[...], stacked)

    m_ref[...] = jnp.zeros_like(m_ref)
    gram = jnp.zeros((fields, fields), jnp.float32)
    for z in range(depth):
        one = planes[z].astype(jnp.bfloat16)
        gram = gram + lax.dot_general(
            one, one, (((1,), (1,)), ((), ())), preferred_element_type=jnp.float32
        )
    m_ref[:, :fields] = gram
    pieces = rows * NX // LANES
    for p in range(fields):
        for t in range(pieces):
            out_ref[p, t] = updated[p * depth : (p + 1) * depth, t * LANES : (t + 1) * LANES]
        mine, other = m_ref[p : p + 1, :], m_ref[p ^ 1 : (p ^ 1) + 1, :]
        out_ref[p, pieces] = jnp.where(iota((depth, LANES), 0) == 1, other, mine)


VMEM = pl.BlockSpec(memory_space=pltpu.VMEM)
SMEM = pl.BlockSpec(memory_space=pltpu.SMEM)
ANY = pl.BlockSpec(memory_space=pl.ANY)


def in_vmem(*arrays):
    return [pltpu.with_memory_space_constraint(array, pltpu.VMEM) for array in arrays]


def in_hbm(array):
    return pltpu.with_memory_space_constraint(array, pltpu.HBM)


def swapped(to_a, to_b, axis):
    count = lax.axis_size(axis)
    pairs_a = [(i, i ^ 1) for i in range(count)]
    pairs_b = [(i, i + 1 if i % 2 else i - 1) for i in range(1, count - 1)]
    got_a = lax.ppermute(to_a, axis, pairs_a)
    got_b = lax.ppermute(to_b, axis, pairs_b)
    return got_a, got_b


def rows_plan(potentials, orbitals, energies, local_potential, inverse_factor):
    pots = lax.axis_size("pot")
    grids = lax.axis_size("grid")
    depth = potentials.shape[1]
    count, _, width = orbitals.shape
    rows = width // NX
    fields = pots
    half = count // 2
    f32, bf16 = jnp.float32, jnp.bfloat16
    shape = pltpu.VMEM
    tile = (half + fields, LANES)

    region = (depth + 2 * HALO, rows + 2 * HALO)
    pieces = width // LANES
    window = pieces + 2 * (LEAD * NX // LANES) - 1
    limit = pltpu.CompilerParams(vmem_limit_bytes=VMEM_LIMIT)
    call = functools.partial(pl.pallas_call, compiler_params=limit)
    side = len(row_cells(depth))
    lp_shape = (rows // 2 + LEAD, local_potential.shape[0], LANES)
    fields_tiles = potentials.reshape(depth, pots * pieces, LANES).transpose(1, 0, 2)
    windows, own, to_a, to_b, lp = call(
        first_kernel,
        out_shape=[
            pltpu.HBM((pots, window, depth, LANES), f32),
            shape((depth, rows, half, LANES), bf16),
            shape((side, half, LANES), bf16),
            shape((side, half, LANES), bf16),
            shape(lp_shape, f32),
        ],
        in_specs=[ANY] * 3,
        out_specs=[ANY] + [VMEM] * 4,
        scratch_shapes=[
            pltpu.VMEM((pots * pieces + window + 1 - pieces, depth, LANES), f32),
            pltpu.VMEM((pots, depth, LANES), f32),
            pltpu.VMEM(orbitals.shape, bf16),
            pltpu.VMEM((half * rows * depth, LANES), f32),
            pltpu.SemaphoreType.DMA((2 + 2 * pots,)),
            pltpu.SemaphoreType.DMA(lp_shape[:1]),
        ],
        name="first",
    )(in_hbm(fields_tiles), in_hbm(orbitals), in_hbm(local_potential))
    got_a, got_b = swapped(to_a, to_b, "pot")
    parts = lax.all_to_all(windows, "pot", 0, 0, tiled=True)
    parts = parts.reshape(pots * window * depth, LANES)

    inverse_diagonal = call(
        diagonal_kernel,
        out_shape=shape(region + (half, LANES), f32),
        in_specs=[SMEM, VMEM],
        out_specs=VMEM,
        scratch_shapes=[pltpu.VMEM((rows + 2 * LEAD, region[0] * SPLIT, LANES), f32)]
        + [pltpu.VMEM(lp_shape, f32)] * 3,
        name="diagonal",
    )(in_hbm(energies), *in_vmem(lp))

    parts, inverse_diagonal = lax.optimization_barrier((parts, inverse_diagonal))
    edge = len(plane_cells(rows))
    up, down = call(
        send_kernel,
        out_shape=[shape((edge,) + tile, bf16)] * 2,
        in_specs=[VMEM] * 4,
        out_specs=[VMEM] * 2,
        name="sends",
    )(*in_vmem(parts, own, got_a, got_b))
    z_a, z_b = swapped(up, down, "grid")

    group_count = half // SPLIT
    iterates = [
        shape((group_count, region[0] - 2 * n, region[1] - 2 * n, SPLIT, fields, LANES), f32)
        for n in range(SWEEPS - 1)
    ]
    per_orbital = shape(region + (half, LANES), f32)
    sums = shape((depth, rows, SPLIT, fields, LANES), f32)
    ro, first, acc, later = call(
        prepare_kernel,
        out_shape=[per_orbital, iterates[0], sums, per_orbital],
        in_specs=[VMEM] * 5,
        out_specs=[VMEM] * 4,
        scratch_shapes=[pltpu.VMEM((rows, half, LANES), f32)],
        name="prepare",
    )(*in_vmem(parts, own, got_a, got_b, inverse_diagonal))
    second, third, wide = call(
        inner_kernel,
        out_shape=iterates[1:] + [shape((depth * fields,) * 2, bf16)],
        in_specs=[VMEM] * 4,
        out_specs=[VMEM] * 3,
        name="inner",
    )(*in_vmem(first, inverse_diagonal, later), in_hbm(inverse_factor))
    prepared = [ro, first, second, third, acc]
    own_values = [per_orbital, *iterates, sums]
    sent, *_ = call(
        sweep_kernel,
        out_shape=[shape((fields, pieces + 1, depth, LANES), f32)] + own_values,
        in_specs=[VMEM] * 11,
        out_specs=[VMEM] * 6,
        scratch_shapes=[pltpu.VMEM((fields, LANES), f32)],
        input_output_aliases={6 + i: 1 + i for i in range(5)},
        name="sweeps",
    )(*in_vmem(parts, z_a, z_b, inverse_diagonal, later, wide, *prepared))

    back = lax.all_to_all(sent, "pot", 0, 0, tiled=True)
    updated = back[:, :pieces].reshape(pots * pieces, depth, LANES).transpose(1, 0, 2)
    updated = updated.reshape(1, depth, pots * width)
    margins = jnp.sum(back[:, pieces], axis=0)
    step = 1
    while step < grids:
        pairs = [
            (i * grids + g, i * grids + (g ^ step)) for i in range(1, pots, 2) for g in range(grids)
        ]
        margins = margins + lax.ppermute(margins, ("pot", "grid"), pairs)
        step *= 2
    handed = lax.ppermute(margins, "pot", [(i, i - 1) for i in range(1, pots, 2)])
    odd = lax.rem(lax.axis_index("pot"), 2) == 1
    margins = jnp.where(odd, margins[:1, :fields], handed[1:2, :fields]) / local_potential.size
    return updated, margins


def local(potentials, orbitals, energies, local_potential, inverse_factor):
    pots = lax.axis_size("pot")
    grids = lax.axis_size("grid")
    depth = potentials.shape[1]
    count, _, width = orbitals.shape
    fits = (
        potentials.shape[0] == 1
        and pots == 8
        and width % LANES == 0
        and LANES == 2 * NX
        and width // NX >= HALO
        and depth == 8
        and count % (BATCH * SPLIT) == 0
        and count // BATCH in (2, 4)
        and grids & (grids - 1) == 0
    )
    plan = rows_plan if fits else gathered_plan
    return plan(potentials, orbitals, energies, local_potential, inverse_factor)


def solution(mesh):
    in_specs = (P("pot", "grid", None), P(None, "grid", "pot"), P(), P(), P())
    out_specs = (P("pot", "grid", None), P("pot", None))
    return jax.shard_map(local, mesh=mesh, in_specs=in_specs, out_specs=out_specs, check_vma=False)
```

```python
import functools
import math

import jax
import jax.numpy as jnp
from jax import lax
from jax.experimental import pallas as pl
from jax.experimental.pallas import tpu as pltpu
from jax.sharding import PartitionSpec as P


NX = 64
SWEEPS = 4
DAMPING = 0.8
COEFFS = tuple(
    sum(math.comb(n, m) * (1.0 - DAMPING) ** (n - m) for n in range(m, SWEEPS))
    for m in range(SWEEPS)
)
START = COEFFS[SWEEPS - 2]
WEIGHTS = [COEFFS[SWEEPS - 2 - n] / START for n in range(SWEEPS - 2)]
INNER = tuple(
    ((1.0 / START) if n == 0 else WEIGHTS[n - 1]) / WEIGHTS[n] for n in range(SWEEPS - 2)
)
LAST = WEIGHTS[-1]
assert SWEEPS == 4
HALO = SWEEPS - 1
LEAD = HALO + HALO % 2
LANES = 128
SUBLANES = 8
VMEM_LIMIT = 8 << 20


def padded_2(block, sides, width):
    for axis, dim in sides:
        count = lax.axis_size(axis)
        forward = [(i, i + 1) for i in range(count - 1)]
        backward = [(target, source) for source, target in forward]
        low = lax.ppermute(
            lax.slice_in_dim(block, block.shape[dim] - width, None, axis=dim), axis, forward
        )
        high = lax.ppermute(lax.slice_in_dim(block, 0, width, axis=dim), axis, backward)
        block = jnp.concatenate([low, block, high], axis=dim)
    return block


def plane_neighbours(field, row_width):
    plane_size = field.shape[-1]
    widths = [(0, 0)] * (field.ndim - 1)
    padded = jnp.pad(field, widths + [(row_width, row_width)])
    along_y = padded[..., 2 * row_width :] + padded[..., :plane_size]
    column = jnp.arange(plane_size, dtype=jnp.int32) % row_width
    padded = jnp.pad(field, widths + [(1, 1)])
    right_side = jnp.where(column == row_width - 1, 0.0, padded[..., 2:])
    left_side = jnp.where(column == 0, 0.0, padded[..., :plane_size])
    return along_y + right_side + left_side


def across_slabs(answer):
    padded = padded_2(answer, (("grid", 2),), 1)
    return padded[:, :, 2:] + padded[:, :, :-2]


def absorb(orbital_block, energy_block, fields, local_here, along_planes):
    orbital = orbital_block.astype(jnp.float32)[:, None]
    diagonal = (3.0 + local_here[None] - energy_block[:, None, None])[:, None]
    source = -orbital * fields[None]
    answer = DAMPING * source / diagonal
    for _ in range(SWEEPS - 1):
        nearby = along_planes(answer) + plane_neighbours(answer, NX)
        answer = answer + DAMPING * (source - diagonal * answer + 0.5 * nearby) / diagonal
    return jnp.sum(orbital * answer, axis=0)


def gathered_plan(potentials, orbitals, energies, local_potential, inverse_factor):
    slab_depth = potentials.shape[1]
    count = orbitals.shape[0]
    cells = local_potential.size
    grid_index = lax.axis_index("grid")
    local_here = lax.dynamic_slice_in_dim(local_potential, grid_index * slab_depth, slab_depth, 0)
    blocks = 4 if count % 4 == 0 else 1
    block_size = count // blocks
    response = jnp.zeros(potentials.shape, jnp.float32)
    for number in range(blocks):
        orbital_block = orbitals[number * block_size : (number + 1) * block_size]
        gathered = lax.all_gather(orbital_block, "pot", axis=2, tiled=True)
        energy_block = energies[number * block_size : (number + 1) * block_size]
        response = response + absorb(gathered, energy_block, potentials, local_here, across_slabs)
    trial_block = (potentials + 4.0 / count * response).astype(jnp.bfloat16)
    by_cells = lax.all_to_all(trial_block, "pot", split_axis=2, concat_axis=0, tiled=True)
    row_count = by_cells.shape[0]
    flattened = by_cells.reshape(row_count, -1)
    partial_margins = lax.dot_general(
        flattened, flattened, (((1,), (1,)), ((), ())), preferred_element_type=jnp.float32
    )
    combined = jnp.dot(inverse_factor, flattened, preferred_element_type=jnp.float32).reshape(
        by_cells.shape
    )
    updated = lax.all_to_all(combined, "pot", split_axis=0, concat_axis=2, tiled=True)
    scattered = lax.psum_scatter(partial_margins, "pot", scatter_dimension=0, tiled=True)
    own_rows = lax.psum(scattered, "grid")
    margins = own_rows / cells
    return (updated, margins)


def row_cells(depth):
    return [(d, z) for d in range(1, HALO + 1) for z in range(depth)]


def plane_cells(rows):
    return [(d, y) for d in range(1, HALO + 1) for y in range(d - HALO, rows + HALO - d)]


def iota(shape, dim):
    return lax.broadcasted_iota(jnp.int32, shape, dim)


def bf16_dot(a, b):
    return jnp.dot(a, b, preferred_element_type=jnp.float32)


def one_hot(mask):
    return mask.astype(jnp.float32).astype(jnp.bfloat16)


def lane_halves(shape):
    return iota(shape, len(shape) - 1) < NX


SPLIT = 4
STEPS = NX // SPLIT
BATCH = LANES // STEPS


def first_kernel(
    fields_ref, orbitals_ref, potential_ref, windows_ref, own_ref, a_ref, b_ref, lp_ref,
    wide_ref, outer_ref, orb_ref, s_ref, sem_ref, lp_sem_ref,
):
    receivers, window = windows_ref.shape[:2]
    total = fields_ref.shape[0]
    ahead = LEAD * NX // LANES
    fetch = pltpu.make_async_copy(fields_ref, wide_ref.at[pl.ds(ahead, total)], sem_ref.at[0])
    fetch_orbitals = pltpu.make_async_copy(orbitals_ref, orb_ref, sem_ref.at[1])
    fetch.start()
    fetch_orbitals.start()
    first_pair = (lax.axis_index("pot") * own_ref.shape[1] - LEAD) // 2
    last_pair = potential_ref.shape[1] // LANES - 1
    fetches = []
    for p in range(lp_ref.shape[0]):
        at = pl.multiple_of(jnp.clip(first_pair + p, 0, last_pair) * LANES, LANES)
        source = potential_ref.at[:, pl.ds(at, LANES)]
        fetches.append(pltpu.make_async_copy(source, lp_ref.at[p], lp_sem_ref.at[p]))
    for copy in fetches:
        copy.start()
    for t in range(ahead):
        wide_ref[t] = jnp.zeros(wide_ref.shape[1:], wide_ref.dtype)
        wide_ref[ahead + total + t] = jnp.zeros(wide_ref.shape[1:], wide_ref.dtype)
    fetch.wait()
    copies = []
    for p in range(receivers):
        at = p * (total // receivers)
        left = lane_halves(outer_ref.shape[1:])
        outer_ref[p] = jnp.where(left, wide_ref[at + window], wide_ref[at])
        inner = wide_ref.at[pl.ds(at + 1, window - 1)]
        for source, target in (
            (outer_ref.at[pl.ds(p, 1)], windows_ref.at[p, pl.ds(0, 1)]),
            (inner, windows_ref.at[p, pl.ds(1, window - 1)]),
        ):
            copies.append(pltpu.make_async_copy(source, target, sem_ref.at[2 + len(copies)]))
    for copy in copies:
        copy.start()
    fetch_orbitals.wait()
    relayout(orb_ref, own_ref, a_ref, b_ref, s_ref)
    for copy in fetches + copies:
        copy.wait()


def relayout(orb_ref, own_ref, a_ref, b_ref, s_ref):
    count, depth, width = orb_ref.shape
    groups = count // BATCH
    rows = width // NX
    lane_in, lane_out = iota((LANES, LANES), 0), iota((LANES, LANES), 1)
    wanted = (lane_out // NX) * NX + SPLIT * (lane_out % STEPS) + lane_out // STEPS % SPLIT
    permute = one_hot(lane_in == wanted)
    lane = iota((depth, LANES), 1) // STEPS
    for t in range(width // LANES):
        lanes = slice(t * LANES, (t + 1) * LANES)
        tile = orb_ref[:, :, lanes].astype(jnp.float32).reshape(count * depth, LANES)
        tile = bf16_dot(tile.astype(jnp.bfloat16), permute)
        for g in range(groups):
            first = g * BATCH * depth
            regs = [tile[first + b * depth : first + (b + 1) * depth] for b in range(BATCH)]
            step = BATCH // 2
            while step:
                stays = lane // step % 2 == 0
                for b in range(BATCH):
                    if b & step == 0:
                        lo, hi = regs[b], regs[b + step]
                        regs[b] = jnp.where(stays, lo, pltpu.roll(hi, step * STEPS, 1))
                        regs[b + step] = jnp.where(
                            stays, pltpu.roll(lo, LANES - step * STEPS, 1), hi
                        )
                step //= 2
            for c in range(BATCH):
                y, m = 2 * t + c // SPLIT, c % SPLIT
                at = ((m * groups + g) * rows + y) * depth
                s_ref[at : at + depth] = regs[c]
    for z in range(depth):
        for y in range(rows):
            tile = s_ref[pl.ds(y * depth + z, SPLIT * groups, stride=rows * depth), :]
            own_ref[z, y] = tile.astype(jnp.bfloat16)
    even = lax.rem(lax.axis_index("pot"), 2) == 0
    for at, (d, z) in enumerate(row_cells(depth)):
        a_ref[at] = own_ref[z, jnp.where(even, rows - d, d - 1)]
        b_ref[at] = own_ref[z, jnp.where(even, d - 1, rows - d)]


def of_fields(parts_ref, fields, depth, z, y):
    pieces = parts_ref.shape[0] // (fields * depth)
    start = (y + LEAD) // 2 % pieces * depth + z
    return parts_ref[pl.ds(start, fields, stride=pieces * depth), :]


def two_parts(value, y):
    left = lane_halves(value.shape)
    upper = value.astype(jnp.bfloat16).astype(jnp.float32)
    lower = value - upper
    if y % 2:
        return jnp.where(left, pltpu.roll(upper, NX, 1), lower)
    return jnp.where(left, upper, pltpu.roll(lower, NX, 1))


def row_tile(own_ref, a_ref, b_ref, z, y):
    depth, rows = own_ref.shape[:2]
    even = lax.rem(lax.axis_index("pot"), 2) == 0
    if 0 <= y < rows:
        return own_ref[z, y]
    at = (-y - 1 if y < 0 else y - rows) * depth + z
    a, b = a_ref[at].astype(jnp.float32), b_ref[at].astype(jnp.float32)
    return jnp.where(even == (y < 0), b, a).astype(jnp.bfloat16)


def send_kernel(v_ref, own_ref, a_ref, b_ref, to_a_ref, to_b_ref):
    depth, rows = own_ref.shape[:2]
    fields = lax.axis_size("pot")
    even = lax.rem(lax.axis_index("grid"), 2) == 0

    def tile_of(z, y):
        value = of_fields(v_ref, fields, depth, z, y)
        orbitals = row_tile(own_ref, a_ref, b_ref, z, y).astype(jnp.float32)
        return jnp.concatenate([orbitals, two_parts(value, y)], axis=0)

    for at, (d, y) in enumerate(plane_cells(rows)):
        top, bottom = tile_of(depth - d, y), tile_of(d - 1, y)
        to_a_ref[at] = jnp.where(even, top, bottom).astype(jnp.bfloat16)
        to_b_ref[at] = jnp.where(even, bottom, top).astype(jnp.bfloat16)


def diagonal_kernel(energy_ref, lp_ref, r_ref, lp_ref2, *part_refs):
    pairs, planes_all, _ = lp_ref.shape
    region_z, region_y, size, _ = r_ref.shape
    depth, rows = region_z - 2 * HALO, region_y - 2 * HALO
    groups = size // SPLIT
    z_base = lax.axis_index("grid") * depth
    y_base = lax.axis_index("pot") * rows
    rows_all = lax.axis_size("pot") * rows

    shift = jnp.zeros((size, LANES), jnp.float32)
    group_of = iota((size, LANES), 0) % groups
    member = iota((size, LANES), 1) // STEPS
    for g in range(groups):
        for b in range(BATCH):
            here = (group_of == g) & (member == b)
            shift = jnp.where(here, 3.0 - energy_ref[g * BATCH + b], shift)

    for p in range(pairs):
        rest = lp_ref[p]
        for part_ref in part_refs:
            part = rest.astype(jnp.bfloat16).astype(jnp.float32)
            part_ref[p] = part
            rest = rest - part
    from_lane, to_lane = iota((LANES, 2 * LANES), 0), iota((LANES, 2 * LANES), 1)
    pick = one_hot(
        (from_lane // NX == to_lane // LANES) & (from_lane % NX // SPLIT == to_lane % STEPS)
    )
    tile = (SUBLANES, LANES)
    keep = iota(tile, 1) % SPLIT == iota(tile, 0) % SPLIT
    per_tile = SUBLANES // SPLIT
    plane_of = iota(tile, 0) // SPLIT

    def clipped(zi):
        return jnp.clip(z_base + zi - HALO, 0, planes_all - 1)

    def chosen(index, values):
        out = jnp.broadcast_to(values[0], tile)
        for number, value in enumerate(values[1:], 1):
            out = jnp.where(index == number, jnp.broadcast_to(value, tile), out)
        return out

    for p in range(pairs):
        stacked = []
        for ref in part_refs:
            for zi in range(0, region_z, per_tile):
                values = [ref[p, pl.ds(clipped(zi + i), 1), :] for i in range(per_tile)]
                stacked.append(jnp.where(keep, chosen(plane_of, values), 0.0))
        parts = bf16_dot(jnp.concatenate(stacked, axis=0).astype(jnp.bfloat16), pick)
        length = region_z * SPLIT
        lp = (parts[:length] + parts[length : 2 * length]) + parts[2 * length :]
        lp_ref2[2 * p] = lp[:, :LANES]
        lp_ref2[2 * p + 1] = lp[:, LANES:]

    m_of = iota(tile, 0) // groups
    ms = SUBLANES // groups

    def plane(zi, carry):
        zg = z_base + zi - HALO
        z_inside = (zg >= 0) & (zg < planes_all)
        for y in range(-HALO, rows + HALO):
            yg = y_base + y
            inside = z_inside & (yg >= 0) & (yg < rows_all)
            scale = jnp.where(inside, INNER[0] * 0.5 * DAMPING, 0.0)
            for part in range(size // SUBLANES):
                values = [
                    lp_ref2[y + LEAD, pl.ds(zi * SPLIT + part * ms + i, 1), :] for i in range(ms)
                ]
                at = slice(part * SUBLANES, (part + 1) * SUBLANES)
                r_ref[zi, y + HALO, at] = scale / (shift[at] + chosen(m_of, values))
        return carry

    lax.fori_loop(0, region_z, plane, 0)


def spread_matrix():
    from_lane = iota((LANES, SPLIT * LANES), 0)
    to_lane = iota((LANES, SPLIT * LANES), 1)
    return one_hot(from_lane % NX == SPLIT * (to_lane % STEPS) + to_lane // LANES)


def place(cells, r_ref, ro_ref, first_ref, then=None):
    fields = first_ref.shape[4]
    packed = jnp.concatenate([parts for _, parts, _, _ in cells], axis=0).astype(jnp.bfloat16)
    values = (START / LAST) * bf16_dot(packed, spread_matrix())
    for number, (orbitals, _, z, y) in enumerate(cells):
        zi, yi = z + HALO, y + HALO
        o = (-2.0 * START * LAST) * orbitals.astype(jnp.float32)
        ro = r_ref[zi, yi] * o
        ro_ref[zi, yi] = ro
        own = [
            values[number * fields : (number + 1) * fields, m * LANES : (m + 1) * LANES]
            for m in range(SPLIT)
        ]
        first_sweep(ro_ref, first_ref, z, y, own)
        if then is not None:
            then(z, y, o * ro, own)


def sweep(number, g, z, reaches, rows, scale_ref, first_ref, source_ref, target_ref):
    groups, fields = first_ref.shape[0], first_ref.shape[4]
    deep = len(reaches)
    before_number = number - 1
    last = number == SWEEPS - 1
    step = iota((fields, LANES), 1) % STEPS
    first_k = step == 0
    last_k = step == STEPS - 1

    def row(i, y):
        return [source_ref[g, z + i - before_number, y - before_number, m] for m in range(SPLIT)]

    most = max(reaches)
    ys = range(HALO - most, HALO + rows + most)
    before = [row(i, ys[0] - 1) for i in range(deep)]
    here = [row(i, ys[0]) for i in range(deep)]
    for y in ys:
        after = [row(i, y + 1) for i in range(deep)]
        under, over = row(-1, y), row(deep, y)
        for i in range(deep):
            if not -reaches[i] <= y - HALO < rows + reaches[i]:
                continue
            lower = here[i - 1] if i else under
            upper = here[i + 1] if i + 1 < deep else over
            mid = here[i]
            for m in range(SPLIT):
                if m:
                    left = mid[m - 1]
                else:
                    left = jnp.where(first_k, 0.0, pltpu.roll(mid[SPLIT - 1], 1, 1))
                if m + 1 < SPLIT:
                    right = mid[m + 1]
                else:
                    right = jnp.where(last_k, 0.0, pltpu.roll(mid[0], LANES - 1, 1))
                near = (before[i][m] + after[i][m]) + (lower[m] + upper[m])
                near = near + (left + right)
                scale = scale_ref[z + i, y, pl.ds(m * groups + g, 1), :]
                near = jnp.broadcast_to(scale, (fields, LANES)) * near
                if last:
                    target_ref[z + i - HALO, y - HALO, m] += near
                else:
                    base = mid[m] if number == 1 else first_ref[g, z + i, y, m]
                    target_ref[g, z + i - number, y - number, m] = near + base
        before, here = here, after


def first_sweep(ro_ref, first_ref, z, y, values):
    groups = first_ref.shape[0]
    zi, yi = z + HALO, y + HALO
    for g in range(groups):
        for m in range(SPLIT):
            at = m * groups + g
            ro = jnp.broadcast_to(ro_ref[zi, yi, at : at + 1], values[m].shape)
            first_ref[g, zi, yi, m] = ro * values[m]


def prepare_kernel(
    parts_ref, own_ref, a_ref, b_ref, r_ref, inverse_ref,
    ro_ref, first_ref, x_ref, y_ref, acc_ref, later_ref, wide_ref, w_ref,
):
    depth, rows = own_ref.shape[:2]
    fields = first_ref.shape[4]
    size = ro_ref.shape[2]
    groups = size // SPLIT

    def first_term(z, y, weight, values):
        if not 0 <= y < rows:
            return
        turn = groups // 2
        while turn:
            weight = weight + pltpu.roll(weight, size - turn, 0)
            turn //= 2
        w_ref[y] = (COEFFS[0] / (START * START * LAST)) * weight
        for m in range(SPLIT):
            at = m * groups
            w = jnp.broadcast_to(w_ref[y, at : at + 1], (fields, LANES))
            acc_ref[z, y, m] = w * values[m]

    def plane(z, carry):
        cells = []
        for y in range(-HALO, rows + HALO):
            value = of_fields(parts_ref, fields, depth, z, y)
            cells.append((row_tile(own_ref, a_ref, b_ref, z, y), two_parts(value, y), z, y))
        place(cells, r_ref, ro_ref, first_ref, first_term)
        return carry

    lax.fori_loop(0, depth, plane, 0, unroll=2)

    def scaled(z, carry):
        later_ref[z] = (INNER[-1] / INNER[0]) * r_ref[z]
        return carry

    lax.fori_loop(0, r_ref.shape[0], scaled, 0)

    all_rows = depth * fields

    pick = one_hot(iota((all_rows, fields), 0) // depth == iota((all_rows, fields), 1))
    tile = one_hot(iota((fields, all_rows), 1) % fields == iota((fields, all_rows), 0))
    wide = bf16_dot(bf16_dot(pick, inverse_ref[...]).astype(jnp.bfloat16), tile)
    square = (all_rows, all_rows)
    same = iota(square, 0) % depth == iota(square, 1) // fields
    wide_ref[...] = jnp.where(same, wide, 0.0).astype(jnp.bfloat16)

    def group(g, carry):
        for z in range(1, depth - 1, 2):
            sweep(1, g, HALO + z, (HALO - 1,) * 2, rows, r_ref, first_ref, first_ref, x_ref)
        for z in range(2, depth - 2, 2):
            sweep(2, g, HALO + z, (HALO - 2,) * 2, rows, later_ref, first_ref, x_ref, y_ref)
        return carry

    lax.fori_loop(0, groups, group, 0)


def sweep_kernel(
    parts_ref, a_ref, b_ref, r_ref, later_ref, wide_ref, ro_in, first_in, x_in, y_in, acc_in,
    out_ref, ro_ref, first_ref, x_ref, y_ref, acc_ref, m_ref,
):
    depth, rows = acc_ref.shape[:2]
    fields = first_ref.shape[4]
    size = ro_ref.shape[2]
    groups = size // SPLIT
    count = groups * BATCH
    even = lax.rem(lax.axis_index("grid"), 2) == 0
    all_cells = list(enumerate(plane_cells(rows)))
    for d in range(1, HALO + 1):
        z_a = jnp.where(even, depth - 1 + d, -d)
        z_b = jnp.where(even, -d, depth - 1 + d)
        cells = []
        for at, (distance, y) in all_cells:
            if distance == d:
                for ref, z in ((a_ref, z_a), (b_ref, z_b)):
                    tile = ref[at].astype(jnp.float32)
                    cells.append((tile[:size], tile[size:], z, y))
        place(cells, r_ref, ro_ref, first_ref)

    top = HALO + depth

    def group(g, carry):
        for z, reaches in (
            (HALO - 2, (0,)),
            (HALO - 1, (1, 2)),
            (top - 1, (2, 1)),
            (top + 1, (0,)),
        ):
            sweep(1, g, z, reaches, rows, r_ref, first_ref, first_ref, x_ref)
        for z, reaches in ((HALO - 1, (0,)), (HALO, (1, 1)), (top - 2, (1, 1)), (top, (0,))):
            sweep(2, g, z, reaches, rows, later_ref, first_ref, x_ref, y_ref)

        def inner(pair, c):
            sweep(3, g, HALO + 2 * pair, (0, 0), rows, ro_ref, first_ref, y_ref, acc_ref)
            return c

        lax.fori_loop(0, depth // 2, inner, 0, unroll=2)
        return carry

    lax.fori_loop(0, groups, group, 0)

    lane_in, x_out = iota((SPLIT * LANES, LANES), 0), iota((SPLIT * LANES, LANES), 1) % NX
    gather = one_hot(x_out == SPLIT * (lane_in % STEPS) + lane_in // LANES)
    left = lane_halves((fields, LANES))
    factor = 4.0 / count * -0.5
    planes = []
    for z in range(depth):
        parts = [
            jnp.concatenate([acc_ref[z, y, m] for y in range(rows)], axis=0) for m in range(SPLIT)
        ]
        acc = jnp.concatenate(parts, axis=1)
        upper = acc.astype(jnp.bfloat16)
        lower = (acc - upper.astype(jnp.float32)).astype(jnp.bfloat16)
        total = bf16_dot(upper, gather) + bf16_dot(lower, gather)
        tiles = []
        for y in range(rows):
            tiles.append(total[y * fields : (y + 1) * fields])
        pieces = []
        for y in range(0, rows, 2):
            value = of_fields(parts_ref, fields, depth, z, y)
            pieces.append(value + factor * jnp.where(left, tiles[y], tiles[y + 1]))
        planes.append(jnp.concatenate(pieces, axis=1))
    stacked = jnp.concatenate(planes, axis=0).astype(jnp.bfloat16)
    updated = bf16_dot(wide_ref[...], stacked)

    m_ref[...] = jnp.zeros_like(m_ref)
    gram = jnp.zeros((fields, fields), jnp.float32)
    for z in range(depth):
        one = planes[z].astype(jnp.bfloat16)
        gram = gram + lax.dot_general(
            one, one, (((1,), (1,)), ((), ())), preferred_element_type=jnp.float32
        )
    m_ref[:, :fields] = gram
    pieces = rows * NX // LANES
    for p in range(fields):
        for t in range(pieces):
            block = updated[p * depth : (p + 1) * depth, t * LANES : (t + 1) * LANES]
            out_ref[p, t] = block.astype(out_ref.dtype)
        rest = jnp.broadcast_to(m_ref[p : p + 1, :], (depth, LANES))
        spread = jnp.zeros((depth, LANES), jnp.float32)
        for number in range(3):
            part = rest.astype(jnp.bfloat16).astype(jnp.float32)
            spread = jnp.where(iota((depth, LANES), 0) == number, part, spread)
            rest = rest - part
        out_ref[p, pieces] = spread.astype(out_ref.dtype)


VMEM = pl.BlockSpec(memory_space=pltpu.VMEM)
SMEM = pl.BlockSpec(memory_space=pltpu.SMEM)
ANY = pl.BlockSpec(memory_space=pl.ANY)


def in_vmem(*arrays):
    return [pltpu.with_memory_space_constraint(array, pltpu.VMEM) for array in arrays]


def in_hbm(array):
    return pltpu.with_memory_space_constraint(array, pltpu.HBM)


def swapped(to_a, to_b, axis):
    count = lax.axis_size(axis)
    pairs_a = [(i, i ^ 1) for i in range(count)]
    pairs_b = [(i, i + 1 if i % 2 else i - 1) for i in range(1, count - 1)]
    got_a = lax.ppermute(to_a, axis, pairs_a)
    got_b = lax.ppermute(to_b, axis, pairs_b)
    return got_a, got_b


def rows_plan(potentials, orbitals, energies, local_potential, inverse_factor):
    pots = lax.axis_size("pot")
    grids = lax.axis_size("grid")
    depth = potentials.shape[1]
    count, _, width = orbitals.shape
    rows = width // NX
    fields = pots
    half = count // 2
    f32, bf16 = jnp.float32, jnp.bfloat16
    shape = pltpu.VMEM
    tile = (half + fields, LANES)

    region = (depth + 2 * HALO, rows + 2 * HALO)
    pieces = width // LANES
    window = pieces + 2 * (LEAD * NX // LANES) - 1
    limit = pltpu.CompilerParams(vmem_limit_bytes=VMEM_LIMIT)
    call = functools.partial(pl.pallas_call, compiler_params=limit)
    side = len(row_cells(depth))
    lp_shape = (rows // 2 + LEAD, local_potential.shape[0], LANES)
    fields_tiles = potentials.reshape(depth, pots * pieces, LANES).transpose(1, 0, 2)
    windows, own, to_a, to_b, lp = call(
        first_kernel,
        out_shape=[
            pltpu.HBM((pots, window, depth, LANES), f32),
            shape((depth, rows, half, LANES), bf16),
            shape((side, half, LANES), bf16),
            shape((side, half, LANES), bf16),
            shape(lp_shape, f32),
        ],
        in_specs=[ANY] * 3,
        out_specs=[ANY] + [VMEM] * 4,
        scratch_shapes=[
            pltpu.VMEM((pots * pieces + window + 1 - pieces, depth, LANES), f32),
            pltpu.VMEM((pots, depth, LANES), f32),
            pltpu.VMEM(orbitals.shape, bf16),
            pltpu.VMEM((half * rows * depth, LANES), f32),
            pltpu.SemaphoreType.DMA((2 + 2 * pots,)),
            pltpu.SemaphoreType.DMA(lp_shape[:1]),
        ],
        name="first",
    )(in_hbm(fields_tiles), in_hbm(orbitals), in_hbm(local_potential))
    got_a, got_b = swapped(to_a, to_b, "pot")
    parts = lax.all_to_all(windows, "pot", 0, 0, tiled=True)
    parts = parts.reshape(pots * window * depth, LANES)

    inverse_diagonal = call(
        diagonal_kernel,
        out_shape=shape(region + (half, LANES), f32),
        in_specs=[SMEM, VMEM],
        out_specs=VMEM,
        scratch_shapes=[pltpu.VMEM((rows + 2 * LEAD, region[0] * SPLIT, LANES), f32)]
        + [pltpu.VMEM(lp_shape, f32)] * 3,
        name="diagonal",
    )(in_hbm(energies), *in_vmem(lp))

    parts, inverse_diagonal = lax.optimization_barrier((parts, inverse_diagonal))
    edge = len(plane_cells(rows))
    up, down = call(
        send_kernel,
        out_shape=[shape((edge,) + tile, bf16)] * 2,
        in_specs=[VMEM] * 4,
        out_specs=[VMEM] * 2,
        name="sends",
    )(*in_vmem(parts, own, got_a, got_b))
    z_a, z_b = swapped(up, down, "grid")

    own_values = [
        shape(region + (half, LANES), f32),
        *(
            shape((half // SPLIT, region[0] - 2 * n, region[1] - 2 * n, SPLIT, fields, LANES), f32)
            for n in range(SWEEPS - 1)
        ),
        shape((depth, rows, SPLIT, fields, LANES), f32),
    ]
    *prepared, later, wide = call(
        prepare_kernel,
        out_shape=own_values + own_values[:1] + [shape((depth * fields,) * 2, bf16)],
        in_specs=[VMEM] * 6,
        out_specs=[VMEM] * 7,
        scratch_shapes=[pltpu.VMEM((rows, half, LANES), f32)],
        name="prepare",
    )(*in_vmem(parts, own, got_a, got_b, inverse_diagonal), in_hbm(inverse_factor))
    sent, *_ = call(
        sweep_kernel,
        out_shape=[shape((fields, pieces + 1, depth, LANES), bf16)] + own_values,
        in_specs=[VMEM] * 11,
        out_specs=[VMEM] * 6,
        scratch_shapes=[pltpu.VMEM((fields, LANES), f32)],
        input_output_aliases={6 + i: 1 + i for i in range(5)},
        name="sweeps",
    )(*in_vmem(parts, z_a, z_b, inverse_diagonal, later, wide, *prepared))

    back = lax.all_to_all(sent, "pot", 0, 0, tiled=True)
    updated = back[:, :pieces].astype(f32).reshape(pots * pieces, depth, LANES).transpose(1, 0, 2)
    updated = updated.reshape(1, depth, pots * width)
    margins = jnp.sum(back[:, pieces].astype(f32), axis=(0, 1))[None]
    step = 1
    while step < grids:
        margins = margins + lax.ppermute(margins, "grid", [(i, i ^ step) for i in range(grids)])
        step *= 2
    margins = margins[:1, :fields] / local_potential.size
    return updated, margins


def local(potentials, orbitals, energies, local_potential, inverse_factor):
    pots = lax.axis_size("pot")
    grids = lax.axis_size("grid")
    depth = potentials.shape[1]
    count, _, width = orbitals.shape
    fits = (
        potentials.shape[0] == 1
        and pots == 8
        and width % LANES == 0
        and LANES == 2 * NX
        and width // NX >= HALO
        and depth == 8
        and count % (BATCH * SPLIT) == 0
        and count // BATCH in (2, 4)
        and grids & (grids - 1) == 0
    )
    plan = rows_plan if fits else gathered_plan
    return plan(potentials, orbitals, energies, local_potential, inverse_factor)


def solution(mesh):
    in_specs = (P("pot", "grid", None), P(None, "grid", "pot"), P(), P(), P())
    out_specs = (P("pot", "grid", None), P("pot", None))
    return jax.shard_map(local, mesh=mesh, in_specs=in_specs, out_specs=out_specs, check_vma=False)
```

```python
import functools
import math

import jax
import jax.numpy as jnp
from jax import lax
from jax.experimental import pallas as pl
from jax.experimental.pallas import tpu as pltpu
from jax.sharding import PartitionSpec as P


NX = 64
SWEEPS = 4
DAMPING = 0.8
COEFFS = tuple(
    sum(math.comb(n, m) * (1.0 - DAMPING) ** (n - m) for n in range(m, SWEEPS))
    for m in range(SWEEPS)
)
START = COEFFS[SWEEPS - 2]
WEIGHTS = [COEFFS[SWEEPS - 2 - n] / START for n in range(SWEEPS - 2)]
INNER = tuple(
    ((1.0 / START) if n == 0 else WEIGHTS[n - 1]) / WEIGHTS[n] for n in range(SWEEPS - 2)
)
LAST = WEIGHTS[-1]
assert SWEEPS == 4
HALO = SWEEPS - 1
LEAD = HALO + HALO % 2
LANES = 128
SUBLANES = 8
VMEM_LIMIT = 8 << 20


def padded_2(block, sides, width):
    for axis, dim in sides:
        count = lax.axis_size(axis)
        forward = [(i, i + 1) for i in range(count - 1)]
        backward = [(target, source) for source, target in forward]
        low = lax.ppermute(
            lax.slice_in_dim(block, block.shape[dim] - width, None, axis=dim), axis, forward
        )
        high = lax.ppermute(lax.slice_in_dim(block, 0, width, axis=dim), axis, backward)
        block = jnp.concatenate([low, block, high], axis=dim)
    return block


def plane_neighbours(field, row_width):
    plane_size = field.shape[-1]
    widths = [(0, 0)] * (field.ndim - 1)
    padded = jnp.pad(field, widths + [(row_width, row_width)])
    along_y = padded[..., 2 * row_width :] + padded[..., :plane_size]
    column = jnp.arange(plane_size, dtype=jnp.int32) % row_width
    padded = jnp.pad(field, widths + [(1, 1)])
    right_side = jnp.where(column == row_width - 1, 0.0, padded[..., 2:])
    left_side = jnp.where(column == 0, 0.0, padded[..., :plane_size])
    return along_y + right_side + left_side


def across_slabs(answer):
    padded = padded_2(answer, (("grid", 2),), 1)
    return padded[:, :, 2:] + padded[:, :, :-2]


def absorb(orbital_block, energy_block, fields, local_here, along_planes):
    orbital = orbital_block.astype(jnp.float32)[:, None]
    diagonal = (3.0 + local_here[None] - energy_block[:, None, None])[:, None]
    source = -orbital * fields[None]
    answer = DAMPING * source / diagonal
    for _ in range(SWEEPS - 1):
        nearby = along_planes(answer) + plane_neighbours(answer, NX)
        answer = answer + DAMPING * (source - diagonal * answer + 0.5 * nearby) / diagonal
    return jnp.sum(orbital * answer, axis=0)


def gathered_plan(potentials, orbitals, energies, local_potential, inverse_factor):
    slab_depth = potentials.shape[1]
    count = orbitals.shape[0]
    cells = local_potential.size
    grid_index = lax.axis_index("grid")
    local_here = lax.dynamic_slice_in_dim(local_potential, grid_index * slab_depth, slab_depth, 0)
    blocks = 4 if count % 4 == 0 else 1
    block_size = count // blocks
    response = jnp.zeros(potentials.shape, jnp.float32)
    for number in range(blocks):
        orbital_block = orbitals[number * block_size : (number + 1) * block_size]
        gathered = lax.all_gather(orbital_block, "pot", axis=2, tiled=True)
        energy_block = energies[number * block_size : (number + 1) * block_size]
        response = response + absorb(gathered, energy_block, potentials, local_here, across_slabs)
    trial_block = (potentials + 4.0 / count * response).astype(jnp.bfloat16)
    by_cells = lax.all_to_all(trial_block, "pot", split_axis=2, concat_axis=0, tiled=True)
    row_count = by_cells.shape[0]
    flattened = by_cells.reshape(row_count, -1)
    partial_margins = lax.dot_general(
        flattened, flattened, (((1,), (1,)), ((), ())), preferred_element_type=jnp.float32
    )
    combined = jnp.dot(inverse_factor, flattened, preferred_element_type=jnp.float32).reshape(
        by_cells.shape
    )
    updated = lax.all_to_all(combined, "pot", split_axis=0, concat_axis=2, tiled=True)
    scattered = lax.psum_scatter(partial_margins, "pot", scatter_dimension=0, tiled=True)
    own_rows = lax.psum(scattered, "grid")
    margins = own_rows / cells
    return (updated, margins)


def row_cells(depth):
    return [(d, z) for d in range(1, HALO + 1) for z in range(depth)]


def plane_cells(rows):
    return [(d, y) for d in range(1, HALO + 1) for y in range(d - HALO, rows + HALO - d)]


def iota(shape, dim):
    return lax.broadcasted_iota(jnp.int32, shape, dim)


def bf16_dot(a, b):
    return jnp.dot(a, b, preferred_element_type=jnp.float32)


def one_hot(mask):
    return mask.astype(jnp.float32).astype(jnp.bfloat16)


def lane_halves(shape):
    return iota(shape, len(shape) - 1) < NX


SPLIT = 4
STEPS = NX // SPLIT
BATCH = LANES // STEPS


def first_kernel(
    fields_ref, orbitals_ref, potential_ref, windows_ref, own_ref, a_ref, b_ref, lp_ref,
    wide_ref, outer_ref, orb_ref, s_ref, sem_ref, lp_sem_ref,
):
    receivers, window = windows_ref.shape[:2]
    total = fields_ref.shape[0]
    ahead = LEAD * NX // LANES
    fetch = pltpu.make_async_copy(fields_ref, wide_ref.at[pl.ds(ahead, total)], sem_ref.at[0])
    fetch_orbitals = pltpu.make_async_copy(orbitals_ref, orb_ref, sem_ref.at[1])
    fetch.start()
    fetch_orbitals.start()
    first_pair = (lax.axis_index("pot") * own_ref.shape[1] - LEAD) // 2
    last_pair = potential_ref.shape[1] // LANES - 1
    fetches = []
    for p in range(lp_ref.shape[0]):
        at = pl.multiple_of(jnp.clip(first_pair + p, 0, last_pair) * LANES, LANES)
        source = potential_ref.at[:, pl.ds(at, LANES)]
        fetches.append(pltpu.make_async_copy(source, lp_ref.at[p], lp_sem_ref.at[p]))
    for copy in fetches:
        copy.start()
    for t in range(ahead):
        wide_ref[t] = jnp.zeros(wide_ref.shape[1:], wide_ref.dtype)
        wide_ref[ahead + total + t] = jnp.zeros(wide_ref.shape[1:], wide_ref.dtype)
    fetch.wait()
    copies = []
    for p in range(receivers):
        at = p * (total // receivers)
        left = lane_halves(outer_ref.shape[1:])
        outer_ref[p] = jnp.where(left, wide_ref[at + window], wide_ref[at])
        inner = wide_ref.at[pl.ds(at + 1, window - 1)]
        for source, target in (
            (outer_ref.at[pl.ds(p, 1)], windows_ref.at[p, pl.ds(0, 1)]),
            (inner, windows_ref.at[p, pl.ds(1, window - 1)]),
        ):
            copies.append(pltpu.make_async_copy(source, target, sem_ref.at[2 + len(copies)]))
    for copy in copies:
        copy.start()
    fetch_orbitals.wait()
    relayout(orb_ref, own_ref, a_ref, b_ref, s_ref)
    for copy in fetches + copies:
        copy.wait()


def relayout(orb_ref, own_ref, a_ref, b_ref, s_ref):
    count, depth, width = orb_ref.shape
    groups = count // BATCH
    rows = width // NX
    lane_in, lane_out = iota((LANES, LANES), 0), iota((LANES, LANES), 1)
    wanted = (lane_out // NX) * NX + SPLIT * (lane_out % STEPS) + lane_out // STEPS % SPLIT
    permute = one_hot(lane_in == wanted)
    lane = iota((depth, LANES), 1) // STEPS
    for t in range(width // LANES):
        lanes = slice(t * LANES, (t + 1) * LANES)
        tile = orb_ref[:, :, lanes].astype(jnp.float32).reshape(count * depth, LANES)
        tile = bf16_dot(tile.astype(jnp.bfloat16), permute)
        for g in range(groups):
            first = g * BATCH * depth
            regs = [tile[first + b * depth : first + (b + 1) * depth] for b in range(BATCH)]
            step = BATCH // 2
            while step:
                stays = lane // step % 2 == 0
                for b in range(BATCH):
                    if b & step == 0:
                        lo, hi = regs[b], regs[b + step]
                        regs[b] = jnp.where(stays, lo, pltpu.roll(hi, step * STEPS, 1))
                        regs[b + step] = jnp.where(
                            stays, pltpu.roll(lo, LANES - step * STEPS, 1), hi
                        )
                step //= 2
            for c in range(BATCH):
                y, m = 2 * t + c // SPLIT, c % SPLIT
                at = ((m * groups + g) * rows + y) * depth
                s_ref[at : at + depth] = regs[c]
    for z in range(depth):
        for y in range(rows):
            tile = s_ref[pl.ds(y * depth + z, SPLIT * groups, stride=rows * depth), :]
            own_ref[z, y] = tile.astype(jnp.bfloat16)
    even = lax.rem(lax.axis_index("pot"), 2) == 0
    for at, (d, z) in enumerate(row_cells(depth)):
        a_ref[at] = own_ref[z, jnp.where(even, rows - d, d - 1)]
        b_ref[at] = own_ref[z, jnp.where(even, d - 1, rows - d)]


def of_fields(parts_ref, fields, depth, z, y):
    pieces = parts_ref.shape[0] // (fields * depth)
    start = (y + LEAD) // 2 % pieces * depth + z
    return parts_ref[pl.ds(start, fields, stride=pieces * depth), :]


def two_parts(value, y):
    left = lane_halves(value.shape)
    upper = value.astype(jnp.bfloat16).astype(jnp.float32)
    lower = value - upper
    if y % 2:
        return jnp.where(left, pltpu.roll(upper, NX, 1), lower)
    return jnp.where(left, upper, pltpu.roll(lower, NX, 1))


def row_tile(own_ref, a_ref, b_ref, z, y):
    depth, rows = own_ref.shape[:2]
    even = lax.rem(lax.axis_index("pot"), 2) == 0
    if 0 <= y < rows:
        return own_ref[z, y]
    at = (-y - 1 if y < 0 else y - rows) * depth + z
    a, b = a_ref[at].astype(jnp.float32), b_ref[at].astype(jnp.float32)
    return jnp.where(even == (y < 0), b, a).astype(jnp.bfloat16)


def send_kernel(v_ref, own_ref, a_ref, b_ref, to_a_ref, to_b_ref):
    depth, rows = own_ref.shape[:2]
    fields = lax.axis_size("pot")
    even = lax.rem(lax.axis_index("grid"), 2) == 0

    def tile_of(z, y):
        value = of_fields(v_ref, fields, depth, z, y)
        orbitals = row_tile(own_ref, a_ref, b_ref, z, y).astype(jnp.float32)
        return jnp.concatenate([orbitals, two_parts(value, y)], axis=0)

    for at, (d, y) in enumerate(plane_cells(rows)):
        top, bottom = tile_of(depth - d, y), tile_of(d - 1, y)
        to_a_ref[at] = jnp.where(even, top, bottom).astype(jnp.bfloat16)
        to_b_ref[at] = jnp.where(even, bottom, top).astype(jnp.bfloat16)


def diagonal_kernel(energy_ref, lp_ref, r_ref, lp_ref2, *part_refs):
    pairs, planes_all, _ = lp_ref.shape
    region_z, region_y, size, _ = r_ref.shape
    depth, rows = region_z - 2 * HALO, region_y - 2 * HALO
    groups = size // SPLIT
    z_base = lax.axis_index("grid") * depth
    y_base = lax.axis_index("pot") * rows
    rows_all = lax.axis_size("pot") * rows

    shift = jnp.zeros((size, LANES), jnp.float32)
    group_of = iota((size, LANES), 0) % groups
    member = iota((size, LANES), 1) // STEPS
    for g in range(groups):
        for b in range(BATCH):
            here = (group_of == g) & (member == b)
            shift = jnp.where(here, 3.0 - energy_ref[g * BATCH + b], shift)

    for p in range(pairs):
        rest = lp_ref[p]
        for part_ref in part_refs:
            part = rest.astype(jnp.bfloat16).astype(jnp.float32)
            part_ref[p] = part
            rest = rest - part
    from_lane, to_lane = iota((LANES, 2 * LANES), 0), iota((LANES, 2 * LANES), 1)
    pick = one_hot(
        (from_lane // NX == to_lane // LANES) & (from_lane % NX // SPLIT == to_lane % STEPS)
    )
    tile = (SUBLANES, LANES)
    keep = iota(tile, 1) % SPLIT == iota(tile, 0) % SPLIT
    per_tile = SUBLANES // SPLIT
    plane_of = iota(tile, 0) // SPLIT

    def clipped(zi):
        return jnp.clip(z_base + zi - HALO, 0, planes_all - 1)

    def chosen(index, values):
        out = jnp.broadcast_to(values[0], tile)
        for number, value in enumerate(values[1:], 1):
            out = jnp.where(index == number, jnp.broadcast_to(value, tile), out)
        return out

    for p in range(pairs):
        stacked = []
        for ref in part_refs:
            for zi in range(0, region_z, per_tile):
                values = [ref[p, pl.ds(clipped(zi + i), 1), :] for i in range(per_tile)]
                stacked.append(jnp.where(keep, chosen(plane_of, values), 0.0))
        parts = bf16_dot(jnp.concatenate(stacked, axis=0).astype(jnp.bfloat16), pick)
        length = region_z * SPLIT
        lp = (parts[:length] + parts[length : 2 * length]) + parts[2 * length :]
        lp_ref2[2 * p] = lp[:, :LANES]
        lp_ref2[2 * p + 1] = lp[:, LANES:]

    m_of = iota(tile, 0) // groups
    ms = SUBLANES // groups

    def plane(zi, carry):
        zg = z_base + zi - HALO
        z_inside = (zg >= 0) & (zg < planes_all)
        for y in range(-HALO, rows + HALO):
            yg = y_base + y
            inside = z_inside & (yg >= 0) & (yg < rows_all)
            scale = jnp.where(inside, INNER[0] * 0.5 * DAMPING, 0.0)
            for part in range(size // SUBLANES):
                values = [
                    lp_ref2[y + LEAD, pl.ds(zi * SPLIT + part * ms + i, 1), :] for i in range(ms)
                ]
                at = slice(part * SUBLANES, (part + 1) * SUBLANES)
                r_ref[zi, y + HALO, at] = scale / (shift[at] + chosen(m_of, values))
        return carry

    lax.fori_loop(0, region_z, plane, 0)


def spread_matrix():
    from_lane = iota((LANES, SPLIT * LANES), 0)
    to_lane = iota((LANES, SPLIT * LANES), 1)
    return one_hot(from_lane % NX == SPLIT * (to_lane % STEPS) + to_lane // LANES)


def place(cells, r_ref, ro_ref, first_ref, then=None):
    fields = first_ref.shape[4]
    packed = jnp.concatenate([parts for _, parts, _, _ in cells], axis=0).astype(jnp.bfloat16)
    values = (START / LAST) * bf16_dot(packed, spread_matrix())
    for number, (orbitals, _, z, y) in enumerate(cells):
        zi, yi = z + HALO, y + HALO
        o = (-2.0 * START * LAST) * orbitals.astype(jnp.float32)
        ro = r_ref[zi, yi] * o
        ro_ref[zi, yi] = ro
        own = [
            values[number * fields : (number + 1) * fields, m * LANES : (m + 1) * LANES]
            for m in range(SPLIT)
        ]
        first_sweep(ro_ref, first_ref, z, y, own)
        if then is not None:
            then(z, y, o * ro, own)


def sweep(number, g, z, reaches, rows, scale_ref, first_ref, source_ref, target_ref):
    groups, fields = first_ref.shape[0], first_ref.shape[4]
    deep = len(reaches)
    before_number = number - 1
    last = number == SWEEPS - 1
    step = iota((fields, LANES), 1) % STEPS
    first_k = step == 0
    last_k = step == STEPS - 1

    def row(i, y):
        return [source_ref[g, z + i - before_number, y - before_number, m] for m in range(SPLIT)]

    most = max(reaches)
    ys = range(HALO - most, HALO + rows + most)
    before = [row(i, ys[0] - 1) for i in range(deep)]
    here = [row(i, ys[0]) for i in range(deep)]
    for y in ys:
        after = [row(i, y + 1) for i in range(deep)]
        under, over = row(-1, y), row(deep, y)
        for i in range(deep):
            if not -reaches[i] <= y - HALO < rows + reaches[i]:
                continue
            lower = here[i - 1] if i else under
            upper = here[i + 1] if i + 1 < deep else over
            mid = here[i]
            for m in range(SPLIT):
                if m:
                    left = mid[m - 1]
                else:
                    left = jnp.where(first_k, 0.0, pltpu.roll(mid[SPLIT - 1], 1, 1))
                if m + 1 < SPLIT:
                    right = mid[m + 1]
                else:
                    right = jnp.where(last_k, 0.0, pltpu.roll(mid[0], LANES - 1, 1))
                near = (before[i][m] + after[i][m]) + (lower[m] + upper[m])
                near = near + (left + right)
                scale = scale_ref[z + i, y, pl.ds(m * groups + g, 1), :]
                near = jnp.broadcast_to(scale, (fields, LANES)) * near
                if last:
                    target_ref[z + i - HALO, y - HALO, m] += near
                else:
                    base = mid[m] if number == 1 else first_ref[g, z + i, y, m]
                    target_ref[g, z + i - number, y - number, m] = near + base
        before, here = here, after


def first_sweep(ro_ref, first_ref, z, y, values):
    groups = first_ref.shape[0]
    zi, yi = z + HALO, y + HALO
    for g in range(groups):
        for m in range(SPLIT):
            at = m * groups + g
            ro = jnp.broadcast_to(ro_ref[zi, yi, at : at + 1], values[m].shape)
            first_ref[g, zi, yi, m] = ro * values[m]


def prepare_kernel(
    parts_ref, own_ref, a_ref, b_ref, r_ref, inverse_ref,
    ro_ref, first_ref, x_ref, y_ref, acc_ref, later_ref, wide_ref, w_ref,
):
    depth, rows = own_ref.shape[:2]
    fields = first_ref.shape[4]
    size = ro_ref.shape[2]
    groups = size // SPLIT

    def first_term(z, y, weight, values):
        if not 0 <= y < rows:
            return
        turn = groups // 2
        while turn:
            weight = weight + pltpu.roll(weight, size - turn, 0)
            turn //= 2
        w_ref[y] = (COEFFS[0] / (START * START * LAST)) * weight
        for m in range(SPLIT):
            at = m * groups
            w = jnp.broadcast_to(w_ref[y, at : at + 1], (fields, LANES))
            acc_ref[z, y, m] = w * values[m]

    def plane(z, carry):
        cells = []
        for y in range(-HALO, rows + HALO):
            value = of_fields(parts_ref, fields, depth, z, y)
            cells.append((row_tile(own_ref, a_ref, b_ref, z, y), two_parts(value, y), z, y))
        place(cells, r_ref, ro_ref, first_ref, first_term)
        return carry

    lax.fori_loop(0, depth, plane, 0, unroll=4)

    def scaled(z, carry):
        later_ref[z] = (INNER[-1] / INNER[0]) * r_ref[z]
        return carry

    lax.fori_loop(0, r_ref.shape[0], scaled, 0)

    all_rows = depth * fields

    pick = one_hot(iota((all_rows, fields), 0) // depth == iota((all_rows, fields), 1))
    tile = one_hot(iota((fields, all_rows), 1) % fields == iota((fields, all_rows), 0))
    wide = bf16_dot(bf16_dot(pick, inverse_ref[...]).astype(jnp.bfloat16), tile)
    square = (all_rows, all_rows)
    same = iota(square, 0) % depth == iota(square, 1) // fields
    wide_ref[...] = jnp.where(same, wide, 0.0).astype(jnp.bfloat16)

    def group(g, carry):
        for z in range(1, depth - 1, 2):
            sweep(1, g, HALO + z, (HALO - 1,) * 2, rows, r_ref, first_ref, first_ref, x_ref)
        for z in range(2, depth - 2, 2):
            sweep(2, g, HALO + z, (HALO - 2,) * 2, rows, later_ref, first_ref, x_ref, y_ref)
        return carry

    lax.fori_loop(0, groups, group, 0)


def sweep_kernel(
    parts_ref, a_ref, b_ref, r_ref, later_ref, wide_ref, ro_in, first_in, x_in, y_in, acc_in,
    out_ref, ro_ref, first_ref, x_ref, y_ref, acc_ref, m_ref,
):
    depth, rows = acc_ref.shape[:2]
    fields = first_ref.shape[4]
    size = ro_ref.shape[2]
    groups = size // SPLIT
    count = groups * BATCH
    even = lax.rem(lax.axis_index("grid"), 2) == 0
    all_cells = list(enumerate(plane_cells(rows)))
    for d in range(1, HALO + 1):
        z_a = jnp.where(even, depth - 1 + d, -d)
        z_b = jnp.where(even, -d, depth - 1 + d)
        cells = []
        for at, (distance, y) in all_cells:
            if distance == d:
                for ref, z in ((a_ref, z_a), (b_ref, z_b)):
                    tile = ref[at].astype(jnp.float32)
                    cells.append((tile[:size], tile[size:], z, y))
        place(cells, r_ref, ro_ref, first_ref)

    top = HALO + depth

    def group(g, carry):
        for z, reaches in (
            (HALO - 2, (0,)),
            (HALO - 1, (1, 2)),
            (top - 1, (2, 1)),
            (top + 1, (0,)),
        ):
            sweep(1, g, z, reaches, rows, r_ref, first_ref, first_ref, x_ref)
        for z, reaches in ((HALO - 1, (0,)), (HALO, (1, 1)), (top - 2, (1, 1)), (top, (0,))):
            sweep(2, g, z, reaches, rows, later_ref, first_ref, x_ref, y_ref)

        def inner(pair, c):
            sweep(3, g, HALO + 2 * pair, (0, 0), rows, ro_ref, first_ref, y_ref, acc_ref)
            return c

        lax.fori_loop(0, depth // 2, inner, 0, unroll=2)
        return carry

    lax.fori_loop(0, groups, group, 0)

    lane_in, x_out = iota((SPLIT * LANES, LANES), 0), iota((SPLIT * LANES, LANES), 1) % NX
    gather = one_hot(x_out == SPLIT * (lane_in % STEPS) + lane_in // LANES)
    left = lane_halves((fields, LANES))
    factor = 4.0 / count * -0.5
    planes = []
    for z in range(depth):
        parts = [
            jnp.concatenate([acc_ref[z, y, m] for y in range(rows)], axis=0) for m in range(SPLIT)
        ]
        acc = jnp.concatenate(parts, axis=1)
        upper = acc.astype(jnp.bfloat16)
        lower = (acc - upper.astype(jnp.float32)).astype(jnp.bfloat16)
        total = bf16_dot(upper, gather) + bf16_dot(lower, gather)
        tiles = []
        for y in range(rows):
            tiles.append(total[y * fields : (y + 1) * fields])
        pieces = []
        for y in range(0, rows, 2):
            value = of_fields(parts_ref, fields, depth, z, y)
            pieces.append(value + factor * jnp.where(left, tiles[y], tiles[y + 1]))
        planes.append(jnp.concatenate(pieces, axis=1))
    stacked = jnp.concatenate(planes, axis=0).astype(jnp.bfloat16)
    updated = bf16_dot(wide_ref[...], stacked)

    m_ref[...] = jnp.zeros_like(m_ref)
    gram = jnp.zeros((fields, fields), jnp.float32)
    for z in range(depth):
        one = planes[z].astype(jnp.bfloat16)
        gram = gram + lax.dot_general(
            one, one, (((1,), (1,)), ((), ())), preferred_element_type=jnp.float32
        )
    m_ref[:, :fields] = gram
    pieces = rows * NX // LANES
    for p in range(fields):
        for t in range(pieces):
            block = updated[p * depth : (p + 1) * depth, t * LANES : (t + 1) * LANES]
            out_ref[p, t] = block.astype(out_ref.dtype)
        rest = jnp.broadcast_to(m_ref[p : p + 1, :], (depth, LANES))
        spread = jnp.zeros((depth, LANES), jnp.float32)
        for number in range(3):
            part = rest.astype(jnp.bfloat16).astype(jnp.float32)
            spread = jnp.where(iota((depth, LANES), 0) == number, part, spread)
            rest = rest - part
        out_ref[p, pieces] = spread.astype(out_ref.dtype)


VMEM = pl.BlockSpec(memory_space=pltpu.VMEM)
SMEM = pl.BlockSpec(memory_space=pltpu.SMEM)
ANY = pl.BlockSpec(memory_space=pl.ANY)


def in_vmem(*arrays):
    return [pltpu.with_memory_space_constraint(array, pltpu.VMEM) for array in arrays]


def in_hbm(array):
    return pltpu.with_memory_space_constraint(array, pltpu.HBM)


def swapped(to_a, to_b, axis, name):
    count = lax.axis_size(axis)
    pairs_a = [(i, i ^ 1) for i in range(count)]
    pairs_b = [(i, i + 1 if i % 2 else i - 1) for i in range(1, count - 1)]
    if name == "row":
        pairs_b = [(i, (i + 1 if i % 2 else i - 1) % count) for i in range(count)]
    got_a = lax.ppermute(to_a, axis, pairs_a)
    got_b = lax.ppermute(to_b, axis, pairs_b)
    return got_a, got_b


def rows_plan(potentials, orbitals, energies, local_potential, inverse_factor):
    pots = lax.axis_size("pot")
    grids = lax.axis_size("grid")
    depth = potentials.shape[1]
    count, _, width = orbitals.shape
    rows = width // NX
    fields = pots
    half = count // 2
    f32, bf16 = jnp.float32, jnp.bfloat16
    shape = pltpu.VMEM
    tile = (half + fields, LANES)

    region = (depth + 2 * HALO, rows + 2 * HALO)
    pieces = width // LANES
    window = pieces + 2 * (LEAD * NX // LANES) - 1
    limit = pltpu.CompilerParams(vmem_limit_bytes=VMEM_LIMIT)
    call = functools.partial(pl.pallas_call, compiler_params=limit)
    side = len(row_cells(depth))
    lp_shape = (rows // 2 + LEAD, local_potential.shape[0], LANES)
    fields_tiles = potentials.reshape(depth, pots * pieces, LANES).transpose(1, 0, 2)
    windows, own, to_a, to_b, lp = call(
        first_kernel,
        out_shape=[
            pltpu.HBM((pots, window, depth, LANES), f32),
            shape((depth, rows, half, LANES), bf16),
            shape((side, half, LANES), bf16),
            shape((side, half, LANES), bf16),
            shape(lp_shape, f32),
        ],
        in_specs=[ANY] * 3,
        out_specs=[ANY] + [VMEM] * 4,
        scratch_shapes=[
            pltpu.VMEM((pots * pieces + window + 1 - pieces, depth, LANES), f32),
            pltpu.VMEM((pots, depth, LANES), f32),
            pltpu.VMEM(orbitals.shape, bf16),
            pltpu.VMEM((half * rows * depth, LANES), f32),
            pltpu.SemaphoreType.DMA((2 + 2 * pots,)),
            pltpu.SemaphoreType.DMA(lp_shape[:1]),
        ],
        name="first",
    )(in_hbm(fields_tiles), in_hbm(orbitals), in_hbm(local_potential))
    got_a, got_b = swapped(to_a, to_b, "pot", "row")
    parts = lax.all_to_all(windows, "pot", 0, 0, tiled=True)
    parts = parts.reshape(pots * window * depth, LANES)

    inverse_diagonal = call(
        diagonal_kernel,
        out_shape=shape(region + (half, LANES), f32),
        in_specs=[SMEM, VMEM],
        out_specs=VMEM,
        scratch_shapes=[pltpu.VMEM((rows + 2 * LEAD, region[0] * SPLIT, LANES), f32)]
        + [pltpu.VMEM(lp_shape, f32)] * 3,
        name="diagonal",
    )(in_hbm(energies), *in_vmem(lp))

    parts, inverse_diagonal = lax.optimization_barrier((parts, inverse_diagonal))
    edge = len(plane_cells(rows))
    up, down = call(
        send_kernel,
        out_shape=[shape((edge,) + tile, bf16)] * 2,
        in_specs=[VMEM] * 4,
        out_specs=[VMEM] * 2,
        name="sends",
    )(*in_vmem(parts, own, got_a, got_b))
    z_a, z_b = swapped(up, down, "grid", "plane")

    own_values = [
        shape(region + (half, LANES), f32),
        *(
            shape((half // SPLIT, region[0] - 2 * n, region[1] - 2 * n, SPLIT, fields, LANES), f32)
            for n in range(SWEEPS - 1)
        ),
        shape((depth, rows, SPLIT, fields, LANES), f32),
    ]
    *prepared, later, wide = call(
        prepare_kernel,
        out_shape=own_values + own_values[:1] + [shape((depth * fields,) * 2, bf16)],
        in_specs=[VMEM] * 6,
        out_specs=[VMEM] * 7,
        scratch_shapes=[pltpu.VMEM((rows, half, LANES), f32)],
        name="prepare",
    )(*in_vmem(parts, own, got_a, got_b, inverse_diagonal), in_hbm(inverse_factor))
    sent, *_ = call(
        sweep_kernel,
        out_shape=[shape((fields, pieces + 1, depth, LANES), bf16)] + own_values,
        in_specs=[VMEM] * 11,
        out_specs=[VMEM] * 6,
        scratch_shapes=[pltpu.VMEM((fields, LANES), f32)],
        input_output_aliases={6 + i: 1 + i for i in range(5)},
        name="sweeps",
    )(*in_vmem(parts, z_a, z_b, inverse_diagonal, later, wide, *prepared))

    back = lax.all_to_all(sent, "pot", 0, 0, tiled=True)
    updated = back[:, :pieces].astype(f32).reshape(pots * pieces, depth, LANES).transpose(1, 0, 2)
    updated = updated.reshape(1, depth, pots * width)
    margins = jnp.sum(back[:, pieces].astype(f32), axis=(0, 1))[None]
    step = 1
    while step < grids:
        margins = margins + lax.ppermute(margins, "grid", [(i, i ^ step) for i in range(grids)])
        step *= 2
    margins = margins[:1, :fields] / local_potential.size
    return updated, margins


def local(potentials, orbitals, energies, local_potential, inverse_factor):
    pots = lax.axis_size("pot")
    grids = lax.axis_size("grid")
    depth = potentials.shape[1]
    count, _, width = orbitals.shape
    fits = (
        potentials.shape[0] == 1
        and pots == 8
        and width % LANES == 0
        and LANES == 2 * NX
        and width // NX >= HALO
        and depth == 8
        and count % (BATCH * SPLIT) == 0
        and count // BATCH in (2, 4)
        and grids & (grids - 1) == 0
    )
    plan = rows_plan if fits else gathered_plan
    return plan(potentials, orbitals, energies, local_potential, inverse_factor)


def solution(mesh):
    in_specs = (P("pot", "grid", None), P(None, "grid", "pot"), P(), P(), P())
    out_specs = (P("pot", "grid", None), P("pot", None))
    return jax.shard_map(local, mesh=mesh, in_specs=in_specs, out_specs=out_specs, check_vma=False)
```

```python
import functools
import math

import jax
import jax.numpy as jnp
from jax import lax
from jax.experimental import pallas as pl
from jax.experimental.pallas import tpu as pltpu
from jax.sharding import PartitionSpec as P


NX = 64
SWEEPS = 4
DAMPING = 0.8
COEFFS = tuple(
    sum(math.comb(n, m) * (1.0 - DAMPING) ** (n - m) for n in range(m, SWEEPS))
    for m in range(SWEEPS)
)
START = COEFFS[SWEEPS - 2]
WEIGHTS = [COEFFS[SWEEPS - 2 - n] / START for n in range(SWEEPS - 2)]
INNER = tuple(
    ((1.0 / START) if n == 0 else WEIGHTS[n - 1]) / WEIGHTS[n] for n in range(SWEEPS - 2)
)
LAST = WEIGHTS[-1]
assert SWEEPS == 4
HALO = SWEEPS - 1
LEAD = HALO + HALO % 2
LANES = 128
SUBLANES = 8
VMEM_LIMIT = 8 << 20


def padded_2(block, sides, width):
    for axis, dim in sides:
        count = lax.axis_size(axis)
        forward = [(i, i + 1) for i in range(count - 1)]
        backward = [(target, source) for source, target in forward]
        low = lax.ppermute(
            lax.slice_in_dim(block, block.shape[dim] - width, None, axis=dim), axis, forward
        )
        high = lax.ppermute(lax.slice_in_dim(block, 0, width, axis=dim), axis, backward)
        block = jnp.concatenate([low, block, high], axis=dim)
    return block


def plane_neighbours(field, row_width):
    plane_size = field.shape[-1]
    widths = [(0, 0)] * (field.ndim - 1)
    padded = jnp.pad(field, widths + [(row_width, row_width)])
    along_y = padded[..., 2 * row_width :] + padded[..., :plane_size]
    column = jnp.arange(plane_size, dtype=jnp.int32) % row_width
    padded = jnp.pad(field, widths + [(1, 1)])
    right_side = jnp.where(column == row_width - 1, 0.0, padded[..., 2:])
    left_side = jnp.where(column == 0, 0.0, padded[..., :plane_size])
    return along_y + right_side + left_side


def across_slabs(answer):
    padded = padded_2(answer, (("grid", 2),), 1)
    return padded[:, :, 2:] + padded[:, :, :-2]


def absorb(orbital_block, energy_block, fields, local_here, along_planes):
    orbital = orbital_block.astype(jnp.float32)[:, None]
    diagonal = (3.0 + local_here[None] - energy_block[:, None, None])[:, None]
    source = -orbital * fields[None]
    answer = DAMPING * source / diagonal
    for _ in range(SWEEPS - 1):
        nearby = along_planes(answer) + plane_neighbours(answer, NX)
        answer = answer + DAMPING * (source - diagonal * answer + 0.5 * nearby) / diagonal
    return jnp.sum(orbital * answer, axis=0)


def gathered_plan(potentials, orbitals, energies, local_potential, inverse_factor):
    slab_depth = potentials.shape[1]
    count = orbitals.shape[0]
    cells = local_potential.size
    grid_index = lax.axis_index("grid")
    local_here = lax.dynamic_slice_in_dim(local_potential, grid_index * slab_depth, slab_depth, 0)
    blocks = 4 if count % 4 == 0 else 1
    block_size = count // blocks
    response = jnp.zeros(potentials.shape, jnp.float32)
    for number in range(blocks):
        orbital_block = orbitals[number * block_size : (number + 1) * block_size]
        gathered = lax.all_gather(orbital_block, "pot", axis=2, tiled=True)
        energy_block = energies[number * block_size : (number + 1) * block_size]
        response = response + absorb(gathered, energy_block, potentials, local_here, across_slabs)
    trial_block = (potentials + 4.0 / count * response).astype(jnp.bfloat16)
    by_cells = lax.all_to_all(trial_block, "pot", split_axis=2, concat_axis=0, tiled=True)
    row_count = by_cells.shape[0]
    flattened = by_cells.reshape(row_count, -1)
    partial_margins = lax.dot_general(
        flattened, flattened, (((1,), (1,)), ((), ())), preferred_element_type=jnp.float32
    )
    combined = jnp.dot(inverse_factor, flattened, preferred_element_type=jnp.float32).reshape(
        by_cells.shape
    )
    updated = lax.all_to_all(combined, "pot", split_axis=0, concat_axis=2, tiled=True)
    scattered = lax.psum_scatter(partial_margins, "pot", scatter_dimension=0, tiled=True)
    own_rows = lax.psum(scattered, "grid")
    margins = own_rows / cells
    return (updated, margins)


def row_cells(depth):
    return [(d, z) for d in range(1, HALO + 1) for z in range(depth)]


def plane_cells(rows):
    return [(d, y) for d in range(1, HALO + 1) for y in range(d - HALO, rows + HALO - d)]


def iota(shape, dim):
    return lax.broadcasted_iota(jnp.int32, shape, dim)


def bf16_dot(a, b):
    return jnp.dot(a, b, preferred_element_type=jnp.float32)


def one_hot(mask):
    return mask.astype(jnp.float32).astype(jnp.bfloat16)


def lane_halves(shape):
    return iota(shape, len(shape) - 1) < NX


SPLIT = 4
STEPS = NX // SPLIT
BATCH = LANES // STEPS


def first_kernel(
    fields_ref, orbitals_ref, potential_ref, windows_ref, own_ref, a_ref, b_ref, lp_ref,
    wide_ref, outer_ref, orb_ref, s_ref, sem_ref, lp_sem_ref,
):
    receivers, window = windows_ref.shape[:2]
    total = fields_ref.shape[0]
    ahead = LEAD * NX // LANES
    fetch = pltpu.make_async_copy(fields_ref, wide_ref.at[pl.ds(ahead, total)], sem_ref.at[0])
    fetch_orbitals = pltpu.make_async_copy(orbitals_ref, orb_ref, sem_ref.at[1])
    fetch.start()
    fetch_orbitals.start()
    first_pair = (lax.axis_index("pot") * own_ref.shape[1] - LEAD) // 2
    last_pair = potential_ref.shape[1] // LANES - 1
    fetches = []
    for p in range(lp_ref.shape[0]):
        at = pl.multiple_of(jnp.clip(first_pair + p, 0, last_pair) * LANES, LANES)
        source = potential_ref.at[:, pl.ds(at, LANES)]
        fetches.append(pltpu.make_async_copy(source, lp_ref.at[p], lp_sem_ref.at[p]))
    for copy in fetches:
        copy.start()
    for t in range(ahead):
        wide_ref[t] = jnp.zeros(wide_ref.shape[1:], wide_ref.dtype)
        wide_ref[ahead + total + t] = jnp.zeros(wide_ref.shape[1:], wide_ref.dtype)
    fetch.wait()
    copies = []
    for p in range(receivers):
        at = p * (total // receivers)
        left = lane_halves(outer_ref.shape[1:])
        outer_ref[p] = jnp.where(left, wide_ref[at + window], wide_ref[at])
        inner = wide_ref.at[pl.ds(at + 1, window - 1)]
        for source, target in (
            (outer_ref.at[pl.ds(p, 1)], windows_ref.at[p, pl.ds(0, 1)]),
            (inner, windows_ref.at[p, pl.ds(1, window - 1)]),
        ):
            copies.append(pltpu.make_async_copy(source, target, sem_ref.at[2 + len(copies)]))
    for copy in copies:
        copy.start()
    fetch_orbitals.wait()
    relayout(orb_ref, own_ref, a_ref, b_ref, s_ref)
    for copy in fetches + copies:
        copy.wait()


def relayout(orb_ref, own_ref, a_ref, b_ref, s_ref):
    count, depth, width = orb_ref.shape
    groups = count // BATCH
    rows = width // NX
    lane_in, lane_out = iota((LANES, LANES), 0), iota((LANES, LANES), 1)
    wanted = (lane_out // NX) * NX + SPLIT * (lane_out % STEPS) + lane_out // STEPS % SPLIT
    permute = one_hot(lane_in == wanted)
    lane = iota((depth, LANES), 1) // STEPS
    for t in range(width // LANES):
        lanes = slice(t * LANES, (t + 1) * LANES)
        tile = orb_ref[:, :, lanes].astype(jnp.float32).reshape(count * depth, LANES)
        tile = bf16_dot(tile.astype(jnp.bfloat16), permute)
        for g in range(groups):
            first = g * BATCH * depth
            regs = [tile[first + b * depth : first + (b + 1) * depth] for b in range(BATCH)]
            step = BATCH // 2
            while step:
                stays = lane // step % 2 == 0
                for b in range(BATCH):
                    if b & step == 0:
                        lo, hi = regs[b], regs[b + step]
                        regs[b] = jnp.where(stays, lo, pltpu.roll(hi, step * STEPS, 1))
                        regs[b + step] = jnp.where(
                            stays, pltpu.roll(lo, LANES - step * STEPS, 1), hi
                        )
                step //= 2
            for c in range(BATCH):
                y, m = 2 * t + c // SPLIT, c % SPLIT
                at = ((m * groups + g) * rows + y) * depth
                s_ref[at : at + depth] = regs[c]
    for z in range(depth):
        for y in range(rows):
            tile = s_ref[pl.ds(y * depth + z, SPLIT * groups, stride=rows * depth), :]
            own_ref[z, y] = tile.astype(jnp.bfloat16)
    even = lax.rem(lax.axis_index("pot"), 2) == 0
    for at, (d, z) in enumerate(row_cells(depth)):
        a_ref[at] = own_ref[z, jnp.where(even, rows - d, d - 1)]
        b_ref[at] = own_ref[z, jnp.where(even, d - 1, rows - d)]


def of_fields(parts_ref, fields, depth, z, y):
    pieces = parts_ref.shape[0] // (fields * depth)
    start = (y + LEAD) // 2 % pieces * depth + z
    return parts_ref[pl.ds(start, fields, stride=pieces * depth), :]


def two_parts(value, y):
    left = lane_halves(value.shape)
    upper = value.astype(jnp.bfloat16).astype(jnp.float32)
    lower = value - upper
    if y % 2:
        return jnp.where(left, pltpu.roll(upper, NX, 1), lower)
    return jnp.where(left, upper, pltpu.roll(lower, NX, 1))


def row_tile(own_ref, a_ref, b_ref, z, y):
    depth, rows = own_ref.shape[:2]
    even = lax.rem(lax.axis_index("pot"), 2) == 0
    if 0 <= y < rows:
        return own_ref[z, y]
    at = (-y - 1 if y < 0 else y - rows) * depth + z
    a, b = a_ref[at].astype(jnp.float32), b_ref[at].astype(jnp.float32)
    return jnp.where(even == (y < 0), b, a).astype(jnp.bfloat16)


def send_kernel(v_ref, own_ref, a_ref, b_ref, to_a_ref, to_b_ref):
    depth, rows = own_ref.shape[:2]
    fields = lax.axis_size("pot")
    even = lax.rem(lax.axis_index("grid"), 2) == 0

    def tile_of(z, y):
        value = of_fields(v_ref, fields, depth, z, y)
        orbitals = row_tile(own_ref, a_ref, b_ref, z, y).astype(jnp.float32)
        return jnp.concatenate([orbitals, two_parts(value, y)], axis=0)

    for at, (d, y) in enumerate(plane_cells(rows)):
        top, bottom = tile_of(depth - d, y), tile_of(d - 1, y)
        to_a_ref[at] = jnp.where(even, top, bottom).astype(jnp.bfloat16)
        to_b_ref[at] = jnp.where(even, bottom, top).astype(jnp.bfloat16)


def diagonal_kernel(
    energy_ref, lp_ref, r_ref, spread_ref, gather_ref, lp_ref2, *part_refs
):
    pairs, planes_all, _ = lp_ref.shape
    region_z, region_y, size, _ = r_ref.shape
    depth, rows = region_z - 2 * HALO, region_y - 2 * HALO
    groups = size // SPLIT
    z_base = lax.axis_index("grid") * depth
    y_base = lax.axis_index("pot") * rows
    rows_all = lax.axis_size("pot") * rows

    shift = jnp.zeros((size, LANES), jnp.float32)
    group_of = iota((size, LANES), 0) % groups
    member = iota((size, LANES), 1) // STEPS
    for g in range(groups):
        for b in range(BATCH):
            here = (group_of == g) & (member == b)
            shift = jnp.where(here, 3.0 - energy_ref[g * BATCH + b], shift)

    for p in range(pairs):
        rest = lp_ref[p]
        for part_ref in part_refs:
            part = rest.astype(jnp.bfloat16).astype(jnp.float32)
            part_ref[p] = part
            rest = rest - part
    from_lane, to_lane = iota((LANES, 2 * LANES), 0), iota((LANES, 2 * LANES), 1)
    pick = one_hot(
        (from_lane // NX == to_lane // LANES) & (from_lane % NX // SPLIT == to_lane % STEPS)
    )
    tile = (SUBLANES, LANES)
    keep = iota(tile, 1) % SPLIT == iota(tile, 0) % SPLIT
    per_tile = SUBLANES // SPLIT
    plane_of = iota(tile, 0) // SPLIT

    def clipped(zi):
        return jnp.clip(z_base + zi - HALO, 0, planes_all - 1)

    def chosen(index, values):
        out = jnp.broadcast_to(values[0], tile)
        for number, value in enumerate(values[1:], 1):
            out = jnp.where(index == number, jnp.broadcast_to(value, tile), out)
        return out

    for p in range(pairs):
        stacked = []
        for ref in part_refs:
            for zi in range(0, region_z, per_tile):
                values = [ref[p, pl.ds(clipped(zi + i), 1), :] for i in range(per_tile)]
                stacked.append(jnp.where(keep, chosen(plane_of, values), 0.0))
        parts = bf16_dot(jnp.concatenate(stacked, axis=0).astype(jnp.bfloat16), pick)
        length = region_z * SPLIT
        lp = (parts[:length] + parts[length : 2 * length]) + parts[2 * length :]
        lp_ref2[2 * p] = lp[:, :LANES]
        lp_ref2[2 * p + 1] = lp[:, LANES:]

    m_of = iota(tile, 0) // groups
    ms = SUBLANES // groups

    def plane(zi, carry):
        zg = z_base + zi - HALO
        z_inside = (zg >= 0) & (zg < planes_all)
        for y in range(-HALO, rows + HALO):
            yg = y_base + y
            inside = z_inside & (yg >= 0) & (yg < rows_all)
            scale = jnp.where(inside, INNER[0] * 0.5 * DAMPING, 0.0)
            for part in range(size // SUBLANES):
                values = [
                    lp_ref2[y + LEAD, pl.ds(zi * SPLIT + part * ms + i, 1), :] for i in range(ms)
                ]
                at = slice(part * SUBLANES, (part + 1) * SUBLANES)
                r_ref[zi, y + HALO, at] = scale / (shift[at] + chosen(m_of, values))
        return carry

    lax.fori_loop(0, region_z, plane, 0)
    spread_ref[...] = spread_matrix()
    gather_ref[...] = gather_matrix()


def spread_matrix():
    from_lane = iota((LANES, SPLIT * LANES), 0)
    to_lane = iota((LANES, SPLIT * LANES), 1)
    return one_hot(from_lane % NX == SPLIT * (to_lane % STEPS) + to_lane // LANES)


def gather_matrix():
    lane_in, x_out = iota((SPLIT * LANES, LANES), 0), iota((SPLIT * LANES, LANES), 1) % NX
    return one_hot(x_out == SPLIT * (lane_in % STEPS) + lane_in // LANES)


def place(cells, spread_ref, r_ref, ro_ref, first_ref, then=None):
    fields = first_ref.shape[4]
    packed = jnp.concatenate([parts for _, parts, _, _ in cells], axis=0).astype(jnp.bfloat16)
    values = (START / LAST) * bf16_dot(packed, spread_ref[...])
    for number, (orbitals, _, z, y) in enumerate(cells):
        zi, yi = z + HALO, y + HALO
        o = (-2.0 * START * LAST) * orbitals.astype(jnp.float32)
        ro = r_ref[zi, yi] * o
        ro_ref[zi, yi] = ro
        own = [
            values[number * fields : (number + 1) * fields, m * LANES : (m + 1) * LANES]
            for m in range(SPLIT)
        ]
        first_sweep(ro_ref, first_ref, z, y, own)
        if then is not None:
            then(z, y, o * ro, own)


def sweep(number, g, z, reaches, rows, scale_ref, first_ref, source_ref, target_ref):
    groups, fields = first_ref.shape[0], first_ref.shape[4]
    deep = len(reaches)
    before_number = number - 1
    last = number == SWEEPS - 1
    step = iota((fields, LANES), 1) % STEPS
    first_k = step == 0
    last_k = step == STEPS - 1

    def row(i, y):
        return [source_ref[g, z + i - before_number, y - before_number, m] for m in range(SPLIT)]

    most = max(reaches)
    ys = range(HALO - most, HALO + rows + most)
    before = [row(i, ys[0] - 1) for i in range(deep)]
    here = [row(i, ys[0]) for i in range(deep)]
    for y in ys:
        after = [row(i, y + 1) for i in range(deep)]
        under, over = row(-1, y), row(deep, y)
        for i in range(deep):
            if not -reaches[i] <= y - HALO < rows + reaches[i]:
                continue
            lower = here[i - 1] if i else under
            upper = here[i + 1] if i + 1 < deep else over
            mid = here[i]
            for m in range(SPLIT):
                if m:
                    left = mid[m - 1]
                else:
                    left = jnp.where(first_k, 0.0, pltpu.roll(mid[SPLIT - 1], 1, 1))
                if m + 1 < SPLIT:
                    right = mid[m + 1]
                else:
                    right = jnp.where(last_k, 0.0, pltpu.roll(mid[0], LANES - 1, 1))
                near = (before[i][m] + after[i][m]) + (lower[m] + upper[m])
                near = near + (left + right)
                scale = scale_ref[z + i, y, pl.ds(m * groups + g, 1), :]
                near = jnp.broadcast_to(scale, (fields, LANES)) * near
                if last:
                    target_ref[z + i - HALO, y - HALO, m] += near
                else:
                    base = mid[m] if number == 1 else first_ref[g, z + i, y, m]
                    target_ref[g, z + i - number, y - number, m] = near + base
        before, here = here, after


def first_sweep(ro_ref, first_ref, z, y, values):
    groups = first_ref.shape[0]
    zi, yi = z + HALO, y + HALO
    for g in range(groups):
        for m in range(SPLIT):
            at = m * groups + g
            ro = jnp.broadcast_to(ro_ref[zi, yi, at : at + 1], values[m].shape)
            first_ref[g, zi, yi, m] = ro * values[m]


def prepare_kernel(
    parts_ref, own_ref, a_ref, b_ref, r_ref, spread_ref, inverse_ref,
    ro_ref, first_ref, x_ref, y_ref, acc_ref, later_ref, wide_ref, w_ref,
):
    depth, rows = own_ref.shape[:2]
    fields = first_ref.shape[4]
    size = ro_ref.shape[2]
    groups = size // SPLIT

    def first_term(z, y, weight, values):
        if not 0 <= y < rows:
            return
        turn = groups // 2
        while turn:
            weight = weight + pltpu.roll(weight, size - turn, 0)
            turn //= 2
        w_ref[y] = (COEFFS[0] / (START * START * LAST)) * weight
        for m in range(SPLIT):
            at = m * groups
            w = jnp.broadcast_to(w_ref[y, at : at + 1], (fields, LANES))
            acc_ref[z, y, m] = w * values[m]

    def plane(z, carry):
        cells = []
        for y in range(-HALO, rows + HALO):
            value = of_fields(parts_ref, fields, depth, z, y)
            cells.append((row_tile(own_ref, a_ref, b_ref, z, y), two_parts(value, y), z, y))
        place(cells, spread_ref, r_ref, ro_ref, first_ref, first_term)
        return carry

    lax.fori_loop(0, depth, plane, 0, unroll=4)

    def scaled(z, carry):
        later_ref[z] = (INNER[-1] / INNER[0]) * r_ref[z]
        return carry

    lax.fori_loop(0, r_ref.shape[0], scaled, 0)

    all_rows = depth * fields

    pick = one_hot(iota((all_rows, fields), 0) // depth == iota((all_rows, fields), 1))
    tile = one_hot(iota((fields, all_rows), 1) % fields == iota((fields, all_rows), 0))
    wide = bf16_dot(bf16_dot(pick, inverse_ref[...]).astype(jnp.bfloat16), tile)
    square = (all_rows, all_rows)
    same = iota(square, 0) % depth == iota(square, 1) // fields
    wide_ref[...] = jnp.where(same, wide, 0.0).astype(jnp.bfloat16)

    def group(g, carry):
        for z in range(1, depth - 1, 2):
            sweep(1, g, HALO + z, (HALO - 1,) * 2, rows, r_ref, first_ref, first_ref, x_ref)
        for z in range(2, depth - 2, 2):
            sweep(2, g, HALO + z, (HALO - 2,) * 2, rows, later_ref, first_ref, x_ref, y_ref)
        return carry

    lax.fori_loop(0, groups, group, 0)


def sweep_kernel(
    parts_ref, a_ref, b_ref, r_ref, later_ref, wide_ref, spread_ref, gather_ref, ro_in, first_in, x_in, y_in, acc_in,
    out_ref, ro_ref, first_ref, x_ref, y_ref, acc_ref, m_ref,
):
    depth, rows = acc_ref.shape[:2]
    fields = first_ref.shape[4]
    size = ro_ref.shape[2]
    groups = size // SPLIT
    count = groups * BATCH
    even = lax.rem(lax.axis_index("grid"), 2) == 0
    all_cells = list(enumerate(plane_cells(rows)))
    for d in range(1, HALO + 1):
        z_a = jnp.where(even, depth - 1 + d, -d)
        z_b = jnp.where(even, -d, depth - 1 + d)
        cells = []
        for at, (distance, y) in all_cells:
            if distance == d:
                for ref, z in ((a_ref, z_a), (b_ref, z_b)):
                    tile = ref[at].astype(jnp.float32)
                    cells.append((tile[:size], tile[size:], z, y))
        place(cells, spread_ref, r_ref, ro_ref, first_ref)

    top = HALO + depth

    def group(g, carry):
        for z, reaches in (
            (HALO - 2, (0,)),
            (HALO - 1, (1, 2)),
            (top - 1, (2, 1)),
            (top + 1, (0,)),
        ):
            sweep(1, g, z, reaches, rows, r_ref, first_ref, first_ref, x_ref)
        for z, reaches in ((HALO - 1, (0,)), (HALO, (1, 1)), (top - 2, (1, 1)), (top, (0,))):
            sweep(2, g, z, reaches, rows, later_ref, first_ref, x_ref, y_ref)

        def inner(pair, c):
            sweep(3, g, HALO + 2 * pair, (0, 0), rows, ro_ref, first_ref, y_ref, acc_ref)
            return c

        lax.fori_loop(0, depth // 2, inner, 0, unroll=2)
        return carry

    lax.fori_loop(0, groups, group, 0)

    gather = gather_ref[...]
    left = lane_halves((fields, LANES))
    factor = 4.0 / count * -0.5
    planes = []
    per_plane = rows * fields
    acc = jnp.concatenate(
        [acc_ref[:, :, m].reshape(depth * per_plane, LANES) for m in range(SPLIT)], axis=1
    )
    upper = acc.astype(jnp.bfloat16)
    lower = (acc - upper.astype(jnp.float32)).astype(jnp.bfloat16)
    totals = bf16_dot(jnp.concatenate([upper, lower], axis=0), gather)
    totals = totals[: depth * per_plane] + totals[depth * per_plane :]
    for z in range(depth):
        total = totals[z * per_plane : (z + 1) * per_plane]
        tiles = []
        for y in range(rows):
            tiles.append(total[y * fields : (y + 1) * fields])
        pieces = []
        for y in range(0, rows, 2):
            value = of_fields(parts_ref, fields, depth, z, y)
            pieces.append(value + factor * jnp.where(left, tiles[y], tiles[y + 1]))
        planes.append(jnp.concatenate(pieces, axis=1))
    stacked = jnp.concatenate(planes, axis=0).astype(jnp.bfloat16)
    updated = bf16_dot(wide_ref[...], stacked)

    m_ref[...] = jnp.zeros_like(m_ref)
    gram = jnp.zeros((fields, fields), jnp.float32)
    for z in range(depth):
        one = planes[z].astype(jnp.bfloat16)
        gram = gram + lax.dot_general(
            one, one, (((1,), (1,)), ((), ())), preferred_element_type=jnp.float32
        )
    m_ref[:, :fields] = gram
    pieces = rows * NX // LANES
    for p in range(fields):
        for t in range(pieces):
            block = updated[p * depth : (p + 1) * depth, t * LANES : (t + 1) * LANES]
            out_ref[p, t] = block.astype(out_ref.dtype)
        rest = jnp.broadcast_to(m_ref[p : p + 1, :], (depth, LANES))
        spread = jnp.zeros((depth, LANES), jnp.float32)
        for number in range(3):
            part = rest.astype(jnp.bfloat16).astype(jnp.float32)
            spread = jnp.where(iota((depth, LANES), 0) == number, part, spread)
            rest = rest - part
        out_ref[p, pieces] = spread.astype(out_ref.dtype)


VMEM = pl.BlockSpec(memory_space=pltpu.VMEM)
SMEM = pl.BlockSpec(memory_space=pltpu.SMEM)
ANY = pl.BlockSpec(memory_space=pl.ANY)


def in_vmem(*arrays):
    return [pltpu.with_memory_space_constraint(array, pltpu.VMEM) for array in arrays]


def in_hbm(array):
    return pltpu.with_memory_space_constraint(array, pltpu.HBM)


def swapped(to_a, to_b, axis, name):
    count = lax.axis_size(axis)
    pairs_a = [(i, i ^ 1) for i in range(count)]
    pairs_b = [(i, i + 1 if i % 2 else i - 1) for i in range(1, count - 1)]
    if name == "row":
        pairs_b = [(i, (i + 1 if i % 2 else i - 1) % count) for i in range(count)]
    got_a = lax.ppermute(to_a, axis, pairs_a)
    got_b = lax.ppermute(to_b, axis, pairs_b)
    return got_a, got_b


def rows_plan(potentials, orbitals, energies, local_potential, inverse_factor):
    pots = lax.axis_size("pot")
    grids = lax.axis_size("grid")
    depth = potentials.shape[1]
    count, _, width = orbitals.shape
    rows = width // NX
    fields = pots
    half = count // 2
    f32, bf16 = jnp.float32, jnp.bfloat16
    shape = pltpu.VMEM
    tile = (half + fields, LANES)

    region = (depth + 2 * HALO, rows + 2 * HALO)
    pieces = width // LANES
    window = pieces + 2 * (LEAD * NX // LANES) - 1
    limit = pltpu.CompilerParams(vmem_limit_bytes=VMEM_LIMIT)
    call = functools.partial(pl.pallas_call, compiler_params=limit)
    side = len(row_cells(depth))
    lp_shape = (rows // 2 + LEAD, local_potential.shape[0], LANES)
    fields_tiles = potentials.reshape(depth, pots * pieces, LANES).transpose(1, 0, 2)
    windows, own, to_a, to_b, lp = call(
        first_kernel,
        out_shape=[
            pltpu.HBM((pots, window, depth, LANES), f32),
            shape((depth, rows, half, LANES), bf16),
            shape((side, half, LANES), bf16),
            shape((side, half, LANES), bf16),
            shape(lp_shape, f32),
        ],
        in_specs=[ANY] * 3,
        out_specs=[ANY] + [VMEM] * 4,
        scratch_shapes=[
            pltpu.VMEM((pots * pieces + window + 1 - pieces, depth, LANES), f32),
            pltpu.VMEM((pots, depth, LANES), f32),
            pltpu.VMEM(orbitals.shape, bf16),
            pltpu.VMEM((half * rows * depth, LANES), f32),
            pltpu.SemaphoreType.DMA((2 + 2 * pots,)),
            pltpu.SemaphoreType.DMA(lp_shape[:1]),
        ],
        name="first",
    )(in_hbm(fields_tiles), in_hbm(orbitals), in_hbm(local_potential))
    got_a, got_b = swapped(to_a, to_b, "pot", "row")
    parts = lax.all_to_all(windows, "pot", 0, 0, tiled=True)
    parts = parts.reshape(pots * window * depth, LANES)

    inverse_diagonal, spread, gather = call(
        diagonal_kernel,
        out_shape=[
            shape(region + (half, LANES), f32),
            shape((LANES, SPLIT * LANES), bf16),
            shape((SPLIT * LANES, LANES), bf16),
        ],
        in_specs=[SMEM, VMEM],
        out_specs=[VMEM] * 3,
        scratch_shapes=[pltpu.VMEM((rows + 2 * LEAD, region[0] * SPLIT, LANES), f32)]
        + [pltpu.VMEM(lp_shape, f32)] * 3,
        name="diagonal",
    )(in_hbm(energies), *in_vmem(lp))

    parts, inverse_diagonal = lax.optimization_barrier((parts, inverse_diagonal))
    edge = len(plane_cells(rows))
    up, down = call(
        send_kernel,
        out_shape=[shape((edge,) + tile, bf16)] * 2,
        in_specs=[VMEM] * 4,
        out_specs=[VMEM] * 2,
        name="sends",
    )(*in_vmem(parts, own, got_a, got_b))
    z_a, z_b = swapped(up, down, "grid", "plane")

    own_values = [
        shape(region + (half, LANES), f32),
        *(
            shape((half // SPLIT, region[0] - 2 * n, region[1] - 2 * n, SPLIT, fields, LANES), f32)
            for n in range(SWEEPS - 1)
        ),
        shape((depth, rows, SPLIT, fields, LANES), f32),
    ]
    *prepared, later, wide = call(
        prepare_kernel,
        out_shape=own_values + own_values[:1] + [shape((depth * fields,) * 2, bf16)],
        in_specs=[VMEM] * 7,
        out_specs=[VMEM] * 7,
        scratch_shapes=[pltpu.VMEM((rows, half, LANES), f32)],
        name="prepare",
    )(*in_vmem(parts, own, got_a, got_b, inverse_diagonal, spread), in_hbm(inverse_factor))
    sent, *_ = call(
        sweep_kernel,
        out_shape=[shape((fields, pieces + 1, depth, LANES), bf16)] + own_values,
        in_specs=[VMEM] * 13,
        out_specs=[VMEM] * 6,
        scratch_shapes=[pltpu.VMEM((fields, LANES), f32)],
        input_output_aliases={8 + i: 1 + i for i in range(5)},
        name="sweeps",
    )(*in_vmem(parts, z_a, z_b, inverse_diagonal, later, wide, spread, gather, *prepared))

    back = lax.all_to_all(sent, "pot", 0, 0, tiled=True)
    updated = back[:, :pieces].astype(f32).reshape(pots * pieces, depth, LANES).transpose(1, 0, 2)
    updated = updated.reshape(1, depth, pots * width)
    margins = jnp.sum(back[:, pieces].astype(f32), axis=(0, 1))[None]
    step = 1
    while step < grids:
        margins = margins + lax.ppermute(margins, "grid", [(i, i ^ step) for i in range(grids)])
        step *= 2
    margins = margins[:1, :fields] / local_potential.size
    return updated, margins


def local(potentials, orbitals, energies, local_potential, inverse_factor):
    pots = lax.axis_size("pot")
    grids = lax.axis_size("grid")
    depth = potentials.shape[1]
    count, _, width = orbitals.shape
    fits = (
        potentials.shape[0] == 1
        and pots == 8
        and width % LANES == 0
        and LANES == 2 * NX
        and width // NX >= HALO
        and depth == 8
        and count % (BATCH * SPLIT) == 0
        and count // BATCH in (2, 4)
        and grids & (grids - 1) == 0
    )
    plan = rows_plan if fits else gathered_plan
    return plan(potentials, orbitals, energies, local_potential, inverse_factor)


def solution(mesh):
    in_specs = (P("pot", "grid", None), P(None, "grid", "pot"), P(), P(), P())
    out_specs = (P("pot", "grid", None), P("pot", None))
    return jax.shard_map(local, mesh=mesh, in_specs=in_specs, out_specs=out_specs, check_vma=False)
```
